32 devices in a mesh: dp: 8 (over z, y), tensor: 4 (over x, core).
Axes of the slice: x: 2, y: 2, z: 4, core: 2. Of those that a mesh axis runs over, the one named last changes fastest.
Arguments:
- text_input: bfloat16 [16384, 768], P(('dp', 'tensor')), may hold values from -6 to 6
- layout_input: bfloat16 [16384, 192], P(('dp', 'tensor')), may hold values from -6 to 6
- text_cotangent: float32 [16384, 768], P(('dp', 'tensor')), may hold values from -6 to 6
- layout_cotangent: float32 [16384, 192], P(('dp', 'tensor')), may hold values from -6 to 6
- page_group: int32 [32], P('dp'), may hold values from 0 to 7, never falling along the last dimension, each value on 1 to 16 neighbouring positions
- page_length: int32 [32], P('dp'), may hold values from 1 to 512, 10240 in all
- text_qkv: bfloat16 [768, 3, 768], P('dp', None, 'tensor'), may hold values from -0.21875 to 0.21875
- text_out: bfloat16 [768, 768], P('tensor', 'dp'), may hold values from -1.75 to 1.75
- text_up: bfloat16 [768, 3072], P('dp', 'tensor'), may hold values from -0.21875 to 0.21875
- text_down: bfloat16 [3072, 768], P('tensor', 'dp'), may hold values from -0.109375 to 0.109375
- text_norm: float32 [4, 768], replicated, may hold values from 0.25 to 1.75
- layout_qkv: bfloat16 [192, 3, 192], P('dp', None, 'tensor'), may hold values from -0.4375 to 0.4375
- layout_out: bfloat16 [192, 192], P('tensor', 'dp'), may hold values from -3.5 to 3.5
- layout_up: bfloat16 [192, 768], P('dp', 'tensor'), may hold values from -0.4375 to 0.4375
- layout_down: bfloat16 [768, 192], P('tensor', 'dp'), may hold values from -0.21875 to 0.21875
- layout_norm: float32 [4, 192], replicated, may hold values from 0.25 to 1.75
Outputs:
- text_result: float32 [16384, 768], P(('dp', 'tensor'))
- layout_result: float32 [16384, 192], P(('dp', 'tensor'))
- text_input_grad: float32 [16384, 768], P(('dp', 'tensor'))
- layout_input_grad: float32 [16384, 192], P(('dp', 'tensor'))
- text_qkv_grad: float32 [768, 3, 768], P('dp', None, 'tensor')
- text_out_grad: float32 [768, 768], P('tensor', 'dp')
- text_up_grad: float32 [768, 3072], P('dp', 'tensor')
- text_down_grad: float32 [3072, 768], P('tensor', 'dp')
- text_norm_grad: float32 [4, 768], replicated
- layout_qkv_grad: float32 [192, 3, 192], P('dp', None, 'tensor')
- layout_out_grad: float32 [192, 192], P('tensor', 'dp')
- layout_up_grad: float32 [192, 768], P('dp', 'tensor')
- layout_down_grad: float32 [768, 192], P('tensor', 'dp')
- layout_norm_grad: float32 [4, 192], replicated
The draws below stay inside these ranges and needn't reach their ends.
Inputs may be any that keep to these rules, and one draw needn't show every extreme that they name: `page_group`: group ids never fall along the pages; every group 0 to 7 has 1 to 16 pages, one group exactly that many. page_length sums to 10240 and some page is full.
All inputs are finite; a program needn't handle non-finite values. No bound on the sum of `page_length` on one device may be relied on, other than what follows from the above.
Results may differ from the reference program's by a relative error of at most 0.015.
The reference program's roundings to bfloat16 on the way count: a program that leaves them out, or rounds other values in their place, can miss the bound.
Values may be sent and summed in bfloat16 or wider, within the bound.
No kernel may reach another device: no remote copies, remote signals or barrier semaphores. Data moves between devices by JAX's collectives and lax.ppermute only.
A program may use at most 128 MiB of HBM per device.

```python
import math
import jax
import jax.numpy as jnp
import numpy as np
from jax import lax

HEADS = 12
TEXT_HEAD = 64
LAY_HEAD = 16
D = 768
DL = 192
FF = 3072
FFL = 768
S = 512
NGROUPS = 8
PAGES = 32
TOKENS = 16384


def steps_of(key, shape, split, low, high):
    def one(axis_at, blocks):
        heights = jax.random.uniform(jax.random.fold_in(jax.random.fold_in(key, 6), axis_at), (blocks,), jnp.float32, low / len(split), high / len(split))
        return jnp.repeat(jnp.exp(heights), shape[axis_at] // blocks).reshape((-1,) + (1,) * (len(shape) - axis_at - 1))

    loudness = one(*split[0])
    for cut in split[1:]:
        loudness = loudness * one(*cut)
    return loudness


def split_up(number_of, total, bound, lean):
    weights = [(1 << 20) // math.isqrt(grade ** lean) + 1 for grade in range(2, number_of + 1)]
    rest, given = total - bound - (number_of - 1), [1] * (number_of - 1)
    while rest > 0:
        free = [i for i in range(number_of - 1) if given[i] < bound]
        whole, remaining = sum([weights[i] for i in free]), rest
        for i in free:
            extra = min(bound - given[i], max(1, remaining * weights[i] // whole), rest)
            given[i] = given[i] + extra
            rest = rest - extra
    return np.array([bound] + given)


def uneven(rng, number_of, total, bound, slope):
    if number_of == 2:
        one = jax.random.randint(rng, (), max(1, total - bound), min(bound, total - 1) + 1)
        return jnp.stack([one, total - one])
    sizes = jnp.asarray(split_up(number_of, total, bound, slope), jnp.int32)
    couples = (number_of - 1) // 2
    giver, sink = sizes[1:1 + 2 * couples:2], sizes[2:2 + 2 * couples:2]
    room = jnp.minimum(giver - 1, bound - sink)
    passed = jax.random.randint(jax.random.fold_in(rng, 1), (couples,), 0, 1 << 20) % (room + 1)
    sizes = sizes.at[1:1 + 2 * couples:2].set(giver - passed).at[2:2 + 2 * couples:2].set(sink + passed)
    return sizes[jax.random.permutation(jax.random.fold_in(rng, 2), number_of)]


def bell_draw(rng, extent, deviation, bound, split=(), kind=jnp.bfloat16):
    level = steps_of(rng, extent, split, -0.22, 0.18) if split else 1.0
    values = jax.random.normal(rng, extent, jnp.float32) * deviation * level
    return jnp.minimum(jnp.maximum(values, -bound), bound).astype(kind)


def setup_inputs(seed: int = 0) -> dict:
    keys = jax.random.split(jax.random.key(seed), 17)
    return {
        "text_input": bell_draw(keys[0], (TOKENS, D), 1.0, 6.0, ((0, 32),)),
        "layout_input": bell_draw(keys[1], (TOKENS, DL), 1.0, 6.0, ((0, 32),)),
        "text_cotangent": bell_draw(keys[2], (TOKENS, D), 1.0, 6.0, ((0, 32),), jnp.float32),
        "layout_cotangent": bell_draw(keys[3], (TOKENS, DL), 1.0, 6.0, ((0, 32),), jnp.float32),
        "page_group": jnp.searchsorted(jnp.cumsum(uneven(keys[4], NGROUPS, PAGES, PAGES - 2 * NGROUPS, 2)), jnp.arange(PAGES), side="right").astype(jnp.int32),
        "page_length": uneven(keys[5], PAGES, PAGES * S * 5 // 8, S, 2).astype(jnp.int32),
        "text_qkv": bell_draw(keys[6], (D, 3, D), D ** -0.5, 0.21875, ((0, 8), (2, 4))),
        "text_out": bell_draw(keys[7], (D, D), (max(D // 64, 1)) ** -0.5, 1.75, ((0, 4), (1, 8))),
        "text_up": bell_draw(keys[8], (D, FF), D ** -0.5, 0.21875, ((0, 8), (1, 4))),
        "text_down": bell_draw(keys[9], (FF, D), FF ** -0.5, 0.109375, ((0, 4), (1, 8))),
        "text_norm": jnp.clip(1.0 + 0.15 * jax.random.normal(keys[10], (4, D), jnp.float32), 0.25, 1.75),
        "layout_qkv": bell_draw(keys[11], (DL, 3, DL), DL ** -0.5, 0.4375, ((0, 8), (2, 4))),
        "layout_out": bell_draw(keys[12], (DL, DL), (max(DL // 64, 1)) ** -0.5, 3.5, ((0, 4), (1, 8))),
        "layout_up": bell_draw(keys[13], (DL, FFL), DL ** -0.5, 0.4375, ((0, 8), (1, 4))),
        "layout_down": bell_draw(keys[14], (FFL, DL), FFL ** -0.5, 0.21875, ((0, 4), (1, 8))),
        "layout_norm": jnp.clip(1.0 + 0.15 * jax.random.normal(keys[15], (4, DL), jnp.float32), 0.25, 1.75),
    }


@jax.custom_vjp
def low(v):
    return lax.optimization_barrier(v.astype(jnp.bfloat16)).astype(jnp.float32)

@jax.custom_vjp
def low_back(v):
    return v

def low_keep(v):
    return (low(v), None)

def low_pass(kept, grad):
    return (grad,)

def back_keep(v):
    return (v, None)

def back_low(kept, grad):
    return (low(grad),)
low.defvjp(low_keep, low_pass)
low_back.defvjp(back_keep, back_low)
highest = lax.Precision.HIGHEST
epsilon = 1e-05
neg_large = -1e+30

def layer_norm(values, norm_gain, norm_shift):
    centred = values - lax.optimization_barrier(jnp.mean(values, axis=-1, keepdims=True))
    inverse = lax.rsqrt(lax.optimization_barrier(jnp.mean(centred * centred, axis=-1, keepdims=True)) + epsilon)
    return centred * inverse * norm_gain + norm_shift

def soft_rows(logits, live_keys):
    logits = jnp.where(live_keys, logits, neg_large)
    row_top = lax.optimization_barrier(jnp.max(logits, axis=-1, keepdims=True))
    log_total = row_top + jnp.log(lax.optimization_barrier(jnp.sum(jnp.exp(logits - row_top), axis=-1, keepdims=True)))
    return jnp.exp(logits - log_total)

def feed_forward(middle, w_upper, w_lower, norms):
    before = low_back(jnp.dot(low(middle), w_upper, precision=highest))
    branch = low_back(jnp.dot(low(jax.nn.gelu(before, approximate=False)), w_lower, precision=highest))
    return layer_norm(middle + branch, norms[2], norms[3])

def block_layer(params, text_rows, layout_rows, lengths, const_rows, const_weight):
    t_qkv, t_out, t_up, t_down, t_norm, l_qkv, l_out, l_up, l_down, l_norm = params
    page_count = lengths.shape[0]
    live_slots = jnp.arange(S, dtype=jnp.int32)[None, :] < lengths[:, None]
    row_keep = live_slots.reshape(page_count * S, 1).astype(jnp.float32)
    text_proj = low(low_back(jnp.einsum('rd,dcf->rcf', text_rows, t_qkv, precision=highest)))
    text_proj = text_proj.reshape(page_count, S, 3, HEADS, TEXT_HEAD)
    layout_proj = low(low_back(jnp.einsum('rd,dcf->rcf', layout_rows, l_qkv, precision=highest)))
    layout_proj = layout_proj.reshape(page_count, S, 3, HEADS, LAY_HEAD)
    held_proj = low(jnp.einsum('rd,dcf->rcf', const_rows, const_weight, precision=highest))
    held_proj = held_proj.reshape(page_count, S, 3, HEADS, TEXT_HEAD)
    text_scale = float(TEXT_HEAD) ** (-0.5)
    layout_scale = float(LAY_HEAD) ** (-0.5)
    text_scores = low_back(jnp.einsum('pihd,pjhd->phij', text_proj[:, :, 0], text_proj[:, :, 1], precision=highest) * text_scale)
    layout_scores = low_back(jnp.einsum('pihd,pjhd->phij', layout_proj[:, :, 0], layout_proj[:, :, 1], precision=highest) * layout_scale)
    held_scores = jnp.einsum('pihd,pjhd->phij', held_proj[:, :, 0], held_proj[:, :, 1], precision=highest) * text_scale
    live_keys = live_slots[:, None, None, :]
    text_probs = low(soft_rows(text_scores + layout_scores, live_keys))
    layout_probs = low(soft_rows(layout_scores + held_scores, live_keys))
    text_ctx = low(low_back(jnp.einsum('phij,pjhd->pihd', text_probs, text_proj[:, :, 2], precision=highest)))
    layout_ctx = low(low_back(jnp.einsum('phij,pjhd->pihd', layout_probs, layout_proj[:, :, 2], precision=highest)))
    text_ctx = text_ctx.reshape(page_count * S, D)
    layout_ctx = layout_ctx.reshape(page_count * S, DL)
    text_mid = layer_norm(text_rows + low_back(jnp.dot(text_ctx, t_out, precision=highest)), t_norm[0], t_norm[1])
    layout_mid = layer_norm(layout_rows + low_back(jnp.dot(layout_ctx, l_out, precision=highest)), l_norm[0], l_norm[1])
    text_end = feed_forward(text_mid, t_up, t_down, t_norm) * row_keep
    layout_end = feed_forward(layout_mid, l_up, l_down, l_norm) * row_keep
    return (text_end, layout_end)

def reference(text_input, layout_input, text_cotangent, layout_cotangent, page_group, page_length, text_qkv, text_out, text_up, text_down, text_norm, layout_qkv, layout_out, layout_up, layout_down, layout_norm):
    weights = tuple((weight.astype(jnp.float32) for weight in (text_qkv, text_out, text_up, text_down, text_norm, layout_qkv, layout_out, layout_up, layout_down, layout_norm)))
    text_full = text_input.astype(jnp.float32)
    layout_full = layout_input.astype(jnp.float32)
    per_block = math.gcd(PAGES, max(4096 // S, 1))
    blocks = PAGES // per_block
    const_blocks = text_full.reshape(blocks, per_block * S, D)
    length_blocks = page_length.reshape(blocks, per_block)
    block_step = jax.checkpoint(block_layer)

    def whole_layer(params, text_all, layout_all):

        def scan_step(scan_carry, inputs):
            text_part, layout_part, lengths, const_part = inputs
            return (scan_carry, block_step(params, text_part, layout_part, lengths, const_part, weights[0]))
        scan_carry, outputs = lax.scan(scan_step, jnp.zeros((), jnp.float32), (text_all.reshape(blocks, per_block * S, D), layout_all.reshape(blocks, per_block * S, DL), length_blocks, const_blocks))
        return (outputs[0].reshape(TOKENS, D), outputs[1].reshape(TOKENS, DL))
    (text_end, layout_end), pull_back = jax.vjp(whole_layer, weights, text_full, layout_full)
    labels = jnp.arange(NGROUPS, dtype=jnp.int32)
    member = (page_group[:, None] == labels[None, :]).astype(jnp.float32)
    counts = lax.optimization_barrier(jnp.sum(member * page_length.astype(jnp.float32)[:, None], axis=0))
    weight_base = float(PAGES * S) / (2.0 * NGROUPS)
    page_weight = lax.optimization_barrier(jnp.sum(member * (weight_base / (counts + weight_base))[None, :], axis=1))
    row_weight = jnp.repeat(page_weight, S)[:, None]
    grads, text_grad, layout_grad = pull_back((text_cotangent * row_weight, layout_cotangent * row_weight))
    return (text_end, layout_end, text_grad, layout_grad, grads[0], grads[1], grads[2], grads[3], grads[4], grads[5], grads[6], grads[7], grads[8], grads[9])
```

```python
import functools
import math

import jax
import jax.numpy as jnp
from jax import lax
from jax.experimental import pallas as pl
from jax.experimental.pallas import tpu as pltpu
from jax.sharding import PartitionSpec as P

TEXT_HEAD = 64
LAY_HEAD = 16
S = 512
NGROUPS = 8

TB = 4
DB = 8
LROWS = 32

BITS = ((16, 8, 2, 4, 1), (16, 8, 4, 2, 1), (16, 8, 2, 4, 1))

epsilon = 1e-05
neg_large = -1e30
root_half = 1.0 / math.sqrt(2.0)
root_twopi = 1.0 / math.sqrt(2.0 * math.pi)
text_scale = float(TEXT_HEAD) ** (-0.5)
layout_scale = float(LAY_HEAD) ** (-0.5)

BF = jnp.bfloat16
F32 = jnp.float32
ANY = pl.BlockSpec(memory_space=pl.ANY)
VM = pl.BlockSpec(memory_space=pltpu.VMEM)
SM = pl.BlockSpec(memory_space=pltpu.SMEM)
PARAMS = pltpu.CompilerParams(vmem_limit_bytes=60 * 1024 * 1024)


def nn(a, b):
    return jnp.dot(a, b, preferred_element_type=F32)


def nt(a, b):
    return lax.dot_general(a, b, (((1,), (1,)), ((), ())), preferred_element_type=F32)


def sds(shape, dtype):
    return jax.ShapeDtypeStruct(shape, dtype)


def cost(flops, read, trans=0):
    return pl.CostEstimate(flops=int(flops), bytes_accessed=int(read), transcendentals=int(trans))


def load_pieces(refs, maps, me, rows, lanes, dst, sem):
    for ref, rels in zip(refs, maps):
        for i, rel in enumerate(rels):
            piece = rel ^ me
            spot = pl.multiple_of((piece // TB) * (rows[1] - rows[0]), rows[1] - rows[0])
            pltpu.make_async_copy(
                ref.at[i, rows[0] : rows[1], lanes[0] : lanes[1]],
                dst.at[piece % TB, pl.ds(spot, rows[1] - rows[0]), :],
                sem,
            ).start()


def wait_pieces(dst, sem):
    pltpu.make_async_copy(dst, dst, sem).wait()


def norm_stats(values):
    centred = values - jnp.mean(values, axis=-1, keepdims=True)
    inverse = lax.rsqrt(jnp.mean(centred * centred, axis=-1, keepdims=True) + epsilon)
    return centred * inverse, inverse


def norm_back(upstream, normed, inverse, gain):
    scaled = upstream * gain
    inner = (
        scaled
        - jnp.mean(scaled, axis=-1, keepdims=True)
        - normed * jnp.mean(scaled * normed, axis=-1, keepdims=True)
    )
    return (
        inverse * inner,
        jnp.sum(upstream * normed, axis=0, keepdims=True),
        jnp.sum(upstream, axis=0, keepdims=True),
    )


def attention_forward(maps, n_in, base, lay_rows, *refs):
    me_ref, len_ref, group_ref, cnt_ref, x_ref, xl_ref, e_ref = refs[:7]
    w_refs = refs[7 : 7 + n_in]
    qkv_o, lqkv_o, ctx_o, lctx_o, lse_o, wl_o, pw_o = refs[7 + n_in : 14 + n_in]
    wq, wl, sems = refs[14 + n_in :]
    me = me_ref[0]
    text_rows = wq.shape[1] // DB
    width = wq.shape[2]
    load_pieces(w_refs, maps, me, (0, text_rows), (0, width), wq, sems.at[0])
    load_pieces(w_refs, maps, me, (text_rows, text_rows + LROWS), (0, width), wl, sems.at[1])
    live = lax.broadcasted_iota(jnp.int32, (1, S), 1) < len_ref[0]
    wait_pieces(wq, sems.at[0])
    wait_pieces(wl, sems.at[1])
    heads = width // 3 // TEXT_HEAD
    tw, lw = heads * TEXT_HEAD, heads * LAY_HEAD
    counts = cnt_ref[...]
    if lay_rows is not None:
        place = lax.broadcasted_iota(jnp.int32, (8, wl.shape[1]), 1) % LROWS
        digits = jnp.where(place == lay_rows, 32.0, jnp.where(place == lay_rows + 1, 1.0, 0.0)).astype(BF)
        for t in range(TB):
            counts = counts + nn(digits, wl[t, :, 0:128])[0:1]
    same = lax.broadcasted_iota(jnp.int32, counts.shape, 1) == group_ref[0]
    mine = jnp.sum(jnp.where(same, counts, 0.0), axis=1, keepdims=True)
    pw_o[...] = jnp.broadcast_to(base / (mine + base), pw_o.shape)

    def step(t, carry):
        wlt = nn(e_ref[...], wl[t]).astype(BF)
        wl_o[t] = wlt
        qkv = nn(x_ref[...], wq[t]).astype(BF)
        qkv_o[t] = qkv
        lqkv = nn(xl_ref[...], wlt[:, : 3 * lw]).astype(BF)
        lqkv_o[t] = lqkv
        for h in range(heads):
            a, b = h * TEXT_HEAD, h * LAY_HEAD
            q = jnp.concatenate(
                [qkv[:, a : a + TEXT_HEAD] * BF(text_scale), lqkv[:, b : b + LAY_HEAD] * BF(layout_scale)], axis=1
            )
            k = jnp.concatenate(
                [qkv[:, tw + a : tw + a + TEXT_HEAD], lqkv[:, lw + b : lw + b + LAY_HEAD]], axis=1
            )
            v = jnp.concatenate(
                [qkv[:, 2 * tw + a : 2 * tw + a + TEXT_HEAD], lqkv[:, 2 * lw + b : 2 * lw + b + LAY_HEAD]], axis=1
            )
            logits = jnp.where(live, nt(q, k), neg_large)
            top = jnp.max(logits, axis=-1, keepdims=True)
            raw = jnp.exp(logits - top)
            total = jnp.sum(raw, axis=-1, keepdims=True)
            probs = (raw * (1.0 / total)).astype(BF)
            ctx = nn(probs, v).astype(BF)
            ctx_o[t, :, a : a + TEXT_HEAD] = ctx[:, :TEXT_HEAD]
            lctx_o[t, :, b : b + LAY_HEAD] = ctx[:, TEXT_HEAD:]
            lse_o[t, :, h : h + 1] = top + jnp.log(total)
        return carry

    lax.fori_loop(0, TB, step, 0)


def ffn_forward(maps, n_in, spots, *refs):
    (me_ref, len_ref, pw_ref, x_ref, xl_ref, ctx_ref, lctx_ref, wl_ref, tn_ref, ln_ref, ct_ref, cl_ref) = refs[:12]
    u_refs = refs[12 : 12 + n_in[0]]
    d_refs = refs[12 + n_in[0] : 12 + n_in[0] + n_in[1]]
    rest = refs[12 + n_in[0] + n_in[1] :]
    (res_o, lres_o, hid_o, slope_o, lhid_o, lslope_o, mid_o, lmid_o, gb_o, lgb_o, ge_o, lge_o, n1_o, ln1_o, i1_o,
     tg_o, lg_o) = rest[:17]
    wu, wd, wo, branch, sems = rest[17:]
    me = me_ref[0]
    rows = wu.shape[1] // DB
    load_pieces(u_refs, maps[0], me, (0, rows), (spots[2], spots[2] + wo.shape[2]), wo, sems.at[0])
    load_pieces(u_refs, maps[0], me, (0, rows), (spots[0], spots[0] + wu.shape[2]), wu, sems.at[1])
    load_pieces(d_refs, maps[1], me, (0, rows), (spots[1], spots[1] + wd.shape[2]), wd, sems.at[2])
    keep = (lax.broadcasted_iota(jnp.int32, (S, 1), 0) < len_ref[0]).astype(F32)
    scale = keep * pw_ref[0:1, 0:1]
    tn, ln = tn_ref[...], ln_ref[...]
    lq = wl_ref.shape[2]
    ow = lctx_ref.shape[2]
    lf = (lq - 4 * ow) // 2
    wait_pieces(wo, sems.at[0])
    attn = nt(ctx_ref[0], wo[0])
    lattn = nt(lctx_ref[0], wl_ref[0, :, 3 * ow : 4 * ow])
    for t in range(1, TB):
        attn = attn + nt(ctx_ref[t], wo[t])
        lattn = lattn + nt(lctx_ref[t], wl_ref[t, :, 3 * ow : 4 * ow])
    n1, i1 = norm_stats(x_ref[...].astype(F32) + attn)
    mid = n1 * tn[0:1] + tn[1:2]
    ln1, li1 = norm_stats(xl_ref[...].astype(F32) + lattn)
    lmid = ln1 * ln[0:1] + ln[1:2]
    n1_o[...] = n1
    ln1_o[...] = ln1
    i1_o[:, 0:1] = i1
    i1_o[:, 1:2] = li1
    mid_o[...] = mid.astype(BF)
    lmid_o[...] = lmid.astype(BF)
    branch[...] = mid
    wait_pieces(wu, sems.at[1])
    wait_pieces(wd, sems.at[2])

    def gelu(before):
        cdf = 0.5 * (1.0 + lax.erf(before * root_half))
        return (before * cdf).astype(BF), cdf + before * jnp.exp(-0.5 * before * before) * root_twopi

    def step(t, lbranch):
        hid, slope = gelu(nn(mid_o[...], wu[t]))
        hid_o[t] = hid
        slope_o[t] = slope
        branch[...] += nt(hid, wd[t])
        wlt = wl_ref[t]
        lhid, lslope = gelu(nn(lmid_o[...], wlt[:, 4 * ow : 4 * ow + lf]))
        lhid_o[t] = lhid
        lslope_o[t] = lslope
        return lbranch + nt(lhid, wlt[:, 4 * ow + lf :])

    lend = lax.fori_loop(0, TB, step, lmid)
    n2, i2 = norm_stats(branch[...])
    res_o[...] = (n2 * tn[2:3] + tn[3:4]) * keep
    ge, gain, shift = norm_back(ct_ref[...] * scale, n2, i2, tn[2:3])
    ge_o[...] = ge
    gb_o[...] = ge.astype(BF)
    tg_o[0:1] = gain
    tg_o[1:2] = shift
    ln2, li2 = norm_stats(lend)
    lres_o[...] = (ln2 * ln[2:3] + ln[3:4]) * keep
    lge, lgain, lshift = norm_back(cl_ref[...] * scale, ln2, li2, ln[2:3])
    lge_o[...] = lge
    lgb_o[...] = lge.astype(BF)
    lg_o[0:1] = lgain
    lg_o[1:2] = lshift


def send_pieces(outs, maps, me, buf, rows, lanes, sem):
    for out, rels in zip(outs, maps):
        for i, rel in enumerate(rels):
            piece = rel ^ me
            spot = pl.multiple_of((piece // TB) * (rows[1] - rows[0]), rows[1] - rows[0])
            pltpu.make_async_copy(
                buf.at[piece % TB, pl.ds(spot, rows[1] - rows[0]), :],
                out.at[i, rows[0] : rows[1], lanes[0] : lanes[1]],
                sem,
            ).start()


def down_grads(maps, *refs):
    me_ref, gb_ref, lgb_ref, hid_ref, lhid_ref = refs[:5]
    n_out = len(maps)
    outs = refs[5 : 5 + n_out]
    ld_o = refs[5 + n_out]
    buf, gbt, lgbt, sem = refs[6 + n_out :]
    rows, width = buf.shape[1] // DB, buf.shape[2]
    gbt[...] = gb_ref[...].T
    lgbt[...] = lgb_ref[...].T

    def step(t, carry):
        buf[t] = nn(gbt[...], hid_ref[t]).astype(BF)
        ld_o[t] = nn(lgbt[...], lhid_ref[t]).astype(BF)
        return carry

    lax.fori_loop(0, TB, step, 0)
    send_pieces(outs, maps, me_ref[0], buf, (0, rows), (0, width), sem)
    wait_pieces(buf, sem)


def ffn_backward(maps, n_in, spots, omaps, *refs):
    (me_ref, gb_ref, lgb_ref, ge_ref, lge_ref, slope_ref, lslope_ref, mid_ref, lmid_ref, n1_ref, ln1_ref, i1_ref,
     ctx_ref, lctx_ref, wl_ref, tn_ref, ln_ref) = refs[:17]
    u_refs = refs[17 : 17 + n_in[0]]
    d_refs = refs[17 + n_in[0] : 17 + n_in[0] + n_in[1]]
    rest = refs[17 + n_in[0] + n_in[1] :]
    n_out = len(omaps)
    outs = rest[:n_out]
    g1_o, lg1_o, dctx_o, ldctx_o, luo_o, tg_o, lg_o = rest[n_out : n_out + 7]
    wu, wd, wo, buf, obuf, acc, lacc, midt, lmidt, sems = rest[n_out + 7 :]
    me = me_ref[0]
    rows, width = wu.shape[1] // DB, wu.shape[2]
    load_pieces(d_refs, maps[1], me, (0, rows), (spots[1], spots[1] + wd.shape[2]), wd, sems.at[0])
    load_pieces(u_refs, maps[0], me, (0, rows), (spots[0], spots[0] + wu.shape[2]), wu, sems.at[1])
    load_pieces(u_refs, maps[0], me, (0, rows), (spots[2], spots[2] + wo.shape[2]), wo, sems.at[2])
    tn, ln = tn_ref[...], ln_ref[...]
    ow = lctx_ref.shape[2]
    lf = (wl_ref.shape[2] - 4 * ow) // 2
    midt[...] = mid_ref[...].T
    lmidt[...] = lmid_ref[...].T
    acc[...] = ge_ref[...]
    lacc[...] = lge_ref[...]
    wait_pieces(wd, sems.at[0])
    wait_pieces(wu, sems.at[1])

    def step(t, carry):
        dbef = (nn(gb_ref[...], wd[t]) * slope_ref[t]).astype(BF)
        buf[t] = nn(midt[...], dbef).astype(BF)
        acc[...] += nt(dbef, wu[t])
        wlt = wl_ref[t]
        ldbef = (nn(lgb_ref[...], wlt[:, 4 * ow + lf :]) * lslope_ref[t]).astype(BF)
        luo_o[t, :, ow : ow + lf] = nn(lmidt[...], ldbef).astype(BF)
        lacc[...] += nt(ldbef, wlt[:, 4 * ow : 4 * ow + lf])
        return carry

    lax.fori_loop(0, TB, step, 0)
    send_pieces(outs, omaps, me, buf, (0, rows), (spots[0], spots[0] + width), sems.at[3])
    g1, gain, shift = norm_back(acc[...], n1_ref[...], i1_ref[:, 0:1], tn[0:1])
    g1_o[...] = g1
    tg_o[0:1] = gain
    tg_o[1:2] = shift
    lg1, lgain, lshift = norm_back(lacc[...], ln1_ref[...], i1_ref[:, 1:2], ln[0:1])
    lg1_o[...] = lg1
    lg_o[0:1] = lgain
    lg_o[1:2] = lshift
    ga = g1.astype(BF)
    lga = lg1.astype(BF)
    midt[...] = ga.T
    lmidt[...] = lga.T
    wait_pieces(wo, sems.at[2])
    for t in range(TB):
        dctx_o[t] = nn(ga, wo[t]).astype(BF)
        obuf[t] = nn(midt[...], ctx_ref[t]).astype(BF)
        ldctx_o[t] = nn(lga, wl_ref[t, :, 3 * ow : 4 * ow]).astype(BF)
        luo_o[t, :, 0:ow] = nn(lmidt[...], lctx_ref[t]).astype(BF)
    send_pieces(outs, omaps, me, obuf, (0, rows), (spots[2], spots[2] + obuf.shape[2]), sems.at[4])
    wait_pieces(buf, sems.at[3])
    wait_pieces(obuf, sems.at[4])


def attention_backward(maps, n_in, omaps, *refs):
    (me_ref, len_ref, x_ref, xl_ref, et_ref, qkv_ref, lqkv_ref, ctx_ref, lctx_ref, dctx_ref, ldctx_ref, lse_ref,
     g1_ref, lg1_ref, wl_ref, luo_ref, ld_ref) = refs[:17]
    w_refs = refs[17 : 17 + n_in]
    rest = refs[17 + n_in :]
    n_out = len(omaps)
    outs = rest[:n_out]
    dx_o, dxl_o = rest[n_out : n_out + 2]
    wq, dqkv, ldqkv, buf, lbuf, xt, xlt, sems = rest[n_out + 2 :]
    me = me_ref[0]
    text_rows = wq.shape[1] // DB
    width = wq.shape[2]
    load_pieces(w_refs, maps, me, (0, text_rows), (0, width), wq, sems.at[0])
    live = lax.broadcasted_iota(jnp.int32, (1, S), 1) < len_ref[0]
    heads = width // 3 // TEXT_HEAD
    tw, lw = heads * TEXT_HEAD, heads * LAY_HEAD

    def step(t, carry):
        qkv, lqkv = qkv_ref[t], lqkv_ref[t]
        for h in range(heads):
            a, b = h * TEXT_HEAD, h * LAY_HEAD
            ta, tb = slice(a, a + TEXT_HEAD), slice(b, b + LAY_HEAD)
            qt, ql = qkv[:, ta] * BF(text_scale), lqkv[:, tb] * BF(layout_scale)
            kt, kl = qkv[:, tw + a : tw + a + TEXT_HEAD], lqkv[:, lw + b : lw + b + LAY_HEAD]
            vt, vl = qkv[:, 2 * tw + a : 2 * tw + a + TEXT_HEAD], lqkv[:, 2 * lw + b : 2 * lw + b + LAY_HEAD]
            gt, gl = dctx_ref[t, :, ta], ldctx_ref[t, :, tb]
            q = jnp.concatenate([qt, ql], axis=1)
            k = jnp.concatenate([kt, kl], axis=1)
            v = jnp.concatenate([vt, vl], axis=1)
            g = jnp.concatenate([gt, gl], axis=1)
            dot_t = jnp.sum(gt.astype(F32) * ctx_ref[t, :, ta].astype(F32), axis=-1, keepdims=True)
            dot_s = dot_t + jnp.sum(gl.astype(F32) * lctx_ref[t, :, tb].astype(F32), axis=-1, keepdims=True)
            logits = jnp.where(live, nt(q, k), neg_large)
            probs = jnp.exp(logits - lse_ref[t, :, h : h + 1])
            low = (probs * (nt(gt, vt) - dot_t)).astype(BF)
            llow = (probs * (nt(g, v) - dot_s)).astype(BF)
            dqkv[:, ta] = (nn(low, kt) * text_scale).astype(BF)
            ldqkv[:, tb] = (nn(llow, kl) * layout_scale).astype(BF)
            dk = nn(qt.T, low).T
            dkl = nn(ql.T, llow).T
            dv = nn(g.T, probs.astype(BF)).T
            dqkv[:, tw + a : tw + a + TEXT_HEAD] = dk.astype(BF)
            ldqkv[:, lw + b : lw + b + LAY_HEAD] = dkl.astype(BF)
            dqkv[:, 2 * tw + a : 2 * tw + a + TEXT_HEAD] = dv[:, :TEXT_HEAD].astype(BF)
            ldqkv[:, 2 * lw + b : 2 * lw + b + LAY_HEAD] = dv[:, TEXT_HEAD:].astype(BF)
        dx_o[...] += nt(dqkv[...], wq[t])
        dxl_o[...] += nt(ldqkv[...], wl_ref[t, :, : 3 * lw])
        buf[t] = nn(xt[...], dqkv[...]).astype(BF)
        lgrad = jnp.concatenate([nn(xlt[...], ldqkv[...]).astype(BF), luo_ref[t], ld_ref[t]], axis=1)
        lbuf[t] = nn(et_ref[...], lgrad).astype(BF)
        return carry

    xt[...] = x_ref[...].T
    xlt[...] = xl_ref[...].T
    dx_o[...] = g1_ref[...]
    dxl_o[...] = lg1_ref[...]
    wait_pieces(wq, sems.at[0])
    lax.fori_loop(0, TB, step, 0)
    send_pieces(outs, omaps, me, buf, (0, text_rows), (0, width), sems.at[1])
    send_pieces(outs, omaps, me, lbuf, (text_rows, text_rows + LROWS), (0, width), sems.at[2])
    wait_pieces(buf, sems.at[1])
    wait_pieces(lbuf, sems.at[2])


def call(kernel, name, args, any_args, outs, any_outs, scratch, price):
    specs = [SM if scalar else VM for _, scalar in args] + [ANY] * len(any_args)
    values = [array for array, _ in args] + list(any_args)
    return pl.pallas_call(
        kernel,
        name=name,
        in_specs=specs,
        out_specs=[ANY] * len(any_outs) + [VM] * len(outs),
        out_shape=list(any_outs) + list(outs),
        scratch_shapes=scratch,
        compiler_params=PARAMS,
        cost_estimate=price,
    )(*values)


def exchange(array, bit):
    size = lax.axis_size("dp") * lax.axis_size("tensor")
    return lax.ppermute(array, ("dp", "tensor"), [(i, i ^ bit) for i in range(size)])


def spread(bits):
    low = [
        (bits[0] if i & 1 else 0) | (bits[1] if i & 2 else 0) | (bits[2] if i & 4 else 0) for i in range(8)
    ]
    return tuple(tuple(top | rel for rel in low) for top in (0, bits[3], bits[4], bits[3] | bits[4]))


def gather_pieces(own, bits):
    held = own[None]
    for bit in bits[:3]:
        held = jnp.concatenate([held, exchange(held, bit)], axis=0)
    far = exchange(held, bits[3])
    return [held, far, exchange(held, bits[4]), exchange(far, bits[4])]


def scatter_pieces(arrays, bits):
    a00, a01, a10, a11 = arrays
    parts = [a01, exchange(a11, bits[4])]
    sent = sum(p.astype(F32) for p in parts).astype(BF)
    parts = [a00, exchange(a10, bits[4]), exchange(sent, bits[3])]
    for bit, half in ((bits[2], 4), (bits[1], 2), (bits[0], 1)):
        sent = sum(p[half : 2 * half].astype(F32) for p in parts).astype(BF)
        parts = parts + [exchange(sent, bit)]
    return sum(p[0].astype(F32) for p in parts)


def total_over_all(array, bits):
    for bit in bits:
        array = array + exchange(array, bit)
    return array


def body(
    text_input,
    layout_input,
    text_cotangent,
    layout_cotangent,
    page_group,
    page_length,
    text_qkv,
    text_out,
    text_up,
    text_down,
    text_norm,
    layout_qkv,
    layout_out,
    layout_up,
    layout_down,
    layout_norm,
):
    dp_pages = page_length.shape[0]
    dp, tensor = lax.axis_size("dp"), lax.axis_size("tensor")
    width, lay_width = text_input.shape[1], layout_input.shape[1]
    text_rows, lay_rows = width // DB, lay_width // DB

    own = text_qkv.shape[0]
    qkv_own = text_qkv.reshape(own, -1)
    up_own = jnp.concatenate([text_up, text_out.T], axis=1)
    down_own = text_down.T
    lay_own = jnp.concatenate(
        [layout_qkv.reshape(layout_qkv.shape[0], -1), layout_out.T, layout_up, layout_down.T], axis=1
    )
    lengths = page_length.astype(F32)
    mine = jnp.arange(dp_pages, dtype=jnp.int32) == lax.axis_index("tensor")
    length = jnp.sum(jnp.where(mine, page_length, 0)).reshape(1)
    group = jnp.sum(jnp.where(mine, page_group, 0)).reshape(1)
    base = float(dp_pages * dp * S) / (2.0 * NGROUPS)
    paired = dp == DB and tensor == TB
    everywhere = ("tensor", "dp")
    if paired:
        column = lax.broadcasted_iota(jnp.int32, (LROWS - lay_rows, lay_own.shape[1]), 1) == group[0]
        part = lax.broadcasted_iota(jnp.int32, column.shape, 0)
        digit = jnp.where(part == 0, length[0] // 32, jnp.where(part == 1, length[0] % 32, 0))
        spare = jnp.where(column, digit, 0).astype(BF)
        a_bits, u_bits, d_bits = BITS
        a_in = gather_pieces(jnp.concatenate([qkv_own, lay_own, spare], axis=0), a_bits)
        u_in = gather_pieces(up_own, u_bits)
        d_in = gather_pieces(down_own, d_bits)
        a_map, u_map, d_map = spread(a_bits), spread(u_bits), spread(d_bits)
        me = (lax.axis_index("dp") * TB + lax.axis_index("tensor")).astype(jnp.int32).reshape(1)
        counts = jnp.zeros((NGROUPS,), F32)
    else:

        def gather(array, rows):
            whole = lax.all_gather(array, everywhere, axis=0, tiled=True)
            return whole.reshape(TB * DB, rows, array.shape[1])

        first = jnp.concatenate(
            [
                gather(qkv_own, text_rows),
                jnp.pad(gather(lay_own, lay_rows), ((0, 0), (0, LROWS - lay_rows), (0, 0))),
            ],
            axis=1,
        )
        order = tuple(d * TB + t for t in range(TB) for d in range(DB))
        a_in, u_in, d_in = [first], [gather(up_own, text_rows)], [gather(down_own, text_rows)]
        a_map = u_map = d_map = (order,)
        me = jnp.zeros((1,), jnp.int32)
        labels = jnp.arange(NGROUPS, dtype=jnp.int32)
        member = (page_group[:, None] == labels[None, :]).astype(F32)
        counts = lax.psum(jnp.sum(member * lengths[:, None], axis=0), "dp")
    counts = jnp.pad(counts, (0, 128 - NGROUPS)).reshape(1, 128)

    select = jnp.asarray(
        [[1.0 if b == (a // lay_rows) * LROWS + a % lay_rows else 0.0 for b in range(DB * LROWS)]
         for a in range(lay_width)],
        BF,
    )
    qw, ow, fw = qkv_own.shape[1], text_out.shape[0], text_up.shape[1]
    lqw, low, lfw = layout_qkv.shape[2] * 3, layout_out.shape[0], layout_up.shape[1]
    lpack = lay_own.shape[1]
    spots = (0, 0, fw)
    sems = lambda n: pltpu.SemaphoreType.DMA((n,))
    outs_of = lambda maps, rows, wide: [sds((len(m), rows, wide), BF) for m in maps]
    V = pltpu.VMEM
    flop = 2.0 * S * width

    qkv, lqkv, ctx, lctx, lse, wl, weight = call(
        functools.partial(attention_forward, a_map, len(a_in), base, lay_rows if paired else None),
        "attention_forward",
        [(me, 1), (length, 1), (group, 1), (counts, 0), (text_input, 0), (layout_input, 0), (select, 0)],
        a_in,
        [sds((TB, S, qw), BF), sds((TB, S, lqw), BF), sds((TB, S, ow), BF), sds((TB, S, low), BF),
         sds((TB, S, 128), F32), sds((TB, lay_width, lpack), BF), sds((8, 128), F32)],
        [],
        [V((TB, width, qw), BF), V((TB, DB * LROWS, lpack), BF), sems(2)],
        cost(flop * 4 * (qw + 3 * S), 16e6, 3e6),
    )
    (result, lresult, hid, slope, lhid, lslope, mid, lmid, gb, lgb, ge, lge, n1, ln1, i1, tg2, lg2) = call(
        functools.partial(ffn_forward, (u_map, d_map), (len(u_in), len(d_in)), spots),
        "ffn_forward",
        [(me, 1), (length, 1), (weight, 0), (text_input, 0), (layout_input, 0), (ctx, 0), (lctx, 0), (wl, 0),
         (text_norm, 0), (layout_norm, 0), (text_cotangent, 0), (layout_cotangent, 0)],
        u_in + d_in,
        [sds((S, width), F32), sds((S, lay_width), F32), sds((TB, S, fw), BF), sds((TB, S, fw), F32),
         sds((TB, S, lfw), BF), sds((TB, S, lfw), F32), sds((S, width), BF), sds((S, lay_width), BF),
         sds((S, width), BF), sds((S, lay_width), BF), sds((S, width), F32), sds((S, lay_width), F32),
         sds((S, width), F32), sds((S, lay_width), F32), sds((S, 128), F32), sds((2, width), F32),
         sds((2, lay_width), F32)],
        [],
        [V((TB, width, fw), BF), V((TB, width, fw), BF), V((TB, width, ow), BF), V((S, width), F32), sems(3)],
        cost(flop * 4 * (2 * fw + ow), 40e6, 4e6),
    )
    d_rows, u_wide = down_own.shape[1], up_own.shape[1]
    *d_out, ldg = call(
        functools.partial(down_grads, d_map),
        "down_grads",
        [(me, 1), (gb, 0), (lgb, 0), (hid, 0), (lhid, 0)],
        [],
        [sds((TB, lay_width, lfw), BF)],
        outs_of(d_map, text_rows, fw),
        [V((TB, width, fw), BF), V((width, S), BF), V((lay_width, S), BF), pltpu.SemaphoreType.DMA],
        cost(flop * 4 * fw, 10e6),
    )
    *u_out, g1, lg1, dctx, ldctx, luo, tg1, lg1n = call(
        functools.partial(ffn_backward, (u_map, d_map), (len(u_in), len(d_in)), spots, u_map),
        "ffn_backward",
        [(me, 1), (gb, 0), (lgb, 0), (ge, 0), (lge, 0), (slope, 0), (lslope, 0), (mid, 0), (lmid, 0), (n1, 0),
         (ln1, 0), (i1, 0), (ctx, 0), (lctx, 0), (wl, 0), (text_norm, 0), (layout_norm, 0)],
        u_in + d_in,
        [sds((S, width), F32), sds((S, lay_width), F32), sds((TB, S, ow), BF), sds((TB, S, low), BF),
         sds((TB, lay_width, low + lfw), BF), sds((2, width), F32), sds((2, lay_width), F32)],
        outs_of(u_map, text_rows, u_wide),
        [V((TB, width, fw), BF), V((TB, width, fw), BF), V((TB, width, ow), BF), V((TB, width, fw), BF),
         V((TB, width, ow), BF), V((S, width), F32), V((S, lay_width), F32), V((width, S), BF),
         V((lay_width, S), BF), sems(5)],
        cost(flop * 4 * (3 * fw + 2 * ow), 40e6),
    )
    *a_out, dx, dxl = call(
        functools.partial(attention_backward, a_map, len(a_in), a_map),
        "attention_backward",
        [(me, 1), (length, 1), (text_input, 0), (layout_input, 0), (select.T, 0), (qkv, 0), (lqkv, 0), (ctx, 0),
         (lctx, 0), (dctx, 0), (ldctx, 0), (lse, 0), (g1, 0), (lg1, 0), (wl, 0), (luo, 0), (ldg, 0)],
        a_in,
        [sds((S, width), F32), sds((S, lay_width), F32)],
        outs_of(a_map, text_rows + LROWS, qw),
        [V((TB, width, qw), BF), V((S, qw), BF), V((S, lqw), BF), V((TB, width, qw), BF),
         V((TB, DB * LROWS, lpack), BF), V((width, S), BF), V((lay_width, S), BF), sems(3)],
        cost(flop * 4 * (2 * qw + 6 * S), 30e6, 3e6),
    )

    both = [jnp.concatenate([tg1, tg2]), jnp.concatenate([lg1n, lg2])]
    if paired:
        d_grad = scatter_pieces(d_out, d_bits)
        u_grad = scatter_pieces(u_out, u_bits)
        a_grad = scatter_pieces(a_out, a_bits)
        q_grad, l_grad = a_grad[:text_rows], a_grad[text_rows : text_rows + lay_rows]
        both = total_over_all(jnp.concatenate(both, axis=1), a_bits)
        tg, lg = both[:, :width], both[:, width:]
    else:

        def scatter(array):
            flat = array.reshape(-1, array.shape[2])
            return lax.psum_scatter(flat, everywhere, scatter_dimension=0, tiled=True).astype(F32)

        d_grad = scatter(d_out[0])
        u_grad = scatter(u_out[0])
        q_grad = scatter(a_out[0][:, :text_rows])
        l_grad = scatter(a_out[0][:, text_rows : text_rows + lay_rows])
        tg, lg = lax.psum(tuple(both), ("dp", "tensor"))
    return (
        result,
        lresult,
        dx,
        dxl,
        q_grad.reshape(text_qkv.shape),
        u_grad[:, fw:].T,
        u_grad[:, :fw],
        d_grad.T,
        tg,
        l_grad[:, :lqw].reshape(layout_qkv.shape),
        l_grad[:, lqw : lqw + low].T,
        l_grad[:, lqw + low : lqw + low + lfw],
        l_grad[:, lqw + low + lfw :].T,
        lg,
    )


def solution(mesh):
    in_specs = (
        P(("dp", "tensor"), None),
        P(("dp", "tensor"), None),
        P(("dp", "tensor"), None),
        P(("dp", "tensor"), None),
        P("dp"),
        P("dp"),
        P("dp", None, "tensor"),
        P("tensor", "dp"),
        P("dp", "tensor"),
        P("tensor", "dp"),
        P(),
        P("dp", None, "tensor"),
        P("tensor", "dp"),
        P("dp", "tensor"),
        P("tensor", "dp"),
        P(),
    )
    out_specs = (
        P(("dp", "tensor"), None),
        P(("dp", "tensor"), None),
        P(("dp", "tensor"), None),
        P(("dp", "tensor"), None),
        P("dp", None, "tensor"),
        P("tensor", "dp"),
        P("dp", "tensor"),
        P("tensor", "dp"),
        P(),
        P("dp", None, "tensor"),
        P("tensor", "dp"),
        P("dp", "tensor"),
        P("tensor", "dp"),
        P(),
    )
    return jax.shard_map(body, mesh=mesh, in_specs=in_specs, out_specs=out_specs, check_vma=False)
```

```python
import functools
import math

import jax
import jax.numpy as jnp
import numpy as np
from jax import lax
from jax.experimental import pallas as pl
from jax.experimental.layout import Layout, with_layout_constraint
from jax.experimental.pallas import tpu as pltpu
from jax.sharding import PartitionSpec as P

TEXT_HEAD = 64
LAY_HEAD = 16
S = 512
NGROUPS = 8

TB = 4
DB = 8
LROWS = 32

SPLIT = ((2, 4), (4, 2))
SAME = ((2, 4), (2, 4))

epsilon = 1e-05
neg_large = -1e30
root_half = 1.0 / math.sqrt(2.0)
root_twopi = 1.0 / math.sqrt(2.0 * math.pi)
text_scale = float(TEXT_HEAD) ** (-0.5)
layout_scale = float(LAY_HEAD) ** (-0.5)

HINT = 0.1
BF = jnp.bfloat16
F32 = jnp.float32
ANY = pl.BlockSpec(memory_space=pl.ANY)
VM = pl.BlockSpec(memory_space=pltpu.VMEM)
SM = pl.BlockSpec(memory_space=pltpu.SMEM)
PARAMS = pltpu.CompilerParams(vmem_limit_bytes=60 * 1024 * 1024)


def nn(a, b):
    return jnp.dot(a, b, preferred_element_type=F32)


def nt(a, b):
    return lax.dot_general(a, b, (((1,), (1,)), ((), ())), preferred_element_type=F32)


def sds(shape, dtype):
    return jax.ShapeDtypeStruct(shape, dtype)


def cost(flops, read, trans=0):
    return pl.CostEstimate(flops=int(flops * HINT), bytes_accessed=int(read * HINT), transcendentals=int(trans * HINT))


def load_pieces(refs, maps, d0, size, lanes, dst, sem):
    for ref, entries in zip(refs, maps):
        for i, entry in enumerate(entries):
            if entry is None:
                continue
            rel, start, rows = entry
            spot = pl.multiple_of(((rel // TB) ^ d0) * size + start, rows)
            pltpu.make_async_copy(
                ref.at[i, :, lanes[0] : lanes[1]], dst.at[rel % TB, pl.ds(spot, rows), :], sem
            ).start()


def send_pieces(outs, maps, d0, buf, size, lanes, sem):
    for out, entries in zip(outs, maps):
        for i, entry in enumerate(entries):
            if entry is None:
                continue
            rel, start, rows = entry
            spot = pl.multiple_of(((rel // TB) ^ d0) * size + start, rows)
            pltpu.make_async_copy(
                buf.at[rel % TB, pl.ds(spot, rows), :], out.at[i, :, lanes[0] : lanes[1]], sem
            ).start()


def wait_pieces(dst, sem):
    pltpu.make_async_copy(dst, dst, sem).wait()


class Refs:
    def __init__(self, **entries):
        self.__dict__.update(entries)


def run(kernel, name, price, scalars, arrays, hbm, outs, hbm_outs, scratch):
    ins, in_tree = jax.tree.flatten((scalars, arrays, hbm))
    in_specs = [SM] * len(jax.tree.leaves(scalars)) + [VM] * len(jax.tree.leaves(arrays))
    in_specs += [ANY] * len(jax.tree.leaves(hbm))
    out_shapes, out_tree = jax.tree.flatten((outs, hbm_outs))
    out_specs = [VM] * len(jax.tree.leaves(outs)) + [ANY] * len(jax.tree.leaves(hbm_outs))
    scratch_shapes, scratch_names = list(scratch.values()), list(scratch)

    def inner(*refs):
        a, b = len(ins), len(ins) + len(out_shapes)
        s, v, h = jax.tree.unflatten(in_tree, refs[:a])
        o, ho = jax.tree.unflatten(out_tree, refs[a:b])
        kernel(Refs(**s, **v, **h, **o, **ho, **dict(zip(scratch_names, refs[b:]))))

    got = pl.pallas_call(
        inner,
        name=name,
        in_specs=in_specs,
        out_specs=out_specs,
        out_shape=out_shapes,
        scratch_shapes=scratch_shapes,
        compiler_params=PARAMS,
        cost_estimate=cost(*price),
    )(*ins)
    o, ho = jax.tree.unflatten(out_tree, got)
    return Refs(**o, **ho)


def attention_forward(maps, counted, k):
    d0 = k.me[0] // TB
    lay_width = k.select.shape[1]
    text_rows, lay_rows = k.wq.shape[1] // DB, lay_width // DB
    width = k.qkv.shape[1]
    load_pieces(k.w, maps, d0, text_rows, (0, k.wq.shape[2]), k.wq, k.sem)
    live = lax.broadcasted_iota(jnp.int32, (1, S), 1) < k.length[0]
    heads = width // 3 // TEXT_HEAD
    tw, lw = heads * TEXT_HEAD, heads * LAY_HEAD
    if hasattr(k, "xt"):
        k.xt[...] = k.x[...].T
        k.xlt[...] = k.xl[...].T
    wait_pieces(k.wq, k.sem)
    packed = k.wq[0, :, width:]
    if counted:
        place = lax.broadcasted_iota(jnp.int32, (8, k.wq.shape[1]), 1) % text_rows
        digits = jnp.where(place == lay_rows, 32.0, jnp.where(place == lay_rows + 1, 1.0, 0.0)).astype(BF)
        k.counts[...] = nn(digits, packed[:, 0:128])
    else:
        k.counts[...] = jnp.zeros(k.counts.shape, F32)
    wlt = jnp.concatenate([nn(k.select[j], packed).astype(BF) for j in range(3)], axis=1)
    k.wlay[...] = wlt
    qkv = nn(k.x[...], k.wq[0, :, 0:width]).astype(BF)
    k.qkv[...] = qkv
    lqkv = nn(k.xl[...], wlt[:, : 3 * lw]).astype(BF)
    k.lqkv[...] = lqkv
    for h in range(heads):
        a, b = h * TEXT_HEAD, h * LAY_HEAD
        ta, tb = slice(a, a + TEXT_HEAD), slice(b, b + LAY_HEAD)
        q = jnp.concatenate([qkv[:, ta] * BF(text_scale), lqkv[:, tb] * BF(layout_scale)], axis=1)
        key = jnp.concatenate([qkv[:, tw + a : tw + a + TEXT_HEAD], lqkv[:, lw + b : lw + b + LAY_HEAD]], axis=1)
        v = jnp.concatenate(
            [qkv[:, 2 * tw + a : 2 * tw + a + TEXT_HEAD], lqkv[:, 2 * lw + b : 2 * lw + b + LAY_HEAD]], axis=1
        )
        logits = jnp.where(live, nt(q, key), neg_large)
        top = jnp.max(logits, axis=-1, keepdims=True)
        raw = jnp.exp(logits - top)
        total = jnp.sum(raw, axis=-1, keepdims=True)
        probs = (raw * (1.0 / total)).astype(BF)
        ctx = nn(probs, v).astype(BF)
        k.ctx[:, ta] = ctx[:, :TEXT_HEAD]
        k.lctx[:, tb] = ctx[:, TEXT_HEAD:]
        k.lse[:, h : h + 1] = top + jnp.log(total)


def ffn_forward(maps, spots, base, k):
    d0 = k.me[0] // TB
    rows, fw, ow = k.wu.shape[1] // DB, k.wu.shape[2], k.wo.shape[2]
    low = k.lctx[0].shape[1]
    lf = (k.wlay[0].shape[1] - 4 * low) // 2
    load_pieces(k.u, maps[0], d0, rows, (fw, fw + ow), k.wo, k.sems.at[0])
    load_pieces(k.u, maps[0], d0, rows, (0, fw), k.wu, k.sems.at[1])
    load_pieces(k.d, maps[1], d0, rows, (0, fw), k.wd, k.sems.at[2])
    counts = k.known[...]
    for t in range(TB):
        counts = counts + k.counts[t][0:1]
    same = lax.broadcasted_iota(jnp.int32, counts.shape, 1) == k.group[0]
    mine = jnp.sum(jnp.where(same, counts, 0.0), axis=1, keepdims=True)
    keep = (lax.broadcasted_iota(jnp.int32, (S, 1), 0) < k.length[0]).astype(F32)
    scale = keep * (base / (mine + base))
    tn, ln = k.tn[...], k.ln[...]
    lattn = nt(k.lctx[0][...], k.wlay[0][:, 3 * low : 4 * low])
    for t in range(1, TB):
        lattn = lattn + nt(k.lctx[t][...], k.wlay[t][:, 3 * low : 4 * low])
    wait_pieces(k.wo, k.sems.at[0])
    attn = nt(k.ctx[0][...], k.wo[0])
    for t in range(1, TB):
        attn = attn + nt(k.ctx[t][...], k.wo[t])
    n1, i1 = norm_stats(k.x[...].astype(F32) + attn)
    mid = n1 * tn[0:1] + tn[1:2]
    ln1, li1 = norm_stats(k.xl[...].astype(F32) + lattn)
    lmid = ln1 * ln[0:1] + ln[1:2]
    k.n1[...] = n1
    k.ln1[...] = ln1
    k.i1[:, 0:1] = i1
    k.i1[:, 1:2] = li1
    k.mid[...] = mid.astype(BF)
    k.lmid[...] = lmid.astype(BF)
    k.branch[...] = mid
    k.lbranch[...] = lmid
    wait_pieces(k.wu, k.sems.at[1])
    wait_pieces(k.wd, k.sems.at[2])

    def gelu(before):
        cdf = 0.5 * (1.0 + lax.erf(before * root_half))
        return (before * cdf).astype(BF), cdf + before * jnp.exp(-0.5 * before * before) * root_twopi

    def step(t, carry):
        hid, slope = gelu(nn(k.mid[...], k.wu[t]))
        k.hid[t] = hid
        k.slope[t] = slope
        k.branch[...] += nt(hid, k.wd[t])
        return carry

    lax.fori_loop(0, TB, step, 0)
    for t in range(TB):
        lhid, lslope = gelu(nn(k.lmid[...], k.wlay[t][:, 4 * low : 4 * low + lf]))
        k.lhid[t] = lhid
        k.lslope[t] = lslope
        k.lbranch[...] += nt(lhid, k.wlay[t][:, 4 * low + lf :])
    n2, i2 = norm_stats(k.branch[...])
    k.result[...] = (n2 * tn[2:3] + tn[3:4]) * keep
    ge, gain, shift = norm_back(k.cot[...] * scale, n2, i2, tn[2:3])
    k.ge[...] = ge
    k.gb[...] = ge.astype(BF)
    k.tg[0:1] = gain
    k.tg[1:2] = shift
    ln2, li2 = norm_stats(k.lbranch[...])
    k.lresult[...] = (ln2 * ln[2:3] + ln[3:4]) * keep
    lge, lgain, lshift = norm_back(k.lcot[...] * scale, ln2, li2, ln[2:3])
    k.lge[...] = lge
    k.lgb[...] = lge.astype(BF)
    k.lg[0:1] = lgain
    k.lg[1:2] = lshift


def down_grads(maps, k):
    rows, width = k.buf.shape[1] // DB, k.buf.shape[2]
    k.gbt[...] = k.gb[...].T
    k.lgbt[...] = k.lgb[...].T

    def step(t, carry):
        k.buf[t] = nn(k.gbt[...], k.hid[t]).astype(BF)
        return carry

    lax.fori_loop(0, TB, step, 0)
    send_pieces(k.out, maps, k.me[0] // TB, k.buf, rows, (0, width), k.sem)
    for t in range(TB):
        k.ldown[t][...] = nn(k.lgbt[...], k.lhid[t]).astype(BF)
    wait_pieces(k.buf, k.sem)


def ffn_backward(maps, k):
    d0 = k.me[0] // TB
    rows, fw, ow = k.wu.shape[1] // DB, k.wu.shape[2], k.wo.shape[2]
    low = k.ldctx[0].shape[1]
    lf = (k.wlay[0].shape[1] - 4 * low) // 2
    load_pieces(k.d, maps[1], d0, rows, (0, fw), k.wd, k.sems.at[0])
    load_pieces(k.u, maps[0], d0, rows, (0, fw), k.wu, k.sems.at[1])
    load_pieces(k.u, maps[0], d0, rows, (fw, fw + ow), k.wo, k.sems.at[2])
    tn, ln = k.tn[...], k.ln[...]
    k.acc[...] = k.ge[...]
    k.lacc[...] = k.lge[...]
    for t in range(TB):
        ldbef = (nn(k.lgb[...], k.wlay[t][:, 4 * low + lf :]) * k.lslope[t]).astype(BF)
        k.ldbef[t] = ldbef
        k.lacc[...] += nt(ldbef, k.wlay[t][:, 4 * low : 4 * low + lf])
    wait_pieces(k.wd, k.sems.at[0])
    wait_pieces(k.wu, k.sems.at[1])

    def step(t, carry):
        dbef = (nn(k.gb[...], k.wd[t]) * k.slope[t]).astype(BF)
        k.dbef[t] = dbef
        k.acc[...] += nt(dbef, k.wu[t])
        return carry

    lax.fori_loop(0, TB, step, 0)
    g1, gain, shift = norm_back(k.acc[...], k.n1[...], k.i1[:, 0:1], tn[0:1])
    k.g1[...] = g1
    k.tg[0:1] = gain
    k.tg[1:2] = shift
    lg1, lgain, lshift = norm_back(k.lacc[...], k.ln1[...], k.i1[:, 1:2], ln[0:1])
    k.lg1[...] = lg1
    k.lg[0:1] = lgain
    k.lg[1:2] = lshift
    ga = g1.astype(BF)
    lga = lg1.astype(BF)
    wait_pieces(k.wo, k.sems.at[2])
    for t in range(TB):
        k.dctx[t][...] = nn(ga, k.wo[t]).astype(BF)
        k.ldctx[t][...] = nn(lga, k.wlay[t][:, 3 * low : 4 * low]).astype(BF)


def up_grads(maps, k):
    rows, fw, ow = k.buf.shape[1] // DB, k.buf.shape[2], k.obuf.shape[2]
    low = k.lctx[0].shape[1]
    d0 = k.me[0] // TB
    k.rt[...] = k.g1[...].astype(BF).T
    k.lrt[...] = k.lg1[...].astype(BF).T
    for t in range(TB):
        k.obuf[t] = nn(k.rt[...], k.ctx[t][...]).astype(BF)
        k.lup[t][:, 0:low] = nn(k.lrt[...], k.lctx[t][...]).astype(BF)
    send_pieces(k.out, maps, d0, k.obuf, rows, (fw, fw + ow), k.sems.at[1])
    k.rt[...] = k.mid[...].T
    k.lrt[...] = k.lmid[...].T

    def step(t, carry):
        k.buf[t] = nn(k.rt[...], k.dbef[t]).astype(BF)
        return carry

    lax.fori_loop(0, TB, step, 0)
    send_pieces(k.out, maps, d0, k.buf, rows, (0, fw), k.sems.at[0])
    for t in range(TB):
        k.lup[t][:, low:] = nn(k.lrt[...], k.ldbef[t]).astype(BF)
    wait_pieces(k.obuf, k.sems.at[1])
    wait_pieces(k.buf, k.sems.at[0])


def attention_backward(maps, k):
    width = k.qkv.shape[1]
    heads = width // 3 // TEXT_HEAD
    tw, lw = heads * TEXT_HEAD, heads * LAY_HEAD
    text_rows = k.buf.shape[1] // DB
    live = lax.broadcasted_iota(jnp.int32, (1, S), 1) < k.length[0]
    for h in range(heads):
        a, b = h * TEXT_HEAD, h * LAY_HEAD
        ta, tb = slice(a, a + TEXT_HEAD), slice(b, b + LAY_HEAD)
        ka, kb = slice(tw + a, tw + a + TEXT_HEAD), slice(lw + b, lw + b + LAY_HEAD)
        va, vb = slice(2 * tw + a, 2 * tw + a + TEXT_HEAD), slice(2 * lw + b, 2 * lw + b + LAY_HEAD)
        qt, ql = k.qkv[:, ta] * BF(text_scale), k.lqkv[:, tb] * BF(layout_scale)
        kt, kl = k.qkv[:, ka], k.lqkv[:, kb]
        vt, vl = k.qkv[:, va], k.lqkv[:, vb]
        gt, gl = k.dctx[:, ta], k.ldctx[:, tb]
        q = jnp.concatenate([qt, ql], axis=1)
        key = jnp.concatenate([kt, kl], axis=1)
        v = jnp.concatenate([vt, vl], axis=1)
        g = jnp.concatenate([gt, gl], axis=1)
        dot_t = jnp.sum(gt.astype(F32) * k.ctx[:, ta].astype(F32), axis=-1, keepdims=True)
        dot_s = dot_t + jnp.sum(gl.astype(F32) * k.lctx[:, tb].astype(F32), axis=-1, keepdims=True)
        logits = jnp.where(live, nt(q, key), neg_large)
        probs = jnp.exp(logits - k.lse[:, h : h + 1])
        low = (probs * (nt(gt, vt) - dot_t)).astype(BF)
        llow = (probs * (nt(g, v) - dot_s)).astype(BF)
        k.dqkv[:, ta] = (nn(low, kt) * text_scale).astype(BF)
        k.ldqkv[:, tb] = (nn(llow, kl) * layout_scale).astype(BF)
        dk = nn(qt.T, low).T
        dkl = nn(ql.T, llow).T
        dv = nn(g.T, probs.astype(BF)).T
        k.dqkv[:, ka] = dk.astype(BF)
        k.ldqkv[:, kb] = dkl.astype(BF)
        k.dqkv[:, va] = dv[:, :TEXT_HEAD].astype(BF)
        k.ldqkv[:, vb] = dv[:, TEXT_HEAD:].astype(BF)
    k.buf[0, :, 0:width] = nn(k.xt[...], k.dqkv[...]).astype(BF)
    lgrad = jnp.concatenate([nn(k.xlt[...], k.ldqkv[...]).astype(BF), k.lup[...], k.ldown[...]], axis=1)
    third = width // 3
    packed = nn(k.selt[0], lgrad[:, 0:third])
    for j in range(1, 3):
        packed = packed + nn(k.selt[j], lgrad[:, j * third : (j + 1) * third])
    k.buf[0, :, width:] = packed.astype(BF)
    d0 = k.me[0] // TB
    send_pieces(k.out, maps, d0, k.buf, text_rows, (0, k.buf.shape[2]), k.sem)
    wait_pieces(k.buf, k.sem)


def input_grads(maps, k):
    d0 = k.me[0] // TB
    text_rows, width = k.wq.shape[1] // DB, k.dqkv[0].shape[1]
    lw = k.ldqkv[0].shape[1]
    load_pieces(k.w, maps, d0, text_rows, (0, k.wq.shape[2]), k.wq, k.sem)
    dxl = k.lg1[...]
    for t in range(TB):
        dxl = dxl + nt(k.ldqkv[t][...], k.wlay[t][:, :lw])
    k.dxl[...] = dxl
    wait_pieces(k.wq, k.sem)
    dx = k.g1[...]
    for t in range(TB):
        dx = dx + nt(k.dqkv[t][...], k.wq[t, :, 0:width])
    k.dx[...] = dx


def norm_stats(values):
    centred = values - jnp.mean(values, axis=-1, keepdims=True)
    inverse = lax.rsqrt(jnp.mean(centred * centred, axis=-1, keepdims=True) + epsilon)
    return centred * inverse, inverse


def norm_back(upstream, normed, inverse, gain):
    scaled = upstream * gain
    inner = (
        scaled
        - jnp.mean(scaled, axis=-1, keepdims=True)
        - normed * jnp.mean(scaled * normed, axis=-1, keepdims=True)
    )
    return (
        inverse * inner,
        jnp.sum(upstream * normed, axis=0, keepdims=True),
        jnp.sum(upstream, axis=0, keepdims=True),
    )


def exchange(array, bit):
    size = lax.axis_size("dp") * lax.axis_size("tensor")
    return lax.ppermute(array, ("dp", "tensor"), [(i, i ^ bit) for i in range(size)])


Z = (0, 8, 16, 24)


def gather_maps(rows):
    half = rows // 2
    tops = ((0, 0, 2), (4, 0, 2), (0, half, 4), (2, half, 4))
    return tuple(
        tuple((z | inner | top | core, start, half) for inner in (0, step) for z in Z)
        for core in (0, 1)
        for top, start, step in tops
    )


def scatter_maps(start, rows, bits):
    return tuple(
        tuple((z | inner | top, start, rows) for inner in (0, bits[1]) for z in Z)
        for top in (0, 1, bits[0], bits[0] | 1)
    )


def block(maps, t):
    return tuple(
        tuple((rel - t, start, rows) if rel % TB == t else None for rel, start, rows in entries) for entries in maps
    )


def after(array, *needed):
    return lax.optimization_barrier((array, needed))[0]


def rows_major(array):
    return with_layout_constraint(array, Layout(major_to_minor=(0, 1, 2)))


class Gather:
    def __init__(self, own):
        self.own, self.half = rows_major(own[None]), own.shape[0] // 2

    def along_z(self):
        got = [self.own] + [rows_major(exchange(self.own, z)) for z in Z[1:]]
        self.upper = rows_major(jnp.concatenate([g[:, : self.half] for g in got], axis=0))
        self.lower = rows_major(jnp.concatenate([g[:, self.half :] for g in got], axis=0))
        return self.lower

    def sides(self):
        self.upper = rows_major(jnp.concatenate([self.upper, exchange(self.upper, 2)], axis=0))
        self.lower = rows_major(jnp.concatenate([self.lower, exchange(self.lower, 4)], axis=0))
        return self.lower

    def cross(self):
        self.here = [self.upper, rows_major(exchange(self.upper, 4)), self.lower, rows_major(exchange(self.lower, 2))]
        return self.here

    def cores(self):
        return [rows_major(exchange(array, 1)) for array in self.here]


def rounded(parts):
    return rows_major(sum(p.astype(F32) for p in parts).astype(BF))


class Scatter:
    def __init__(self, bits):
        self.bits = bits

    def swap(self, arrays):
        return [exchange(array, 1) for array in arrays]

    def first(self, h, far, near):
        self.sent = rounded([far, near])
        return exchange(self.sent, self.bits[h][0])

    def side(self, parts):
        self.parts = parts
        self.sent = [rounded([p[4:8] for p in half]) for half in parts]
        return [exchange(sent, self.bits[h][1]) for h, sent in enumerate(self.sent)]

    def along_z(self, got):
        self.parts = [half + [g] for half, g in zip(self.parts, got)]
        self.sent = [
            rows_major(jnp.concatenate([rounded([p[i : i + 1] for p in half]) for half in self.parts], axis=1))
            for i in range(1, 4)
        ]
        return [exchange(piece, z) for piece, z in zip(self.sent, Z[1:])]

    def finish(self, got):
        kept = jnp.concatenate([sum(p[0].astype(F32) for p in half) for half in self.parts], axis=0)
        return kept + sum(g[0].astype(F32) for g in got)


def body(
    text_input,
    layout_input,
    text_cotangent,
    layout_cotangent,
    page_group,
    page_length,
    text_qkv,
    text_out,
    text_up,
    text_down,
    text_norm,
    layout_qkv,
    layout_out,
    layout_up,
    layout_down,
    layout_norm,
):
    dp_pages = page_length.shape[0]
    dp, tensor = lax.axis_size("dp"), lax.axis_size("tensor")
    width, lay_width = text_input.shape[1], layout_input.shape[1]
    text_rows, lay_rows = width // DB, lay_width // DB

    qkv_own = jnp.concatenate([text_qkv[:, i] for i in range(3)], axis=1)
    up_own = jnp.concatenate([text_up, text_out.T], axis=1)
    down_own = text_down.T
    lay_own = jnp.concatenate(
        [layout_qkv[:, i] for i in range(3)] + [layout_out.T, layout_up, layout_down.T], axis=1
    )
    qw, ow, fw = qkv_own.shape[1], text_out.shape[0], text_up.shape[1]
    low, lfw, lpack = layout_out.shape[0], layout_up.shape[1], lay_own.shape[1]
    mine = jnp.arange(dp_pages, dtype=jnp.int32) == lax.axis_index("tensor")
    length = jnp.sum(jnp.where(mine, page_length, 0)).reshape(1)
    group = jnp.sum(jnp.where(mine, page_group, 0)).reshape(1)
    base = float(dp_pages * dp * S) / (2.0 * NGROUPS)
    paired = dp == DB and tensor == TB
    everywhere = ("tensor", "dp")
    if paired:
        column = lax.broadcasted_iota(jnp.int32, (LROWS - lay_rows, lpack), 1) == group[0]
        part = lax.broadcasted_iota(jnp.int32, column.shape, 0)
        digit = jnp.where(part == 0, length[0] // 32, jnp.where(part == 1, length[0] % 32, 0))
        spare = jnp.where(column, digit, 0).astype(BF)
        packed = jnp.concatenate([lay_own, spare], axis=0)
        packed = jnp.concatenate([packed[:, i * ow : (i + 1) * ow] for i in range(3)], axis=0)
        ga = Gather(jnp.concatenate([qkv_own, packed], axis=1))
        ga.along_z()
        ga.sides()
        gd = Gather(after(down_own, ga.upper, ga.lower))
        ga.cross()
        gd.along_z()
        weights_map = gather_maps(text_rows)
        a_map = [block(weights_map[4 * (t % 2) : 4 * (t % 2) + 4], t) for t in range(TB)]
        u_map = d_map = weights_map
        half = text_rows // 2
        u_send = d_send = scatter_maps(0, half, SPLIT[0]) + scatter_maps(half, half, SPLIT[1])
        a_send = [(block(scatter_maps(0, text_rows, SAME[0]), t)[t],) for t in range(TB)]
        me = (lax.axis_index("dp") * TB + lax.axis_index("tensor")).astype(jnp.int32).reshape(1)
        known = jnp.zeros((1, 128), F32)
    else:

        def gather(array, rows):
            whole = lax.all_gather(array, everywhere, axis=0, tiled=True)
            return whole.reshape(TB * DB, rows, array.shape[1])

        spare = ((0, 0), (0, LROWS - lay_rows), (0, 0))
        packed = jnp.pad(gather(lay_own, lay_rows), spare)
        packed = jnp.concatenate([packed[:, :, i * ow : (i + 1) * ow] for i in range(3)], axis=1)
        first = jnp.concatenate([gather(qkv_own, text_rows), packed], axis=2)
        a_in = [[first[t * DB : (t + 1) * DB]] for t in range(TB)]
        u_in, d_in = [gather(up_own, text_rows)], [gather(down_own, text_rows)]
        u_map = d_map = u_send = d_send = (tuple((d * TB + t, 0, text_rows) for t in range(TB) for d in range(DB)),)
        a_map = a_send = [(tuple((d * TB, 0, text_rows) for d in range(DB)),)] * TB
        me = jnp.zeros((1,), jnp.int32)
        labels = jnp.arange(NGROUPS, dtype=jnp.int32)
        member = (page_group[:, None] == labels[None, :]).astype(F32)
        counts = lax.psum(jnp.sum(member * page_length.astype(F32)[:, None], axis=0), "dp")
        known = jnp.pad(counts, (0, 128 - NGROUPS)).reshape(1, 128)

    chosen = np.zeros((3, lay_width, width), np.float32)
    for j in range(3):
        for a in range(lay_width):
            chosen[j, a, (a // lay_rows) * text_rows + j * LROWS + a % lay_rows] = 1.0
    select, select_t = jnp.asarray(chosen, BF), jnp.asarray(chosen.transpose(0, 2, 1), BF)
    V, dma = pltpu.VMEM, pltpu.SemaphoreType.DMA
    flop = 2.0 * S * width
    rows_f, rows_b = sds((S, width), F32), sds((S, width), BF)
    lay_f, lay_b = sds((S, lay_width), F32), sds((S, lay_width), BF)
    text_w, out_w, qkv_w = V((TB, width, fw), BF), V((TB, width, ow), BF), V((TB, width, qw + ow), BF)

    def attend(t, w):
        outs = dict(
            qkv=sds((S, qw), BF), lqkv=sds((S, 3 * low), BF), ctx=sds((S, ow), BF), lctx=sds((S, low), BF),
            lse=sds((S, 128), F32), wlay=sds((lay_width, lpack), BF), counts=sds((8, 128), F32),
        )
        if t == 0:
            outs.update(xt=sds((width, S), BF), xlt=sds((lay_width, S), BF))
        return run(
            functools.partial(attention_forward, a_map[t], paired), "attention_forward",
            (flop * (qw + 3 * S), 5e6, 1e6),
            dict(me=me, length=length), dict(x=text_input, xl=layout_input, select=select), dict(w=w),
            outs, {},
            dict(wq=V((1, width, qw + ow), BF), sem=dma),
        )

    if paired:
        ga.here, gd.upper, gd.lower = lax.optimization_barrier((ga.here, gd.upper, gd.lower))
        heads = [None] * TB
        gu = Gather(after(up_own, ga.here))
        a_far = ga.cores()
        gd.sides()
        gu.along_z()
        heads[0] = attend(0, ga.here)
        gd.upper, gd.lower, a_far, first, _ = lax.optimization_barrier(
            (gd.upper, gd.lower, a_far, ga.here[0], heads[0].ctx)
        )
        gd.cross()
        heads[2] = attend(2, [first] + ga.here[1:])
        gd.here, gu.upper, gu.lower, first, _ = lax.optimization_barrier(
            (gd.here, gu.upper, gu.lower, a_far[0], heads[2].ctx)
        )
        d_far = gd.cores()
        gu.sides()
        heads[1] = attend(1, [first] + a_far[1:])
        gu.upper, gu.lower, first, _ = lax.optimization_barrier((gu.upper, gu.lower, a_far[0], heads[1].ctx))
        gu.cross()
        heads[3] = attend(3, [first] + a_far[1:])
        gu.here = lax.optimization_barrier((gu.here, heads[3].ctx))[0]
        u_in, d_in = gu.here + gu.cores(), gd.here + d_far
        input_w, input_maps = ga.here + a_far, weights_map
    else:
        heads = [attend(t, a_in[t]) for t in range(TB)]
        input_w = [a[0] for a in a_in]
        input_maps = tuple(tuple((rel + t, start, rows) for rel, start, rows in a_map[t][0]) for t in range(TB))
    ctx, lctx = [h.ctx for h in heads], [h.lctx for h in heads]
    wlay = [h.wlay for h in heads]
    f = run(
        functools.partial(ffn_forward, (u_map, d_map), (0, 0, fw), base), "ffn_forward",
        (flop * 4 * (2 * fw + ow), 40e6, 4e6),
        dict(me=me, length=length, group=group),
        dict(x=text_input, xl=layout_input, ctx=ctx, lctx=lctx, wlay=wlay, counts=[h.counts for h in heads],
             known=known, tn=text_norm, ln=layout_norm, cot=text_cotangent, lcot=layout_cotangent),
        dict(u=u_in, d=d_in),
        dict(result=rows_f, lresult=lay_f, hid=sds((TB, S, fw), BF), slope=sds((TB, S, fw), F32),
             lhid=sds((TB, S, lfw), BF), lslope=sds((TB, S, lfw), F32), mid=rows_b, lmid=lay_b, gb=rows_b, lgb=lay_b,
             ge=rows_f, lge=lay_f, n1=rows_f, ln1=lay_f, i1=sds((S, 128), F32), tg=sds((2, width), F32),
             lg=sds((2, lay_width), F32)),
        {},
        dict(wu=text_w, wd=text_w, wo=out_w, branch=V((S, width), F32), lbranch=V((S, lay_width), F32),
             sems=dma((3,))),
    )

    def outs_of(maps, wide):
        return [sds((len(m), m[0][2], wide), BF) for m in maps]

    dg = run(
        functools.partial(down_grads, d_send), "down_grads", (flop * 4 * fw, 10e6),
        dict(me=me), dict(gb=f.gb, lgb=f.lgb, hid=f.hid, lhid=f.lhid), {},
        dict(ldown=[sds((lay_width, lfw), BF)] * TB), dict(out=outs_of(d_send, fw)),
        dict(buf=text_w, gbt=V((width, S), BF), lgbt=V((lay_width, S), BF), sem=dma),
    )
    b = run(
        functools.partial(ffn_backward, (u_map, d_map)), "ffn_backward", (flop * 4 * (2 * fw + ow), 40e6),
        dict(me=me),
        dict(gb=after(f.gb, dg.ldown[0]), lgb=f.lgb, ge=f.ge, lge=f.lge, slope=f.slope, lslope=f.lslope, n1=f.n1,
             ln1=f.ln1, i1=f.i1, wlay=wlay, tn=text_norm, ln=layout_norm),
        dict(u=u_in, d=d_in),
        dict(g1=rows_f, lg1=lay_f, dctx=[sds((S, ow), BF)] * TB, ldctx=[sds((S, low), BF)] * TB,
             dbef=sds((TB, S, fw), BF), ldbef=sds((TB, S, lfw), BF), tg=sds((2, width), F32),
             lg=sds((2, lay_width), F32)),
        {},
        dict(wu=text_w, wd=text_w, wo=out_w, acc=V((S, width), F32), lacc=V((S, lay_width), F32), sems=dma((3,))),
    )

    def up_part(mid):
        return run(
            functools.partial(up_grads, u_send), "up_grads", (flop * 4 * (fw + ow), 15e6),
            dict(me=me), dict(g1=b.g1, lg1=b.lg1, ctx=ctx, lctx=lctx, mid=mid, lmid=f.lmid, dbef=b.dbef, ldbef=b.ldbef),
            {},
            dict(lup=[sds((lay_width, low + lfw), BF)] * TB), dict(out=outs_of(u_send, fw + ow)),
            dict(buf=text_w, obuf=out_w, rt=V((width, S), BF), lrt=V((lay_width, S), BF), sems=dma((2,))),
        )

    def attend_back(t, dctx, ug):
        h = heads[t]
        return run(
            functools.partial(attention_backward, a_send[t]), "attention_backward", (flop * (qw + 6 * S), 8e6, 1e6),
            dict(me=me, length=length),
            dict(xt=heads[0].xt, xlt=heads[0].xlt, selt=select_t, qkv=h.qkv, lqkv=h.lqkv, ctx=h.ctx, lctx=h.lctx,
                 lse=h.lse, dctx=dctx, ldctx=b.ldctx[t], lup=ug.lup[t], ldown=dg.ldown[t]),
            {},
            dict(dqkv=sds((S, qw), BF), ldqkv=sds((S, 3 * low), BF)),
            dict(out=[sds((DB, text_rows, qw + ow), BF)]),
            dict(buf=V((1, width, qw + ow), BF), sem=dma),
        )

    def input_part(g1, back):
        return run(
            functools.partial(input_grads, input_maps), "input_grads", (flop * 4 * qw, 10e6),
            dict(me=me),
            dict(g1=g1, lg1=b.lg1, dqkv=[k.dqkv for k in back], ldqkv=[k.ldqkv for k in back], wlay=wlay),
            dict(w=input_w), dict(dx=rows_f, dxl=lay_f), {},
            dict(wq=qkv_w, sem=dma),
        )

    both = jnp.concatenate(
        [jnp.concatenate([b.tg, f.tg]), jnp.concatenate([b.lg, f.lg])], axis=1
    )
    if paired:
        ds, us, qs = Scatter(SPLIT), Scatter(SPLIT), Scatter(SAME)
        gate = lax.optimization_barrier
        tops = (0, 4)
        d_near, d_second = ds.swap([dg.out[i + 3] for i in tops]), ds.swap([dg.out[i + 1] for i in tops])
        d_near, d_second, done, both = gate((d_near, d_second, b.g1, both))
        norm = exchange(both, 1)
        got, sent = [], [done]
        for h in range(2):
            got.append(ds.first(h, dg.out[tops[h] + 2], d_near[h]))
            sent.append(ds.sent)
        ug = up_part(after(f.mid, sent))
        got, norm, done = gate((got, norm, ug.lup))
        both = both + norm
        norm = exchange(both, 2)
        u_near, u_second = us.swap([ug.out[i + 3] for i in tops]), us.swap([ug.out[i + 1] for i in tops])
        got = ds.side([[dg.out[tops[h]], d_second[h], got[h]] for h in range(2)])
        back = [None] * TB
        back[3] = attend_back(3, after(b.dctx[3], ds.sent, both, done), ug)
        got, u_near, u_second, norm, done = gate((got, u_near, u_second, norm, back[3].dqkv))
        both = both + norm
        norm = exchange(both, 4)
        a_near = exchange(back[3].out[0], 1)
        d_got = ds.along_z(got)
        got, sent = [], [done, ds.sent, both]
        for h in range(2):
            got.append(us.first(h, ug.out[tops[h] + 2], u_near[h]))
            sent.append(us.sent)
        back[2] = attend_back(2, after(b.dctx[2], sent), ug)
        got, d_got, a_near, norm, done = gate((got, d_got, a_near, norm, back[2].dqkv))
        d_grad = ds.finish(d_got)
        both = both + norm
        norm = exchange(both, 8)
        a_rows = (slice(0, half), slice(half, text_rows))
        got = us.side([[ug.out[tops[h]], u_second[h], got[h]] for h in range(2)])
        a_got = [None, qs.first(1, back[2].out[0][:, a_rows[1]], a_near[:, a_rows[1]])]
        back[1] = attend_back(1, after(b.dctx[1], us.sent, qs.sent, both, done), ug)
        got, a_got[1], norm, done = gate((got, a_got[1], norm, back[1].dqkv))
        both = both + norm
        norm = exchange(both, 16)
        u_got = us.along_z(got)
        a_second = exchange(back[1].out[0], 1)
        a_got[0] = qs.first(0, back[2].out[0][:, a_rows[0]], a_near[:, a_rows[0]])
        back[0] = attend_back(0, after(b.dctx[0], us.sent, qs.sent, both, done), ug)
        u_got, a_got[0], a_second, norm, done = gate((u_got, a_got[0], a_second, norm, back[0].dqkv))
        both = both + norm
        got = qs.side([[back[0].out[0][:, a_rows[h]], a_second[:, a_rows[h]], a_got[h]] for h in range(2)])
        last = input_part(after(b.g1, qs.sent, done), back)
        got, u_got, d_grad, both = gate((got, u_got, d_grad, both, last.dx))[:4]
        a_grad, u_grad = qs.finish(qs.along_z(got)), us.finish(u_got)
        q_grad, packed = a_grad[:, :qw], a_grad[:, qw:]
        l_grad = jnp.concatenate([packed[i * LROWS : i * LROWS + lay_rows] for i in range(3)], axis=1)
    else:

        def scatter(array):
            flat = array.reshape(-1, array.shape[2])
            return lax.psum_scatter(flat, everywhere, scatter_dimension=0, tiled=True).astype(F32)

        ug = up_part(f.mid)
        back = [attend_back(t, b.dctx[t], ug) for t in range(TB)]
        last = input_part(b.g1, back)
        d_grad = scatter(dg.out[0])
        u_grad = scatter(ug.out[0])
        a_out = jnp.concatenate([k.out[0] for k in back])
        packed = [a_out[:, i * LROWS : i * LROWS + lay_rows, qw:] for i in range(3)]
        q_grad = scatter(a_out[:, :, :qw])
        l_grad = scatter(jnp.concatenate(packed, axis=2))
        both = lax.psum(both, ("dp", "tensor"))
    lqw = 3 * low
    return (
        f.result,
        f.lresult,
        last.dx,
        last.dxl,
        jnp.stack([q_grad[:, i * ow : (i + 1) * ow] for i in range(3)], axis=1),
        u_grad[:, fw:].T,
        u_grad[:, :fw],
        d_grad.T,
        both[:, :width],
        jnp.stack([l_grad[:, i * low : (i + 1) * low] for i in range(3)], axis=1),
        l_grad[:, lqw : lqw + low].T,
        l_grad[:, lqw + low : lqw + low + lfw],
        l_grad[:, lqw + low + lfw :].T,
        both[:, width:],
    )


def solution(mesh):
    in_specs = (
        P(("dp", "tensor"), None),
        P(("dp", "tensor"), None),
        P(("dp", "tensor"), None),
        P(("dp", "tensor"), None),
        P("dp"),
        P("dp"),
        P("dp", None, "tensor"),
        P("tensor", "dp"),
        P("dp", "tensor"),
        P("tensor", "dp"),
        P(),
        P("dp", None, "tensor"),
        P("tensor", "dp"),
        P("dp", "tensor"),
        P("tensor", "dp"),
        P(),
    )
    out_specs = (
        P(("dp", "tensor"), None),
        P(("dp", "tensor"), None),
        P(("dp", "tensor"), None),
        P(("dp", "tensor"), None),
        P("dp", None, "tensor"),
        P("tensor", "dp"),
        P("dp", "tensor"),
        P("tensor", "dp"),
        P(),
        P("dp", None, "tensor"),
        P("tensor", "dp"),
        P("dp", "tensor"),
        P("tensor", "dp"),
        P(),
    )
    return jax.shard_map(body, mesh=mesh, in_specs=in_specs, out_specs=out_specs, check_vma=False)
```

```python
import functools
import math

import jax
import jax.numpy as jnp
import numpy as np
from jax import lax
from jax.experimental import pallas as pl
from jax.experimental.layout import Layout, with_layout_constraint
from jax.experimental.pallas import tpu as pltpu
from jax.sharding import PartitionSpec as P

TEXT_HEAD = 64
LAY_HEAD = 16
S = 512
NGROUPS = 8

TB = 4
DB = 8
LROWS = 32

SPLIT = ((2, 4), (4, 2))
SAME = ((2, 4), (2, 4))

epsilon = 1e-05
neg_large = -1e30
root_half = 1.0 / math.sqrt(2.0)
root_twopi = 1.0 / math.sqrt(2.0 * math.pi)
text_scale = float(TEXT_HEAD) ** (-0.5)
layout_scale = float(LAY_HEAD) ** (-0.5)

HINT = 0.1
BF = jnp.bfloat16
F32 = jnp.float32
ANY = pl.BlockSpec(memory_space=pl.ANY)
VM = pl.BlockSpec(memory_space=pltpu.VMEM)
SM = pl.BlockSpec(memory_space=pltpu.SMEM)
PARAMS = pltpu.CompilerParams(vmem_limit_bytes=60 * 1024 * 1024)


def nn(a, b):
    return jnp.dot(a, b, preferred_element_type=F32)


def nt(a, b):
    return lax.dot_general(a, b, (((1,), (1,)), ((), ())), preferred_element_type=F32)


def sds(shape, dtype):
    return jax.ShapeDtypeStruct(shape, dtype)


def cost(flops, read, trans=0):
    return pl.CostEstimate(flops=int(flops * HINT), bytes_accessed=int(read * HINT), transcendentals=int(trans * HINT))


def load_pieces(refs, maps, d0, size, lanes, dst, sem):
    for ref, entries in zip(refs, maps):
        for i, entry in enumerate(entries):
            if entry is None:
                continue
            rel, start, rows = entry
            spot = pl.multiple_of(((rel // TB) ^ d0) * size + start, rows)
            pltpu.make_async_copy(
                ref.at[i, :, lanes[0] : lanes[1]], dst.at[rel % TB, pl.ds(spot, rows), :], sem
            ).start()


def send_pieces(outs, maps, d0, buf, size, lanes, sem):
    for out, entries in zip(outs, maps):
        for i, entry in enumerate(entries):
            if entry is None:
                continue
            rel, start, rows = entry
            spot = pl.multiple_of(((rel // TB) ^ d0) * size + start, rows)
            pltpu.make_async_copy(
                buf.at[rel % TB, pl.ds(spot, rows), :], out.at[i, :, lanes[0] : lanes[1]], sem
            ).start()


def wait_pieces(dst, sem):
    pltpu.make_async_copy(dst, dst, sem).wait()


class Refs:
    def __init__(self, **entries):
        self.__dict__.update(entries)


def run(kernel, name, price, scalars, arrays, hbm, outs, hbm_outs, scratch):
    ins, in_tree = jax.tree.flatten((scalars, arrays, hbm))
    in_specs = [SM] * len(jax.tree.leaves(scalars)) + [VM] * len(jax.tree.leaves(arrays))
    in_specs += [ANY] * len(jax.tree.leaves(hbm))
    out_shapes, out_tree = jax.tree.flatten((outs, hbm_outs))
    out_specs = [VM] * len(jax.tree.leaves(outs)) + [ANY] * len(jax.tree.leaves(hbm_outs))
    scratch_shapes, scratch_names = list(scratch.values()), list(scratch)

    def inner(*refs):
        a, b = len(ins), len(ins) + len(out_shapes)
        s, v, h = jax.tree.unflatten(in_tree, refs[:a])
        o, ho = jax.tree.unflatten(out_tree, refs[a:b])
        kernel(Refs(**s, **v, **h, **o, **ho, **dict(zip(scratch_names, refs[b:]))))

    got = pl.pallas_call(
        inner,
        name=name,
        in_specs=in_specs,
        out_specs=out_specs,
        out_shape=out_shapes,
        scratch_shapes=scratch_shapes,
        compiler_params=PARAMS,
        cost_estimate=cost(*price),
    )(*ins)
    o, ho = jax.tree.unflatten(out_tree, got)
    return Refs(**o, **ho)


def attention_forward(maps, counted, k):
    d0 = k.me[0] // TB
    lay_width = k.select.shape[1]
    text_rows, lay_rows = k.wq.shape[1] // DB, lay_width // DB
    width = k.qkv.shape[1]
    load_pieces(k.w, maps, d0, text_rows, (0, k.wq.shape[2]), k.wq, k.sem)
    live = lax.broadcasted_iota(jnp.int32, (1, S), 1) < k.length[0]
    heads = width // 3 // TEXT_HEAD
    tw, lw = heads * TEXT_HEAD, heads * LAY_HEAD
    if hasattr(k, "xt"):
        k.xt[...] = k.x[...].T
        k.xlt[...] = k.xl[...].T
    wait_pieces(k.wq, k.sem)
    packed = k.wq[0, :, width:]
    if counted:
        place = lax.broadcasted_iota(jnp.int32, (8, k.wq.shape[1]), 1) % text_rows
        digits = jnp.where(place == lay_rows, 32.0, jnp.where(place == lay_rows + 1, 1.0, 0.0)).astype(BF)
        k.counts[...] = nn(digits, packed[:, 0:128])
    else:
        k.counts[...] = jnp.zeros(k.counts.shape, F32)
    wlt = jnp.concatenate([nn(k.select[j], packed).astype(BF) for j in range(3)], axis=1)
    k.wlay[...] = wlt
    qkv = nn(k.x[...], k.wq[0, :, 0:width]).astype(BF)
    k.qkv[...] = qkv
    lqkv = nn(k.xl[...], wlt[:, : 3 * lw]).astype(BF)
    k.lqkv[...] = lqkv
    for h in range(heads):
        a, b = h * TEXT_HEAD, h * LAY_HEAD
        ta, tb = slice(a, a + TEXT_HEAD), slice(b, b + LAY_HEAD)
        q = jnp.concatenate([qkv[:, ta] * BF(text_scale), lqkv[:, tb] * BF(layout_scale)], axis=1)
        key = jnp.concatenate([qkv[:, tw + a : tw + a + TEXT_HEAD], lqkv[:, lw + b : lw + b + LAY_HEAD]], axis=1)
        v = jnp.concatenate(
            [qkv[:, 2 * tw + a : 2 * tw + a + TEXT_HEAD], lqkv[:, 2 * lw + b : 2 * lw + b + LAY_HEAD]], axis=1
        )
        logits = jnp.where(live, nt(q, key), neg_large)
        top = jnp.max(logits, axis=-1, keepdims=True)
        raw = jnp.exp(logits - top)
        total = jnp.sum(raw, axis=-1, keepdims=True)
        probs = (raw * (1.0 / total)).astype(BF)
        ctx = nn(probs, v).astype(BF)
        k.ctx[:, ta] = ctx[:, :TEXT_HEAD]
        k.lctx[:, tb] = ctx[:, TEXT_HEAD:]
        k.lse[:, h : h + 1] = top + jnp.log(total)


def ffn_forward(maps, spots, base, k):
    d0 = k.me[0] // TB
    rows, fw, ow = k.wu.shape[1] // DB, k.wu.shape[2], k.wo.shape[2]
    low = k.lctx[0].shape[1]
    lf = (k.wlay[0].shape[1] - 4 * low) // 2
    load_pieces(k.u, maps[0], d0, rows, (fw, fw + ow), k.wo, k.sems.at[0])
    load_pieces(k.u, maps[0], d0, rows, (0, fw), k.wu, k.sems.at[1])
    load_pieces(k.d, maps[1], d0, rows, (0, fw), k.wd, k.sems.at[2])
    counts = k.known[...]
    for t in range(TB):
        counts = counts + k.counts[t][0:1]
    same = lax.broadcasted_iota(jnp.int32, counts.shape, 1) == k.group[0]
    mine = jnp.sum(jnp.where(same, counts, 0.0), axis=1, keepdims=True)
    keep = (lax.broadcasted_iota(jnp.int32, (S, 1), 0) < k.length[0]).astype(F32)
    scale = keep * (base / (mine + base))
    tn, ln = k.tn[...], k.ln[...]
    lattn = nt(k.lctx[0][...], k.wlay[0][:, 3 * low : 4 * low])
    for t in range(1, TB):
        lattn = lattn + nt(k.lctx[t][...], k.wlay[t][:, 3 * low : 4 * low])
    wait_pieces(k.wo, k.sems.at[0])
    attn = nt(k.ctx[0][...], k.wo[0])
    for t in range(1, TB):
        attn = attn + nt(k.ctx[t][...], k.wo[t])
    n1, i1 = norm_stats(k.x[...].astype(F32) + attn)
    mid = n1 * tn[0:1] + tn[1:2]
    ln1, li1 = norm_stats(k.xl[...].astype(F32) + lattn)
    lmid = ln1 * ln[0:1] + ln[1:2]
    k.n1[...] = n1
    k.ln1[...] = ln1
    k.i1[:, 0:1] = i1
    k.i1[:, 1:2] = li1
    k.mid[...] = mid.astype(BF)
    k.lmid[...] = lmid.astype(BF)
    k.branch[...] = mid
    k.lbranch[...] = lmid
    wait_pieces(k.wu, k.sems.at[1])
    wait_pieces(k.wd, k.sems.at[2])

    def gelu(before):
        cdf = 0.5 * (1.0 + lax.erf(before * root_half))
        return (before * cdf).astype(BF), cdf + before * jnp.exp(-0.5 * before * before) * root_twopi

    def step(t, carry):
        hid, slope = gelu(nn(k.mid[...], k.wu[t]))
        k.hid[t] = hid
        k.slope[t] = slope
        k.branch[...] += nt(hid, k.wd[t])
        return carry

    lax.fori_loop(0, TB, step, 0)
    for t in range(TB):
        lhid, lslope = gelu(nn(k.lmid[...], k.wlay[t][:, 4 * low : 4 * low + lf]))
        k.lhid[t] = lhid
        k.lslope[t] = lslope
        k.lbranch[...] += nt(lhid, k.wlay[t][:, 4 * low + lf :])
    n2, i2 = norm_stats(k.branch[...])
    k.result[...] = (n2 * tn[2:3] + tn[3:4]) * keep
    ge, gain, shift = norm_back(k.cot[...] * scale, n2, i2, tn[2:3])
    k.ge[...] = ge
    k.gb[...] = ge.astype(BF)
    k.tg[0:1] = gain
    k.tg[1:2] = shift
    ln2, li2 = norm_stats(k.lbranch[...])
    k.lresult[...] = ((ln2 * ln[2:3] + ln[3:4]) * keep).T
    lge, lgain, lshift = norm_back(k.lcot[...].T * scale, ln2, li2, ln[2:3])
    k.lge[...] = lge
    k.lgb[...] = lge.astype(BF)
    k.lg[0:1] = lgain
    k.lg[1:2] = lshift


def down_grads(maps, k):
    rows, width = k.buf.shape[1] // DB, k.buf.shape[2]
    k.gbt[...] = k.gb[...].T
    k.lgbt[...] = k.lgb[...].T

    def step(t, carry):
        k.buf[t] = nn(k.gbt[...], k.hid[t]).astype(BF)
        return carry

    lax.fori_loop(0, TB, step, 0)
    send_pieces(k.out, maps, k.me[0] // TB, k.buf, rows, (0, width), k.sem)
    for t in range(TB):
        k.ldown[t][...] = nn(k.lgbt[...], k.lhid[t]).astype(BF)
    wait_pieces(k.buf, k.sem)


def ffn_backward(maps, k):
    d0 = k.me[0] // TB
    rows, fw, ow = k.wu.shape[1] // DB, k.wu.shape[2], k.wo.shape[2]
    low = k.ldctx[0].shape[1]
    lf = (k.wlay[0].shape[1] - 4 * low) // 2
    load_pieces(k.d, maps[1], d0, rows, (0, fw), k.wd, k.sems.at[0])
    load_pieces(k.u, maps[0], d0, rows, (0, fw), k.wu, k.sems.at[1])
    load_pieces(k.u, maps[0], d0, rows, (fw, fw + ow), k.wo, k.sems.at[2])
    tn, ln = k.tn[...], k.ln[...]
    k.acc[...] = k.ge[...]
    k.lacc[...] = k.lge[...]
    for t in range(TB):
        ldbef = (nn(k.lgb[...], k.wlay[t][:, 4 * low + lf :]) * k.lslope[t]).astype(BF)
        k.ldbef[t] = ldbef
        k.lacc[...] += nt(ldbef, k.wlay[t][:, 4 * low : 4 * low + lf])
    wait_pieces(k.wd, k.sems.at[0])
    wait_pieces(k.wu, k.sems.at[1])

    def step(t, carry):
        dbef = (nn(k.gb[...], k.wd[t]) * k.slope[t]).astype(BF)
        k.dbef[t] = dbef
        k.acc[...] += nt(dbef, k.wu[t])
        return carry

    lax.fori_loop(0, TB, step, 0)
    g1, gain, shift = norm_back(k.acc[...], k.n1[...], k.i1[:, 0:1], tn[0:1])
    k.g1[...] = g1
    k.tg[0:1] = gain
    k.tg[1:2] = shift
    lg1, lgain, lshift = norm_back(k.lacc[...], k.ln1[...], k.i1[:, 1:2], ln[0:1])
    k.lg1[...] = lg1
    k.lg[0:1] = lgain
    k.lg[1:2] = lshift
    ga = g1.astype(BF)
    lga = lg1.astype(BF)
    wait_pieces(k.wo, k.sems.at[2])
    for t in range(TB):
        k.dctx[t][...] = nn(ga, k.wo[t]).astype(BF)
        k.ldctx[t][...] = nn(lga, k.wlay[t][:, 3 * low : 4 * low]).astype(BF)


def up_grads(maps, k):
    rows, fw, ow = k.buf.shape[1] // DB, k.buf.shape[2], k.obuf.shape[2]
    low = k.lctx[0].shape[1]
    d0 = k.me[0] // TB
    k.rt[...] = k.g1[...].astype(BF).T
    k.lrt[...] = k.lg1[...].astype(BF).T
    for t in range(TB):
        k.obuf[t] = nn(k.rt[...], k.ctx[t][...]).astype(BF)
        k.lup[t][:, 0:low] = nn(k.lrt[...], k.lctx[t][...]).astype(BF)
    send_pieces(k.out, maps, d0, k.obuf, rows, (fw, fw + ow), k.sems.at[1])
    k.rt[...] = k.mid[...].T
    k.lrt[...] = k.lmid[...].T

    def step(t, carry):
        k.buf[t] = nn(k.rt[...], k.dbef[t]).astype(BF)
        return carry

    lax.fori_loop(0, TB, step, 0)
    send_pieces(k.out, maps, d0, k.buf, rows, (0, fw), k.sems.at[0])
    for t in range(TB):
        k.lup[t][:, low:] = nn(k.lrt[...], k.ldbef[t]).astype(BF)
    wait_pieces(k.obuf, k.sems.at[1])
    wait_pieces(k.buf, k.sems.at[0])


def attention_backward(maps, k):
    width = k.qkv.shape[1]
    heads = width // 3 // TEXT_HEAD
    tw, lw = heads * TEXT_HEAD, heads * LAY_HEAD
    text_rows = k.buf.shape[1] // DB
    live = lax.broadcasted_iota(jnp.int32, (1, S), 1) < k.length[0]
    for h in range(heads):
        a, b = h * TEXT_HEAD, h * LAY_HEAD
        ta, tb = slice(a, a + TEXT_HEAD), slice(b, b + LAY_HEAD)
        ka, kb = slice(tw + a, tw + a + TEXT_HEAD), slice(lw + b, lw + b + LAY_HEAD)
        va, vb = slice(2 * tw + a, 2 * tw + a + TEXT_HEAD), slice(2 * lw + b, 2 * lw + b + LAY_HEAD)
        qt, ql = k.qkv[:, ta] * BF(text_scale), k.lqkv[:, tb] * BF(layout_scale)
        kt, kl = k.qkv[:, ka], k.lqkv[:, kb]
        vt, vl = k.qkv[:, va], k.lqkv[:, vb]
        gt, gl = k.dctx[:, ta], k.ldctx[:, tb]
        q = jnp.concatenate([qt, ql], axis=1)
        key = jnp.concatenate([kt, kl], axis=1)
        v = jnp.concatenate([vt, vl], axis=1)
        g = jnp.concatenate([gt, gl], axis=1)
        dot_t = jnp.sum(gt.astype(F32) * k.ctx[:, ta].astype(F32), axis=-1, keepdims=True)
        dot_s = dot_t + jnp.sum(gl.astype(F32) * k.lctx[:, tb].astype(F32), axis=-1, keepdims=True)
        logits = jnp.where(live, nt(q, key), neg_large)
        probs = jnp.exp(logits - k.lse[:, h : h + 1])
        low = (probs * (nt(gt, vt) - dot_t)).astype(BF)
        llow = (probs * (nt(g, v) - dot_s)).astype(BF)
        k.dqkv[:, ta] = (nn(low, kt) * text_scale).astype(BF)
        k.ldqkv[:, tb] = (nn(llow, kl) * layout_scale).astype(BF)
        dk = nn(qt.T, low).T
        dkl = nn(ql.T, llow).T
        dv = nn(g.T, probs.astype(BF)).T
        k.dqkv[:, ka] = dk.astype(BF)
        k.ldqkv[:, kb] = dkl.astype(BF)
        k.dqkv[:, va] = dv[:, :TEXT_HEAD].astype(BF)
        k.ldqkv[:, vb] = dv[:, TEXT_HEAD:].astype(BF)
    k.buf[0, :, 0:width] = nn(k.xt[...], k.dqkv[...]).astype(BF)
    lgrad = jnp.concatenate([nn(k.xlt[...], k.ldqkv[...]).astype(BF), k.lup[...], k.ldown[...]], axis=1)
    third = width // 3
    packed = nn(k.selt[0], lgrad[:, 0:third])
    for j in range(1, 3):
        packed = packed + nn(k.selt[j], lgrad[:, j * third : (j + 1) * third])
    k.buf[0, :, width:] = packed.astype(BF)
    d0 = k.me[0] // TB
    send_pieces(k.out, maps, d0, k.buf, text_rows, (0, k.buf.shape[2]), k.sem)
    wait_pieces(k.buf, k.sem)


def input_grads(maps, k):
    d0 = k.me[0] // TB
    text_rows, width = k.wq.shape[1] // DB, k.dqkv[0].shape[1]
    lw = k.ldqkv[0].shape[1]
    load_pieces(k.w, maps, d0, text_rows, (0, k.wq.shape[2]), k.wq, k.sem)
    dxl = k.lg1[...]
    for t in range(TB):
        dxl = dxl + nt(k.ldqkv[t][...], k.wlay[t][:, :lw])
    k.dxl[...] = dxl.T
    wait_pieces(k.wq, k.sem)
    dx = k.g1[...]
    for t in range(TB):
        dx = dx + nt(k.dqkv[t][...], k.wq[t, :, 0:width])
    k.dx[...] = dx


def norm_stats(values):
    centred = values - jnp.mean(values, axis=-1, keepdims=True)
    inverse = lax.rsqrt(jnp.mean(centred * centred, axis=-1, keepdims=True) + epsilon)
    return centred * inverse, inverse


def norm_back(upstream, normed, inverse, gain):
    scaled = upstream * gain
    inner = (
        scaled
        - jnp.mean(scaled, axis=-1, keepdims=True)
        - normed * jnp.mean(scaled * normed, axis=-1, keepdims=True)
    )
    return (
        inverse * inner,
        jnp.sum(upstream * normed, axis=0, keepdims=True),
        jnp.sum(upstream, axis=0, keepdims=True),
    )


def exchange(array, bit):
    size = lax.axis_size("dp") * lax.axis_size("tensor")
    return lax.ppermute(array, ("dp", "tensor"), [(i, i ^ bit) for i in range(size)])


Z = (0, 8, 16, 24)


def gather_maps(rows):
    half = rows // 2
    tops = ((0, 0, 2), (4, 0, 2), (0, half, 4), (2, half, 4))
    return tuple(
        tuple((z | inner | top | core, start, half) for inner in (0, step) for z in Z)
        for core in (0, 1)
        for top, start, step in tops
    )


def scatter_maps(start, rows, bits):
    return tuple(
        tuple((z | inner | top, start, rows) for inner in (0, bits[1]) for z in Z)
        for top in (0, 1, bits[0], bits[0] | 1)
    )


def block(maps, t):
    return tuple(
        tuple((rel - t, start, rows) if rel % TB == t else None for rel, start, rows in entries) for entries in maps
    )


def after(array, *needed):
    return lax.optimization_barrier((array, needed))[0]


def rows_major(array):
    return with_layout_constraint(array, Layout(major_to_minor=(0, 1, 2)))


class Gather:
    def __init__(self, own):
        self.own, self.half = rows_major(own[None]), own.shape[0] // 2

    def along_z(self):
        got = [self.own] + [rows_major(exchange(self.own, z)) for z in Z[1:]]
        self.upper = rows_major(jnp.concatenate([g[:, : self.half] for g in got], axis=0))
        self.lower = rows_major(jnp.concatenate([g[:, self.half :] for g in got], axis=0))
        return self.lower

    def over_16(self):
        self.own = rows_major(jnp.concatenate([self.own, exchange(self.own, 16)], axis=0))

    def over_8(self):
        got = [self.own, exchange(self.own, 8)]
        got = [g[i : i + 1] for i in range(2) for g in got]
        self.upper = rows_major(jnp.concatenate([g[:, : self.half] for g in got], axis=0))
        self.lower = rows_major(jnp.concatenate([g[:, self.half :] for g in got], axis=0))

    def sides(self):
        self.upper = rows_major(jnp.concatenate([self.upper, exchange(self.upper, 2)], axis=0))
        self.lower = rows_major(jnp.concatenate([self.lower, exchange(self.lower, 4)], axis=0))
        return self.lower

    def cross(self):
        self.here = [self.upper, rows_major(exchange(self.upper, 4)), self.lower, rows_major(exchange(self.lower, 2))]
        return self.here


def rounded(parts):
    return rows_major(sum(p.astype(F32) for p in parts).astype(BF))


class Scatter:
    def __init__(self, bits):
        self.bits = bits

    def first(self, h, far, near):
        self.sent = rounded([far, near])
        return exchange(self.sent, self.bits[h][0])

    def side(self, parts):
        self.parts = parts
        self.sent = [rounded([p[4:8] for p in half]) for half in parts]
        return [exchange(sent, self.bits[h][1]) for h, sent in enumerate(self.sent)]

    def along_z(self, got):
        self.parts = [half + [g] for half, g in zip(self.parts, got)]
        self.sent = [
            rows_major(jnp.concatenate([rounded([p[i : i + 1] for p in half]) for half in self.parts], axis=1))
            for i in range(1, 4)
        ]
        return [exchange(piece, z) for piece, z in zip(self.sent, Z[1:])]

    def over_8(self, got):
        self.parts = [half + [g] for half, g in zip(self.parts, got)]
        self.sent = rows_major(
            jnp.concatenate(
                [
                    jnp.concatenate([rounded([p[i : i + 1] for p in half]) for half in self.parts], axis=1)
                    for i in (1, 3)
                ]
            )
        )
        return exchange(self.sent, 8)

    def over_16(self, got):
        rows = got.shape[1] // 2
        parts = [[p[2:3] for p in half] + [got[1:2, h * rows : (h + 1) * rows]] for h, half in enumerate(self.parts)]
        self.sent = rows_major(jnp.concatenate([rounded(half) for half in parts], axis=1))
        return exchange(self.sent, 16)

    def settle(self, own, near, first, side, over_8, over_16):
        rows = own[0].shape[1]
        halves = [
            [own[h][0], near[16 * h + 8], first[h][0], side[h][0], over_8[0, h * rows : (h + 1) * rows]]
            for h in range(2)
        ]
        kept = jnp.concatenate([sum(p.astype(F32) for p in half) for half in halves], axis=0)
        return kept + over_16[0].astype(F32)

    def finish(self, got):
        kept = jnp.concatenate([sum(p[0].astype(F32) for p in half) for half in self.parts], axis=0)
        return kept + sum(g[0].astype(F32) for g in got)


def body(
    text_input,
    layout_input,
    text_cotangent,
    layout_cotangent,
    page_group,
    page_length,
    text_qkv,
    text_out,
    text_up,
    text_down,
    text_norm,
    layout_qkv,
    layout_out,
    layout_up,
    layout_down,
    layout_norm,
):
    dp_pages = page_length.shape[0]
    dp, tensor = lax.axis_size("dp"), lax.axis_size("tensor")
    width, lay_width = text_input.shape[1], layout_input.shape[1]
    text_rows, lay_rows = width // DB, lay_width // DB

    qkv_own = jnp.concatenate([text_qkv[:, i] for i in range(3)], axis=1)
    up_own = jnp.concatenate([text_up, text_out.T], axis=1)
    down_own = text_down.T
    lay_own = jnp.concatenate(
        [layout_qkv[:, i] for i in range(3)] + [layout_out.T, layout_up, layout_down.T], axis=1
    )
    qw, ow, fw = qkv_own.shape[1], text_out.shape[0], text_up.shape[1]
    low, lfw, lpack = layout_out.shape[0], layout_up.shape[1], lay_own.shape[1]
    mine = jnp.arange(dp_pages, dtype=jnp.int32) == lax.axis_index("tensor")
    length = jnp.sum(jnp.where(mine, page_length, 0)).reshape(1)
    group = jnp.sum(jnp.where(mine, page_group, 0)).reshape(1)
    base = float(dp_pages * dp * S) / (2.0 * NGROUPS)
    paired = dp == DB and tensor == TB
    everywhere = ("tensor", "dp")
    if paired:
        column = lax.broadcasted_iota(jnp.int32, (LROWS - lay_rows, lpack), 1) == group[0]
        part = lax.broadcasted_iota(jnp.int32, column.shape, 0)
        digit = jnp.where(part == 0, length[0] // 32, jnp.where(part == 1, length[0] % 32, 0))
        spare = jnp.where(column, digit, 0).astype(BF)
        packed = jnp.concatenate([lay_own, spare], axis=0)
        packed = jnp.concatenate([packed[:, i * ow : (i + 1) * ow] for i in range(3)], axis=0)
        ga = Gather(jnp.concatenate([qkv_own, packed], axis=1))
        ga.along_z()
        ga.upper, ga.lower, down_own = lax.optimization_barrier((ga.upper, ga.lower, down_own))
        gd = Gather(down_own)
        ga.sides()
        gd.over_16()
        ga.upper, ga.lower, gd.own, up_own = lax.optimization_barrier((ga.upper, ga.lower, gd.own, up_own))
        gu = Gather(up_own)
        ga.cross()
        gd.over_8()
        gu.over_16()
        weights_map = gather_maps(text_rows)
        a_map = [block(weights_map[4 * (t % 2) : 4 * (t % 2) + 4], t) for t in range(TB)]
        u_map = d_map = weights_map
        half = text_rows // 2
        up, lo = scatter_maps(0, half, SPLIT[0]), scatter_maps(half, half, SPLIT[1])
        u_send = d_send = (up[3] + up[1] + lo[3] + lo[1], up[0], up[2], lo[0], lo[2])
        a_send = [(block(scatter_maps(0, text_rows, SAME[0]), t)[t],) for t in range(TB)]
        me = (lax.axis_index("dp") * TB + lax.axis_index("tensor")).astype(jnp.int32).reshape(1)
        known = jnp.zeros((1, 128), F32)
    else:

        def gather(array, rows):
            whole = lax.all_gather(array, everywhere, axis=0, tiled=True)
            return whole.reshape(TB * DB, rows, array.shape[1])

        spare = ((0, 0), (0, LROWS - lay_rows), (0, 0))
        packed = jnp.pad(gather(lay_own, lay_rows), spare)
        packed = jnp.concatenate([packed[:, :, i * ow : (i + 1) * ow] for i in range(3)], axis=1)
        first = jnp.concatenate([gather(qkv_own, text_rows), packed], axis=2)
        a_in = [[first[t * DB : (t + 1) * DB]] for t in range(TB)]
        u_in, d_in = [gather(up_own, text_rows)], [gather(down_own, text_rows)]
        u_map = d_map = u_send = d_send = (tuple((d * TB + t, 0, text_rows) for t in range(TB) for d in range(DB)),)
        a_map = a_send = [(tuple((d * TB, 0, text_rows) for d in range(DB)),)] * TB
        me = jnp.zeros((1,), jnp.int32)
        labels = jnp.arange(NGROUPS, dtype=jnp.int32)
        member = (page_group[:, None] == labels[None, :]).astype(F32)
        counts = lax.psum(jnp.sum(member * page_length.astype(F32)[:, None], axis=0), "dp")
        known = jnp.pad(counts, (0, 128 - NGROUPS)).reshape(1, 128)

    chosen = np.zeros((3, lay_width, width), np.float32)
    for j in range(3):
        for a in range(lay_width):
            chosen[j, a, (a // lay_rows) * text_rows + j * LROWS + a % lay_rows] = 1.0
    select, select_t = jnp.asarray(chosen, BF), jnp.asarray(chosen.transpose(0, 2, 1), BF)
    V, dma = pltpu.VMEM, pltpu.SemaphoreType.DMA
    flop = 2.0 * S * width
    rows_f, rows_b = sds((S, width), F32), sds((S, width), BF)
    lay_f, lay_b = sds((S, lay_width), F32), sds((S, lay_width), BF)
    text_w, out_w, qkv_w = V((TB, width, fw), BF), V((TB, width, ow), BF), V((TB, width, qw + ow), BF)

    def attend(t, w):
        outs = dict(
            qkv=sds((S, qw), BF), lqkv=sds((S, 3 * low), BF), ctx=sds((S, ow), BF), lctx=sds((S, low), BF),
            lse=sds((S, 128), F32), wlay=sds((lay_width, lpack), BF), counts=sds((8, 128), F32),
        )
        if t == 0:
            outs.update(xt=sds((width, S), BF), xlt=sds((lay_width, S), BF))
        return run(
            functools.partial(attention_forward, a_map[t], paired), "attention_forward",
            (flop * (qw + 3 * S), 5e6, 1e6),
            dict(me=me, length=length), dict(x=text_input, xl=layout_input, select=select), dict(w=w),
            outs, {},
            dict(wq=V((1, width, qw + ow), BF), sem=dma),
        )

    if paired:
        ga.here, gd.upper, gd.lower, gu.own = lax.optimization_barrier((ga.here, gd.upper, gd.lower, gu.own))
        heads = [None] * TB
        gu.over_8()
        near = [rows_major(exchange(array, 1)) for array in ga.here[::2]]
        gd.sides()
        heads[0] = attend(0, ga.here)
        gd.upper, gd.lower, near, here, gu.upper, gu.lower, _ = lax.optimization_barrier(
            (gd.upper, gd.lower, near, ga.here, gu.upper, gu.lower, heads[0].ctx)
        )
        gd.cross()
        far = [rows_major(exchange(array, 1)) for array in here[1::2]]
        a_far = [near[0], far[0], near[1], far[1]]
        heads[2] = attend(2, here)
        gd.here, gu.upper, gu.lower, a_far, _ = lax.optimization_barrier(
            (gd.here, gu.upper, gu.lower, a_far, heads[2].ctx)
        )
        d_far = [rows_major(exchange(array, 1)) for array in gd.here[:3]]
        gu.sides()
        heads[1] = attend(1, a_far)
        gu.upper, gu.lower, first, d_far, last, _ = lax.optimization_barrier(
            (gu.upper, gu.lower, a_far[0], d_far, gd.here[3], heads[1].ctx)
        )
        gu.cross()
        near = [rows_major(exchange(array, 1)) for array in gu.here[::2]]
        d_far = d_far + [rows_major(exchange(last, 1))]
        heads[3] = attend(3, [first] + a_far[1:])
        gu.here, near, d_far, _ = lax.optimization_barrier((gu.here, near, d_far, heads[3].ctx))
        far = [rows_major(exchange(array, 1)) for array in gu.here[1::2]]
        u_in, d_in = gu.here + [near[0], far[0], near[1], far[1]], gd.here + d_far
        input_w, input_maps = ga.here + a_far, weights_map
    else:
        heads = [attend(t, a_in[t]) for t in range(TB)]
        input_w = [a[0] for a in a_in]
        input_maps = tuple(tuple((rel + t, start, rows) for rel, start, rows in a_map[t][0]) for t in range(TB))
    ctx, lctx = [h.ctx for h in heads], [h.lctx for h in heads]
    wlay = [h.wlay for h in heads]
    f = run(
        functools.partial(ffn_forward, (u_map, d_map), (0, 0, fw), base), "ffn_forward",
        (flop * 4 * (2 * fw + ow), 40e6, 4e6),
        dict(me=me, length=length, group=group),
        dict(x=text_input, xl=layout_input, ctx=ctx, lctx=lctx, wlay=wlay, counts=[h.counts for h in heads],
             known=known, tn=text_norm, ln=layout_norm, cot=text_cotangent, lcot=layout_cotangent.T),
        dict(u=u_in, d=d_in),
        dict(result=rows_f, lresult=sds((lay_width, S), F32), hid=sds((TB, S, fw), BF), slope=sds((TB, S, fw), F32),
             lhid=sds((TB, S, lfw), BF), lslope=sds((TB, S, lfw), F32), mid=rows_b, lmid=lay_b, gb=rows_b, lgb=lay_b,
             ge=rows_f, lge=lay_f, n1=rows_f, ln1=lay_f, i1=sds((S, 128), F32), tg=sds((2, width), F32),
             lg=sds((2, lay_width), F32)),
        {},
        dict(wu=text_w, wd=text_w, wo=out_w, branch=V((S, width), F32), lbranch=V((S, lay_width), F32),
             sems=dma((3,))),
    )

    def outs_of(maps, wide):
        return [sds((len(m), m[0][2], wide), BF) for m in maps]

    dg = run(
        functools.partial(down_grads, d_send), "down_grads", (flop * 4 * fw, 10e6),
        dict(me=me), dict(gb=f.gb, lgb=f.lgb, hid=f.hid, lhid=f.lhid), {},
        dict(ldown=[sds((lay_width, lfw), BF)] * TB), dict(out=outs_of(d_send, fw)),
        dict(buf=text_w, gbt=V((width, S), BF), lgbt=V((lay_width, S), BF), sem=dma),
    )
    b = run(
        functools.partial(ffn_backward, (u_map, d_map)), "ffn_backward", (flop * 4 * (2 * fw + ow), 40e6),
        dict(me=me),
        dict(gb=after(f.gb, dg.ldown[0]), lgb=f.lgb, ge=f.ge, lge=f.lge, slope=f.slope, lslope=f.lslope, n1=f.n1,
             ln1=f.ln1, i1=f.i1, wlay=wlay, tn=text_norm, ln=layout_norm),
        dict(u=u_in, d=d_in),
        dict(g1=rows_f, lg1=lay_f, dctx=[sds((S, ow), BF)] * TB, ldctx=[sds((S, low), BF)] * TB,
             dbef=sds((TB, S, fw), BF), ldbef=sds((TB, S, lfw), BF), tg=sds((2, width), F32),
             lg=sds((2, lay_width), F32)),
        {},
        dict(wu=text_w, wd=text_w, wo=out_w, acc=V((S, width), F32), lacc=V((S, lay_width), F32), sems=dma((3,))),
    )

    def up_part(mid):
        return run(
            functools.partial(up_grads, u_send), "up_grads", (flop * 4 * (fw + ow), 15e6),
            dict(me=me), dict(g1=b.g1, lg1=b.lg1, ctx=ctx, lctx=lctx, mid=mid, lmid=f.lmid, dbef=b.dbef, ldbef=b.ldbef),
            {},
            dict(lup=[sds((lay_width, low + lfw), BF)] * TB), dict(out=outs_of(u_send, fw + ow)),
            dict(buf=text_w, obuf=out_w, rt=V((width, S), BF), lrt=V((lay_width, S), BF), sems=dma((2,))),
        )

    def attend_back(t, dctx, ug):
        h = heads[t]
        return run(
            functools.partial(attention_backward, a_send[t]), "attention_backward", (flop * (qw + 6 * S), 8e6, 1e6),
            dict(me=me, length=length),
            dict(xt=heads[0].xt, xlt=heads[0].xlt, selt=select_t, qkv=h.qkv, lqkv=h.lqkv, ctx=h.ctx, lctx=h.lctx,
                 lse=h.lse, dctx=dctx, ldctx=b.ldctx[t], lup=ug.lup[t], ldown=dg.ldown[t]),
            {},
            dict(dqkv=sds((S, qw), BF), ldqkv=sds((S, 3 * low), BF)),
            dict(out=[sds((DB, text_rows, qw + ow), BF)]),
            dict(buf=V((1, width, qw + ow), BF), sem=dma),
        )

    def input_part(g1, back):
        return run(
            functools.partial(input_grads, input_maps), "input_grads", (flop * 4 * qw, 10e6),
            dict(me=me),
            dict(g1=g1, lg1=b.lg1, dqkv=[k.dqkv for k in back], ldqkv=[k.ldqkv for k in back], wlay=wlay),
            dict(w=input_w), dict(dx=rows_f, dxl=sds((lay_width, S), F32)), {},
            dict(wq=qkv_w, sem=dma),
        )

    both = jnp.concatenate(
        [jnp.concatenate([b.tg, f.tg]), jnp.concatenate([b.lg, f.lg])], axis=1
    )
    if paired:
        ds, us, qs = Scatter(SPLIT), Scatter(SPLIT), Scatter(SAME)
        gate = lax.optimization_barrier
        near = exchange(dg.out[0], 1)
        near, done, both = gate((near, b.g1, both))
        norm = exchange(both, 1)
        d_near, d_first, sent = near, [], [done]
        for h in range(2):
            d_first.append(ds.first(h, dg.out[2 * h + 2], near[16 * h : 16 * h + 8]))
            sent.append(ds.sent)
        ug = up_part(after(f.mid, sent))
        d_first, norm, dctx, core, _ = gate((d_first, norm, b.dctx, ug.out[0], ug.lup))
        both = both + norm
        norm = exchange(both, 2)
        near = exchange(core, 1)
        d_side = ds.side([[dg.out[2 * h + 1], d_near[16 * h + 8 : 16 * h + 16], d_first[h]] for h in range(2)])
        back = [None] * TB
        back[3] = attend_back(3, after(dctx[3], ds.sent, both), ug)
        d_side, near, norm, dctx, core, _ = gate((d_side, near, norm, dctx, back[3].out[0], back[3].dqkv))
        both = both + norm
        norm = exchange(both, 4)
        a_near = exchange(core, 1)
        d_8 = ds.over_8(d_side)
        u_near, u_first, sent = near, [], [ds.sent, both]
        for h in range(2):
            u_first.append(us.first(h, ug.out[2 * h + 2], near[16 * h : 16 * h + 8]))
            sent.append(us.sent)
        back[2] = attend_back(2, after(dctx[2], sent), ug)
        u_first, d_8, a_near, norm, dctx, _ = gate((u_first, d_8, a_near, norm, dctx, back[2].dqkv))
        d_16 = ds.over_16(d_8)
        both = both + norm
        norm = exchange(both, 8)
        a_rows = (slice(0, half), slice(half, text_rows))
        u_side = us.side([[ug.out[2 * h + 1], u_near[16 * h + 8 : 16 * h + 16], u_first[h]] for h in range(2)])
        a_got = [None, qs.first(1, back[2].out[0][:, a_rows[1]], a_near[:, a_rows[1]])]
        back[1] = attend_back(1, after(dctx[1], us.sent, qs.sent, ds.sent, both), ug)
        u_side, d_16, a_got[1], norm, dctx, core, _ = gate(
            (u_side, d_16, a_got[1], norm, dctx, back[1].out[0], back[1].dqkv)
        )
        both = both + norm
        norm = exchange(both, 16)
        u_8 = us.over_8(u_side)
        a_second = exchange(core, 1)
        a_got[0] = qs.first(0, back[2].out[0][:, a_rows[0]], a_near[:, a_rows[0]])
        back[0] = attend_back(0, after(dctx[0], us.sent, qs.sent, both), ug)
        u_8, a_got[0], a_second, norm, g1, _ = gate((u_8, a_got[0], a_second, norm, b.g1, back[0].dqkv))
        both = both + norm
        u_16 = us.over_16(u_8)
        got = qs.side([[back[0].out[0][:, a_rows[h]], a_second[:, a_rows[h]], a_got[h]] for h in range(2)])
        last = input_part(after(g1, qs.sent, us.sent), back)
        settled = [
            (dg.out[1::2], d_near, d_first, d_side, d_8, d_16),
            (ug.out[1::2], u_near, u_first, u_side, u_8, u_16),
        ]
        got, settled, both, _ = gate((got, settled, both, last.dx))
        a_grad, d_grad, u_grad = qs.finish(qs.along_z(got)), ds.settle(*settled[0]), us.settle(*settled[1])
        q_grad, packed = a_grad[:, :qw], a_grad[:, qw:]
        l_grad = jnp.concatenate([packed[i * LROWS : i * LROWS + lay_rows] for i in range(3)], axis=1)
    else:

        def scatter(array):
            flat = array.reshape(-1, array.shape[2])
            return lax.psum_scatter(flat, everywhere, scatter_dimension=0, tiled=True).astype(F32)

        ug = up_part(f.mid)
        back = [attend_back(t, b.dctx[t], ug) for t in range(TB)]
        last = input_part(b.g1, back)
        d_grad = scatter(dg.out[0])
        u_grad = scatter(ug.out[0])
        a_out = jnp.concatenate([k.out[0] for k in back])
        packed = [a_out[:, i * LROWS : i * LROWS + lay_rows, qw:] for i in range(3)]
        q_grad = scatter(a_out[:, :, :qw])
        l_grad = scatter(jnp.concatenate(packed, axis=2))
        both = lax.psum(both, ("dp", "tensor"))
    lqw = 3 * low
    return (
        f.result,
        f.lresult.T,
        last.dx,
        last.dxl.T,
        jnp.stack([q_grad[:, i * ow : (i + 1) * ow] for i in range(3)], axis=1),
        u_grad[:, fw:].T,
        u_grad[:, :fw],
        d_grad.T,
        both[:, :width],
        jnp.stack([l_grad[:, i * low : (i + 1) * low] for i in range(3)], axis=1),
        l_grad[:, lqw : lqw + low].T,
        l_grad[:, lqw + low : lqw + low + lfw],
        l_grad[:, lqw + low + lfw :].T,
        both[:, width:],
    )


def solution(mesh):
    in_specs = (
        P(("dp", "tensor"), None),
        P(("dp", "tensor"), None),
        P(("dp", "tensor"), None),
        P(("dp", "tensor"), None),
        P("dp"),
        P("dp"),
        P("dp", None, "tensor"),
        P("tensor", "dp"),
        P("dp", "tensor"),
        P("tensor", "dp"),
        P(),
        P("dp", None, "tensor"),
        P("tensor", "dp"),
        P("dp", "tensor"),
        P("tensor", "dp"),
        P(),
    )
    out_specs = (
        P(("dp", "tensor"), None),
        P(("dp", "tensor"), None),
        P(("dp", "tensor"), None),
        P(("dp", "tensor"), None),
        P("dp", None, "tensor"),
        P("tensor", "dp"),
        P("dp", "tensor"),
        P("tensor", "dp"),
        P(),
        P("dp", None, "tensor"),
        P("tensor", "dp"),
        P("dp", "tensor"),
        P("tensor", "dp"),
        P(),
    )
    return jax.shard_map(body, mesh=mesh, in_specs=in_specs, out_specs=out_specs, check_vma=False)
```

```python
import functools
import math

import jax
import jax.numpy as jnp
import numpy as np
from jax import lax
from jax.experimental import pallas as pl
from jax.experimental.layout import Layout, with_layout_constraint
from jax.experimental.pallas import tpu as pltpu
from jax.sharding import PartitionSpec as P

TEXT_HEAD = 64
LAY_HEAD = 16
S = 512
NGROUPS = 8

TB = 4
DB = 8
LROWS = 32

SPLIT = ((2, 4), (4, 2))
SAME = ((2, 4), (2, 4))

epsilon = 1e-05
neg_large = -1e30
root_half = 1.0 / math.sqrt(2.0)
root_twopi = 1.0 / math.sqrt(2.0 * math.pi)
text_scale = float(TEXT_HEAD) ** (-0.5)
layout_scale = float(LAY_HEAD) ** (-0.5)

HINT = 0.1
BF = jnp.bfloat16
F32 = jnp.float32
ANY = pl.BlockSpec(memory_space=pl.ANY)
VM = pl.BlockSpec(memory_space=pltpu.VMEM)
SM = pl.BlockSpec(memory_space=pltpu.SMEM)
PARAMS = pltpu.CompilerParams(vmem_limit_bytes=60 * 1024 * 1024)


def nn(a, b):
    return jnp.dot(a, b, preferred_element_type=F32)


def nt(a, b):
    return lax.dot_general(a, b, (((1,), (1,)), ((), ())), preferred_element_type=F32)


def sds(shape, dtype):
    return jax.ShapeDtypeStruct(shape, dtype)


def cost(flops, read, trans=0):
    return pl.CostEstimate(flops=int(flops * HINT), bytes_accessed=int(read * HINT), transcendentals=int(trans * HINT))


def load_pieces(refs, maps, d0, size, lanes, dst, sem):
    for ref, entries in zip(refs, maps):
        for i, entry in enumerate(entries):
            if entry is None:
                continue
            rel, start, rows = entry
            spot = pl.multiple_of(((rel // TB) ^ d0) * size + start, rows)
            pltpu.make_async_copy(
                ref.at[i, :, lanes[0] : lanes[1]], dst.at[rel % TB, pl.ds(spot, rows), :], sem
            ).start()


def send_pieces(outs, maps, d0, buf, size, lanes, sem):
    for out, entries in zip(outs, maps):
        for i, entry in enumerate(entries):
            if entry is None:
                continue
            rel, start, rows = entry
            spot = pl.multiple_of(((rel // TB) ^ d0) * size + start, rows)
            pltpu.make_async_copy(
                buf.at[rel % TB, pl.ds(spot, rows), :], out.at[i, :, lanes[0] : lanes[1]], sem
            ).start()


def wait_pieces(dst, sem):
    pltpu.make_async_copy(dst, dst, sem).wait()


class Refs:
    def __init__(self, **entries):
        self.__dict__.update(entries)


def run(kernel, name, price, scalars, arrays, hbm, outs, hbm_outs, scratch):
    ins, in_tree = jax.tree.flatten((scalars, arrays, hbm))
    in_specs = [SM] * len(jax.tree.leaves(scalars)) + [VM] * len(jax.tree.leaves(arrays))
    in_specs += [ANY] * len(jax.tree.leaves(hbm))
    out_shapes, out_tree = jax.tree.flatten((outs, hbm_outs))
    out_specs = [VM] * len(jax.tree.leaves(outs)) + [ANY] * len(jax.tree.leaves(hbm_outs))
    scratch_shapes, scratch_names = list(scratch.values()), list(scratch)

    def inner(*refs):
        a, b = len(ins), len(ins) + len(out_shapes)
        s, v, h = jax.tree.unflatten(in_tree, refs[:a])
        o, ho = jax.tree.unflatten(out_tree, refs[a:b])
        kernel(Refs(**s, **v, **h, **o, **ho, **dict(zip(scratch_names, refs[b:]))))

    got = pl.pallas_call(
        inner,
        name=name,
        in_specs=in_specs,
        out_specs=out_specs,
        out_shape=out_shapes,
        scratch_shapes=scratch_shapes,
        compiler_params=PARAMS,
        cost_estimate=cost(*price),
    )(*ins)
    o, ho = jax.tree.unflatten(out_tree, got)
    return Refs(**o, **ho)


def attention_forward(maps, counted, k):
    d0 = k.me[0] // TB
    lay_width = k.select.shape[1]
    text_rows, lay_rows = k.wq.shape[1] // DB, lay_width // DB
    width = k.qkv.shape[1]
    load_pieces(k.w, maps, d0, text_rows, (0, k.wq.shape[2]), k.wq, k.sem)
    live = lax.broadcasted_iota(jnp.int32, (1, S), 1) < k.length[0]
    heads = width // 3 // TEXT_HEAD
    tw, lw = heads * TEXT_HEAD, heads * LAY_HEAD
    if hasattr(k, "xt"):
        k.xt[...] = k.x[...].T
        k.xlt[...] = k.xl[...].T
    wait_pieces(k.wq, k.sem)
    packed = k.wq[0, :, width:]
    if counted:
        place = lax.broadcasted_iota(jnp.int32, (8, k.wq.shape[1]), 1) % text_rows
        digits = jnp.where(place == lay_rows, 32.0, jnp.where(place == lay_rows + 1, 1.0, 0.0)).astype(BF)
        k.counts[...] = nn(digits, packed[:, 0:128])
    else:
        k.counts[...] = jnp.zeros(k.counts.shape, F32)
    wlt = jnp.concatenate([nn(k.select[j], packed).astype(BF) for j in range(3)], axis=1)
    k.wlay[...] = wlt
    qkv = nn(k.x[...], k.wq[0, :, 0:width]).astype(BF)
    k.qkv[...] = qkv
    lqkv = nn(k.xl[...], wlt[:, : 3 * lw]).astype(BF)
    k.lqkv[...] = lqkv
    for h in range(heads):
        a, b = h * TEXT_HEAD, h * LAY_HEAD
        ta, tb = slice(a, a + TEXT_HEAD), slice(b, b + LAY_HEAD)
        q = jnp.concatenate([qkv[:, ta] * BF(text_scale), lqkv[:, tb] * BF(layout_scale)], axis=1)
        key = jnp.concatenate([qkv[:, tw + a : tw + a + TEXT_HEAD], lqkv[:, lw + b : lw + b + LAY_HEAD]], axis=1)
        v = jnp.concatenate(
            [qkv[:, 2 * tw + a : 2 * tw + a + TEXT_HEAD], lqkv[:, 2 * lw + b : 2 * lw + b + LAY_HEAD]], axis=1
        )
        logits = jnp.where(live, nt(q, key), neg_large)
        top = jnp.max(logits, axis=-1, keepdims=True)
        raw = jnp.exp(logits - top)
        total = jnp.sum(raw, axis=-1, keepdims=True)
        probs = (raw * (1.0 / total)).astype(BF)
        ctx = nn(probs, v).astype(BF)
        k.ctx[:, ta] = ctx[:, :TEXT_HEAD]
        k.lctx[:, tb] = ctx[:, TEXT_HEAD:]
        k.lse[:, h : h + 1] = top + jnp.log(total)


def ffn_up(maps, k):
    d0 = k.me[0] // TB
    rows, fw, ow = k.wu.shape[1] // DB, k.wu.shape[2], k.wo.shape[2]
    low = k.lctx[0].shape[1]
    lf = (k.wlay[0].shape[1] - 4 * low) // 2
    load_pieces(k.u, maps, d0, rows, (fw, fw + ow), k.wo, k.sems.at[0])
    load_pieces(k.u, maps, d0, rows, (0, fw), k.wu, k.sems.at[1])
    tn, ln = k.tn[...], k.ln[...]
    lattn = nt(k.lctx[0][...], k.wlay[0][:, 3 * low : 4 * low])
    for t in range(1, TB):
        lattn = lattn + nt(k.lctx[t][...], k.wlay[t][:, 3 * low : 4 * low])
    wait_pieces(k.wo, k.sems.at[0])
    attn = nt(k.ctx[0][...], k.wo[0])
    for t in range(1, TB):
        attn = attn + nt(k.ctx[t][...], k.wo[t])
    n1, i1 = norm_stats(k.x[...].astype(F32) + attn)
    ln1, li1 = norm_stats(k.xl[...].astype(F32) + lattn)
    k.n1[...] = n1
    k.ln1[...] = ln1
    k.i1[:, 0:1] = i1
    k.i1[:, 1:2] = li1
    k.mid[...] = (n1 * tn[0:1] + tn[1:2]).astype(BF)
    k.lmid[...] = (ln1 * ln[0:1] + ln[1:2]).astype(BF)
    wait_pieces(k.wu, k.sems.at[1])

    def gelu(before):
        cdf = 0.5 * (1.0 + lax.erf(before * root_half))
        slope = cdf + before * jnp.exp(-0.5 * before * before) * root_twopi
        return (before * cdf).astype(BF), slope.astype(BF)

    def step(t, carry):
        hid, slope = gelu(nn(k.mid[...], k.wu[t]))
        k.hid[t] = hid
        k.slope[t] = slope
        return carry

    lax.fori_loop(0, TB, step, 0)
    for t in range(TB):
        lhid, lslope = gelu(nn(k.lmid[...], k.wlay[t][:, 4 * low : 4 * low + lf]))
        k.lhid[t] = lhid
        k.lslope[t] = lslope


def ffn_down(maps, sent, base, k):
    d0 = k.me[0] // TB
    rows, fw = k.wd.shape[1] // DB, k.wd.shape[2]
    lf = k.lhid.shape[2]
    load_pieces(k.d, maps, d0, rows, (0, fw), k.wd, k.sem)
    counts = k.known[...]
    for t in range(TB):
        counts = counts + k.counts[t][0:1]
    same = lax.broadcasted_iota(jnp.int32, counts.shape, 1) == k.group[0]
    mine = jnp.sum(jnp.where(same, counts, 0.0), axis=1, keepdims=True)
    keep = (lax.broadcasted_iota(jnp.int32, (S, 1), 0) < k.length[0]).astype(F32)
    scale = keep * (base / (mine + base))
    tn, ln = k.tn[...], k.ln[...]
    lbranch = k.ln1[...] * ln[0:1] + ln[1:2]
    for t in range(TB):
        lbranch = lbranch + nt(k.lhid[t], k.wlay[t][:, k.wlay[t].shape[1] - lf :])
    ln2, li2 = norm_stats(lbranch)
    k.lresult[...] = ((ln2 * ln[2:3] + ln[3:4]) * keep).T
    lge, lgain, lshift = norm_back(k.lcot[...].T * scale, ln2, li2, ln[2:3])
    k.lge[...] = lge
    k.lgb[...] = lge.astype(BF)
    k.lg[0:1] = lgain
    k.lg[1:2] = lshift
    wait_pieces(k.wd, k.sem)
    branch = k.n1[...] * tn[0:1] + tn[1:2]
    for t in range(TB):
        branch = branch + nt(k.hid[t], k.wd[t])
    n2, i2 = norm_stats(branch)
    k.result[...] = (n2 * tn[2:3] + tn[3:4]) * keep
    ge, gain, shift = norm_back(k.cot[...] * scale, n2, i2, tn[2:3])
    k.ge[...] = ge
    k.gb[...] = ge.astype(BF)
    k.tg[0:1] = gain
    k.tg[1:2] = shift
    k.gbt[...] = k.gb[...].T
    k.lgbt[...] = k.lgb[...].T

    def step(t, carry):
        k.buf[t] = nn(k.gbt[...], k.hid[t]).astype(BF)
        return carry

    lax.fori_loop(0, TB, step, 0)
    send_pieces(k.out, sent, d0, k.buf, rows, (0, fw), k.sem)
    for t in range(TB):
        k.ldown[t][...] = nn(k.lgbt[...], k.lhid[t]).astype(BF)
    wait_pieces(k.buf, k.sem)


def ffn_backward(maps, k):
    d0 = k.me[0] // TB
    rows, fw, ow = k.wu.shape[1] // DB, k.wu.shape[2], k.wo.shape[2]
    low = k.ldctx[0].shape[1]
    lf = (k.wlay[0].shape[1] - 4 * low) // 2
    load_pieces(k.d, maps[1], d0, rows, (0, fw), k.wd, k.sems.at[0])
    load_pieces(k.u, maps[0], d0, rows, (0, fw), k.wu, k.sems.at[1])
    load_pieces(k.u, maps[0], d0, rows, (fw, fw + ow), k.wo, k.sems.at[2])
    tn, ln = k.tn[...], k.ln[...]
    k.acc[...] = k.ge[...]
    k.lacc[...] = k.lge[...]
    for t in range(TB):
        ldbef = (nn(k.lgb[...], k.wlay[t][:, 4 * low + lf :]) * k.lslope[t]).astype(BF)
        k.ldbef[t] = ldbef
        k.lacc[...] += nt(ldbef, k.wlay[t][:, 4 * low : 4 * low + lf])
    wait_pieces(k.wd, k.sems.at[0])
    wait_pieces(k.wu, k.sems.at[1])

    def step(t, carry):
        dbef = (nn(k.gb[...], k.wd[t]) * k.slope[t]).astype(BF)
        k.dbef[t] = dbef
        k.acc[...] += nt(dbef, k.wu[t])
        return carry

    lax.fori_loop(0, TB, step, 0)
    g1, gain, shift = norm_back(k.acc[...], k.n1[...], k.i1[:, 0:1], tn[0:1])
    k.g1[...] = g1
    k.tg[0:1] = gain
    k.tg[1:2] = shift
    lg1, lgain, lshift = norm_back(k.lacc[...], k.ln1[...], k.i1[:, 1:2], ln[0:1])
    k.lg1[...] = lg1
    k.lg[0:1] = lgain
    k.lg[1:2] = lshift
    ga = g1.astype(BF)
    lga = lg1.astype(BF)
    wait_pieces(k.wo, k.sems.at[2])
    for t in range(TB):
        k.dctx[t][...] = nn(ga, k.wo[t]).astype(BF)
        k.ldctx[t][...] = nn(lga, k.wlay[t][:, 3 * low : 4 * low]).astype(BF)


def up_grads(maps, k):
    rows, fw, ow = k.buf.shape[1] // DB, k.buf.shape[2], k.obuf.shape[2]
    low = k.lctx[0].shape[1]
    d0 = k.me[0] // TB
    k.rt[...] = k.g1[...].astype(BF).T
    k.lrt[...] = k.lg1[...].astype(BF).T
    for t in range(TB):
        k.obuf[t] = nn(k.rt[...], k.ctx[t][...]).astype(BF)
        k.lup[t][:, 0:low] = nn(k.lrt[...], k.lctx[t][...]).astype(BF)
    send_pieces(k.out, maps, d0, k.obuf, rows, (fw, fw + ow), k.sems.at[1])
    k.rt[...] = k.mid[...].T
    k.lrt[...] = k.lmid[...].T

    def step(t, carry):
        k.buf[t] = nn(k.rt[...], k.dbef[t]).astype(BF)
        return carry

    lax.fori_loop(0, TB, step, 0)
    send_pieces(k.out, maps, d0, k.buf, rows, (0, fw), k.sems.at[0])
    for t in range(TB):
        k.lup[t][:, low:] = nn(k.lrt[...], k.ldbef[t]).astype(BF)
    wait_pieces(k.obuf, k.sems.at[1])
    wait_pieces(k.buf, k.sems.at[0])


def attention_backward(maps, k):
    width = k.qkv.shape[1]
    heads = width // 3 // TEXT_HEAD
    tw, lw = heads * TEXT_HEAD, heads * LAY_HEAD
    text_rows = k.buf.shape[1] // DB
    live = lax.broadcasted_iota(jnp.int32, (1, S), 1) < k.length[0]
    for h in range(heads):
        a, b = h * TEXT_HEAD, h * LAY_HEAD
        ta, tb = slice(a, a + TEXT_HEAD), slice(b, b + LAY_HEAD)
        for j, (dst, one, two) in enumerate(((k.qs, text_scale, layout_scale), (k.ks, 1.0, 1.0), (k.vs, 1.0, 1.0))):
            c, d = j * tw + a, j * lw + b
            parts = [k.qkv[:, c : c + TEXT_HEAD] * BF(one), k.lqkv[:, d : d + LAY_HEAD] * BF(two)]
            dst[h] = jnp.concatenate(parts, axis=1)
        gt, gl = k.dctx[:, ta], k.ldctx[:, tb]
        k.gs[h] = jnp.concatenate([gt, gl], axis=1)
        dot_t = jnp.sum(gt.astype(F32) * k.ctx[:, ta].astype(F32), axis=-1, keepdims=True)
        dot_l = jnp.sum(gl.astype(F32) * k.lctx[:, tb].astype(F32), axis=-1, keepdims=True)
        k.stats[h, :, 0:1] = dot_t
        k.stats[h, :, 1:2] = dot_t + dot_l
        k.stats[h, :, 2:3] = k.lse[:, h : h + 1]

    def step(h, carry):
        q, key, v, g = k.qs[h], k.ks[h], k.vs[h], k.gs[h]
        gt, vt = g[:, :TEXT_HEAD], v[:, :TEXT_HEAD]
        logits = jnp.where(live, nt(q, key), neg_large)
        probs = jnp.exp(logits - k.stats[h, :, 2:3])
        low = (probs * (nt(gt, vt) - k.stats[h, :, 0:1])).astype(BF)
        llow = (probs * (nt(g, v) - k.stats[h, :, 1:2])).astype(BF)
        dq = nn(low, key[:, :TEXT_HEAD]) * text_scale
        dql = nn(llow, key[:, TEXT_HEAD:]) * layout_scale
        dk = nn(q[:, :TEXT_HEAD].T, low).T
        dkl = nn(q[:, TEXT_HEAD:].T, llow).T
        dv = nn(g.T, probs.astype(BF)).T
        k.qs[h] = jnp.concatenate([dq, dql], axis=1).astype(BF)
        k.ks[h] = jnp.concatenate([dk, dkl], axis=1).astype(BF)
        k.vs[h] = dv.astype(BF)
        return carry

    lax.fori_loop(0, heads, step, 0)
    for h in range(heads):
        for j, src in enumerate((k.qs, k.ks, k.vs)):
            a, b = j * tw + h * TEXT_HEAD, j * lw + h * LAY_HEAD
            k.dqkv[:, a : a + TEXT_HEAD] = src[h, :, :TEXT_HEAD]
            k.ldqkv[:, b : b + LAY_HEAD] = src[h, :, TEXT_HEAD:]
    k.buf[0, :, 0:width] = nn(k.xt[...], k.dqkv[...]).astype(BF)
    lgrad = jnp.concatenate([nn(k.xlt[...], k.ldqkv[...]).astype(BF), k.lup[...], k.ldown[...]], axis=1)
    third = width // 3
    packed = nn(k.selt[0], lgrad[:, 0:third])
    for j in range(1, 3):
        packed = packed + nn(k.selt[j], lgrad[:, j * third : (j + 1) * third])
    k.buf[0, :, width:] = packed.astype(BF)
    d0 = k.me[0] // TB
    send_pieces(k.out, maps, d0, k.buf, text_rows, (0, k.buf.shape[2]), k.sem)
    wait_pieces(k.buf, k.sem)


def input_grads(maps, k):
    d0 = k.me[0] // TB
    text_rows, width = k.wq.shape[1] // DB, k.dqkv[0].shape[1]
    lw = k.ldqkv[0].shape[1]
    load_pieces(k.w, maps, d0, text_rows, (0, k.wq.shape[2]), k.wq, k.sem)
    dxl = k.lg1[...]
    for t in range(TB):
        dxl = dxl + nt(k.ldqkv[t][...], k.wlay[t][:, :lw])
    k.dxl[...] = dxl.T
    wait_pieces(k.wq, k.sem)
    dx = k.g1[...]
    for t in range(TB):
        dx = dx + nt(k.dqkv[t][...], k.wq[t, :, 0:width])
    k.dx[...] = dx


def norm_stats(values):
    centred = values - jnp.mean(values, axis=-1, keepdims=True)
    inverse = lax.rsqrt(jnp.mean(centred * centred, axis=-1, keepdims=True) + epsilon)
    return centred * inverse, inverse


def norm_back(upstream, normed, inverse, gain):
    scaled = upstream * gain
    inner = (
        scaled
        - jnp.mean(scaled, axis=-1, keepdims=True)
        - normed * jnp.mean(scaled * normed, axis=-1, keepdims=True)
    )
    return (
        inverse * inner,
        jnp.sum(upstream * normed, axis=0, keepdims=True),
        jnp.sum(upstream, axis=0, keepdims=True),
    )


def exchange(array, bit):
    size = lax.axis_size("dp") * lax.axis_size("tensor")
    return lax.ppermute(array, ("dp", "tensor"), [(i, i ^ bit) for i in range(size)])


Z = (0, 8, 16, 24)


def gather_maps(rows):
    half = rows // 2
    tops = ((0, 0, 2), (4, 0, 2), (0, half, 4), (2, half, 4))
    return tuple(
        tuple((z | inner | top | core, start, half) for inner in (0, step) for z in Z)
        for core in (0, 1)
        for top, start, step in tops
    )


def scatter_maps(start, rows, bits):
    return tuple(
        tuple((z | inner | top, start, rows) for inner in (0, bits[1]) for z in Z)
        for top in (0, 1, bits[0], bits[0] | 1)
    )


def block(maps, t):
    return tuple(
        tuple((rel - t, start, rows) if rel % TB == t else None for rel, start, rows in entries) for entries in maps
    )


def after(array, *needed):
    return lax.optimization_barrier((array, needed))[0]


def rows_major(array):
    return with_layout_constraint(array, Layout(major_to_minor=(0, 1, 2)))


class Gather:
    def __init__(self, own):
        self.own, self.half = rows_major(own[None]), own.shape[0] // 2

    def along_z(self):
        got = [self.own] + [rows_major(exchange(self.own, z)) for z in Z[1:]]
        self.upper = rows_major(jnp.concatenate([g[:, : self.half] for g in got], axis=0))
        self.lower = rows_major(jnp.concatenate([g[:, self.half :] for g in got], axis=0))
        return self.lower

    def over_16(self):
        self.own = rows_major(jnp.concatenate([self.own, exchange(self.own, 16)], axis=0))

    def over_8(self):
        got = [self.own, exchange(self.own, 8)]
        got = [g[i : i + 1] for i in range(2) for g in got]
        self.upper = rows_major(jnp.concatenate([g[:, : self.half] for g in got], axis=0))
        self.lower = rows_major(jnp.concatenate([g[:, self.half :] for g in got], axis=0))

    def sides(self):
        self.upper = rows_major(jnp.concatenate([self.upper, exchange(self.upper, 2)], axis=0))
        self.lower = rows_major(jnp.concatenate([self.lower, exchange(self.lower, 4)], axis=0))
        return self.lower

    def cross(self):
        self.here = [self.upper, rows_major(exchange(self.upper, 4)), self.lower, rows_major(exchange(self.lower, 2))]
        return self.here


def swap(arrays):
    return [rows_major(exchange(array, 1)) for array in arrays]


def rounded(parts):
    return rows_major(sum(p.astype(F32) for p in parts).astype(BF))


class Scatter:
    def __init__(self, bits):
        self.bits = bits

    def first(self, h, far, near):
        self.sent = rounded([far, near])
        return exchange(self.sent, self.bits[h][0])

    def side(self, parts):
        self.parts = parts
        self.sent = [rounded([p[4:8] for p in half]) for half in parts]
        return [exchange(sent, self.bits[h][1]) for h, sent in enumerate(self.sent)]

    def along_z(self, got):
        self.parts = [half + [g] for half, g in zip(self.parts, got)]
        self.sent = [
            rows_major(jnp.concatenate([rounded([p[i : i + 1] for p in half]) for half in self.parts], axis=1))
            for i in range(1, 4)
        ]
        return [exchange(piece, z) for piece, z in zip(self.sent, Z[1:])]

    def over_8(self, got):
        self.parts = [half + [g] for half, g in zip(self.parts, got)]
        self.sent = rows_major(
            jnp.concatenate(
                [
                    jnp.concatenate([rounded([p[i : i + 1] for p in half]) for half in self.parts], axis=1)
                    for i in (1, 3)
                ]
            )
        )
        return exchange(self.sent, 8)

    def over_16(self, got):
        rows = got.shape[1] // 2
        parts = [[p[2:3] for p in half] + [got[1:2, h * rows : (h + 1) * rows]] for h, half in enumerate(self.parts)]
        self.sent = rows_major(jnp.concatenate([rounded(half) for half in parts], axis=1))
        return exchange(self.sent, 16)

    def settle(self, own, near, first, side, over_8, over_16):
        rows = own[0].shape[1]
        halves = [
            [own[h][0], near[16 * h + 8], first[h][0], side[h][0], over_8[0, h * rows : (h + 1) * rows]]
            for h in range(2)
        ]
        kept = jnp.concatenate([sum(p.astype(F32) for p in half) for half in halves], axis=0)
        return kept + over_16[0].astype(F32)

    def finish(self, got):
        kept = jnp.concatenate([sum(p[0].astype(F32) for p in half) for half in self.parts], axis=0)
        return kept + sum(g[0].astype(F32) for g in got)


def body(
    text_input,
    layout_input,
    text_cotangent,
    layout_cotangent,
    page_group,
    page_length,
    text_qkv,
    text_out,
    text_up,
    text_down,
    text_norm,
    layout_qkv,
    layout_out,
    layout_up,
    layout_down,
    layout_norm,
):
    dp_pages = page_length.shape[0]
    dp, tensor = lax.axis_size("dp"), lax.axis_size("tensor")
    width, lay_width = text_input.shape[1], layout_input.shape[1]
    text_rows, lay_rows = width // DB, lay_width // DB

    qkv_own = jnp.concatenate([text_qkv[:, i] for i in range(3)], axis=1)
    up_own = jnp.concatenate([text_up, text_out.T], axis=1)
    down_own = text_down.T
    lay_own = jnp.concatenate(
        [layout_qkv[:, i] for i in range(3)] + [layout_out.T, layout_up, layout_down.T], axis=1
    )
    qw, ow, fw = qkv_own.shape[1], text_out.shape[0], text_up.shape[1]
    low, lfw, lpack = layout_out.shape[0], layout_up.shape[1], lay_own.shape[1]
    mine = jnp.arange(dp_pages, dtype=jnp.int32) == lax.axis_index("tensor")
    length = jnp.sum(jnp.where(mine, page_length, 0)).reshape(1)
    group = jnp.sum(jnp.where(mine, page_group, 0)).reshape(1)
    base = float(dp_pages * dp * S) / (2.0 * NGROUPS)
    paired = dp == DB and tensor == TB
    everywhere = ("tensor", "dp")
    if paired:
        column = lax.broadcasted_iota(jnp.int32, (LROWS - lay_rows, lpack), 1) == group[0]
        part = lax.broadcasted_iota(jnp.int32, column.shape, 0)
        digit = jnp.where(part == 0, length[0] // 32, jnp.where(part == 1, length[0] % 32, 0))
        spare = jnp.where(column, digit, 0).astype(BF)
        packed = jnp.concatenate([lay_own, spare], axis=0)
        packed = jnp.concatenate([packed[:, i * ow : (i + 1) * ow] for i in range(3)], axis=0)
        ga = Gather(jnp.concatenate([qkv_own, packed], axis=1))
        barrier = lax.optimization_barrier
        ga.along_z()
        ga.sides()
        ga.upper, ga.lower, up_own = barrier((ga.upper, ga.lower, up_own))
        gu = Gather(up_own)
        ga.cross()
        gu.over_16()
        weights_map = gather_maps(text_rows)
        a_map = [block(weights_map[4 * (t % 2) : 4 * (t % 2) + 4], t) for t in range(TB)]
        u_map = d_map = weights_map
        half = text_rows // 2
        up, lo = scatter_maps(0, half, SPLIT[0]), scatter_maps(half, half, SPLIT[1])
        u_send = d_send = (up[3] + up[1] + lo[3] + lo[1], up[0], up[2], lo[0], lo[2])
        a_send = [(block(scatter_maps(0, text_rows, SAME[0]), t)[t],) for t in range(TB)]
        me = (lax.axis_index("dp") * TB + lax.axis_index("tensor")).astype(jnp.int32).reshape(1)
        known = jnp.zeros((1, 128), F32)
    else:

        def gather(array, rows):
            whole = lax.all_gather(array, everywhere, axis=0, tiled=True)
            return whole.reshape(TB * DB, rows, array.shape[1])

        spare = ((0, 0), (0, LROWS - lay_rows), (0, 0))
        packed = jnp.pad(gather(lay_own, lay_rows), spare)
        packed = jnp.concatenate([packed[:, :, i * ow : (i + 1) * ow] for i in range(3)], axis=1)
        first = jnp.concatenate([gather(qkv_own, text_rows), packed], axis=2)
        a_in = [[first[t * DB : (t + 1) * DB]] for t in range(TB)]
        u_in, d_in = [gather(up_own, text_rows)], [gather(down_own, text_rows)]
        u_map = d_map = u_send = d_send = (tuple((d * TB + t, 0, text_rows) for t in range(TB) for d in range(DB)),)
        a_map = a_send = [(tuple((d * TB, 0, text_rows) for d in range(DB)),)] * TB
        me = jnp.zeros((1,), jnp.int32)
        labels = jnp.arange(NGROUPS, dtype=jnp.int32)
        member = (page_group[:, None] == labels[None, :]).astype(F32)
        counts = lax.psum(jnp.sum(member * page_length.astype(F32)[:, None], axis=0), "dp")
        known = jnp.pad(counts, (0, 128 - NGROUPS)).reshape(1, 128)

    chosen = np.zeros((3, lay_width, width), np.float32)
    for j in range(3):
        for a in range(lay_width):
            chosen[j, a, (a // lay_rows) * text_rows + j * LROWS + a % lay_rows] = 1.0
    select, select_t = jnp.asarray(chosen, BF), jnp.asarray(chosen.transpose(0, 2, 1), BF)
    V, dma = pltpu.VMEM, pltpu.SemaphoreType.DMA
    flop = 2.0 * S * width
    rows_f, rows_b = sds((S, width), F32), sds((S, width), BF)
    lay_f, lay_b = sds((S, lay_width), F32), sds((S, lay_width), BF)
    heads_held = ow // TEXT_HEAD
    head, stats = V((heads_held, S, TEXT_HEAD + LAY_HEAD), BF), V((heads_held, S, 128), F32)
    text_w, out_w, qkv_w = V((TB, width, fw), BF), V((TB, width, ow), BF), V((TB, width, qw + ow), BF)

    def attend(t, w):
        outs = dict(
            qkv=sds((S, qw), BF), lqkv=sds((S, 3 * low), BF), ctx=sds((S, ow), BF), lctx=sds((S, low), BF),
            lse=sds((S, 128), F32), wlay=sds((lay_width, lpack), BF), counts=sds((8, 128), F32),
        )
        if t == 0:
            outs.update(xt=sds((width, S), BF), xlt=sds((lay_width, S), BF))
        return run(
            functools.partial(attention_forward, a_map[t], paired), "attention_forward",
            (flop * (qw + 3 * S), 5e6, 1e6),
            dict(me=me, length=length), dict(x=text_input, xl=layout_input, select=select), dict(w=w),
            outs, {},
            dict(wq=V((1, width, qw + ow), BF), sem=dma),
        )

    if paired:
        ga.here, gu.own = barrier((ga.here, gu.own))
        heads = [None] * TB
        gu.over_8()
        near = swap(ga.here[::2])
        heads[0] = attend(0, ga.here)
        gu.upper, gu.lower, near, here, down_own, _ = barrier(
            (gu.upper, gu.lower, near, ga.here, down_own, heads[0].ctx)
        )
        gd = Gather(down_own)
        gu.sides()
        gd.over_16()
        far = swap(here[1::2])
        heads[2] = attend(2, here)
        gu.upper, gu.lower, gd.own, near, far, _ = barrier((gu.upper, gu.lower, gd.own, near, far, heads[2].ctx))
        a_far = [near[0], far[0], near[1], far[1]]
        gu.cross()
        gd.over_8()
        near = swap(gu.here[::2])
        heads[1] = attend(1, a_far)
        gu.here, near, gd.upper, gd.lower, first, _ = barrier(
            (gu.here, near, gd.upper, gd.lower, a_far[0], heads[1].ctx)
        )
        gd.sides()
        far = swap(gu.here[1::2])
        heads[3] = attend(3, [first] + a_far[1:])
        gd.upper, gd.lower, near, far, ctx_last = barrier((gd.upper, gd.lower, near, far, heads[3].ctx))
        u_far = [near[0], far[0], near[1], far[1]]
        gd.cross()
        near = swap(gd.here[::2])
        u_in = gu.here + u_far
        input_w, input_maps = ga.here + a_far, weights_map
    else:
        heads = [attend(t, a_in[t]) for t in range(TB)]
        ctx_last = heads[-1].ctx
        input_w = [a[0] for a in a_in]
        input_maps = tuple(tuple((rel + t, start, rows) for rel, start, rows in a_map[t][0]) for t in range(TB))
    ctx, lctx = [h.ctx for h in heads[:-1]] + [ctx_last], [h.lctx for h in heads]
    wlay = [h.wlay for h in heads]
    e = run(
        functools.partial(ffn_up, u_map), "ffn_up", (flop * 4 * (fw + ow), 25e6, 4e6),
        dict(me=me),
        dict(x=text_input, xl=layout_input, ctx=ctx, lctx=lctx, wlay=wlay, tn=text_norm, ln=layout_norm),
        dict(u=u_in),
        dict(hid=sds((TB, S, fw), BF), slope=sds((TB, S, fw), BF), lhid=sds((TB, S, lfw), BF),
             lslope=sds((TB, S, lfw), BF), mid=rows_b, lmid=lay_b, n1=rows_f, ln1=lay_f, i1=sds((S, 128), F32)),
        {},
        dict(wu=text_w, wo=out_w, sems=dma((2,))),
    )
    if paired:
        gd.here, near, _ = barrier((gd.here, near, e.hid))
        far = swap(gd.here[1::2])
        d_in = gd.here + [near[0], far[0], near[1], far[1]]

    def outs_of(maps, wide):
        return [sds((len(m), m[0][2], wide), BF) for m in maps]

    f = run(
        functools.partial(ffn_down, d_map, d_send, base), "ffn_down", (flop * 8 * fw, 20e6),
        dict(me=me, length=length, group=group),
        dict(n1=e.n1, ln1=e.ln1, hid=e.hid, lhid=e.lhid, wlay=wlay, counts=[h.counts for h in heads],
             known=known, tn=text_norm, ln=layout_norm, cot=text_cotangent, lcot=layout_cotangent.T),
        dict(d=d_in),
        dict(result=rows_f, lresult=sds((lay_width, S), F32), gb=rows_b, lgb=lay_b, ge=rows_f, lge=lay_f,
             tg=sds((2, width), F32), lg=sds((2, lay_width), F32), ldown=[sds((lay_width, lfw), BF)] * TB),
        dict(out=outs_of(d_send, fw)),
        dict(wd=text_w, buf=text_w, gbt=V((width, S), BF), lgbt=V((lay_width, S), BF), sem=dma),
    )
    b = run(
        functools.partial(ffn_backward, (u_map, d_map)), "ffn_backward", (flop * 4 * (2 * fw + ow), 40e6),
        dict(me=me),
        dict(gb=after(f.gb, f.ldown[0]), lgb=f.lgb, ge=f.ge, lge=f.lge, slope=e.slope, lslope=e.lslope, n1=e.n1,
             ln1=e.ln1, i1=e.i1, wlay=wlay, tn=text_norm, ln=layout_norm),
        dict(u=u_in, d=d_in),
        dict(g1=rows_f, lg1=lay_f, dctx=[sds((S, ow), BF)] * TB, ldctx=[sds((S, low), BF)] * TB,
             dbef=sds((TB, S, fw), BF), ldbef=sds((TB, S, lfw), BF), tg=sds((2, width), F32),
             lg=sds((2, lay_width), F32)),
        {},
        dict(wu=text_w, wd=text_w, wo=out_w, acc=V((S, width), F32), lacc=V((S, lay_width), F32), sems=dma((3,))),
    )

    def up_part(mid):
        return run(
            functools.partial(up_grads, u_send), "up_grads", (flop * 4 * (fw + ow), 15e6),
            dict(me=me), dict(g1=b.g1, lg1=b.lg1, ctx=ctx, lctx=lctx, mid=mid, lmid=e.lmid, dbef=b.dbef, ldbef=b.ldbef),
            {},
            dict(lup=[sds((lay_width, low + lfw), BF)] * TB), dict(out=outs_of(u_send, fw + ow)),
            dict(buf=text_w, obuf=out_w, rt=V((width, S), BF), lrt=V((lay_width, S), BF), sems=dma((2,))),
        )

    def attend_back(t, dctx, ug):
        h = heads[t]
        return run(
            functools.partial(attention_backward, a_send[t]), "attention_backward", (flop * (qw + 6 * S), 8e6, 1e6),
            dict(me=me, length=length),
            dict(xt=heads[0].xt, xlt=heads[0].xlt, selt=select_t, qkv=h.qkv, lqkv=h.lqkv, ctx=h.ctx, lctx=h.lctx,
                 lse=h.lse, dctx=dctx, ldctx=b.ldctx[t], lup=ug.lup[t], ldown=f.ldown[t]),
            {},
            dict(dqkv=sds((S, qw), BF), ldqkv=sds((S, 3 * low), BF)),
            dict(out=[sds((DB, text_rows, qw + ow), BF)]),
            dict(buf=V((1, width, qw + ow), BF), qs=head, ks=head, vs=head, gs=head, stats=stats, sem=dma),
        )

    def input_part(g1, back):
        return run(
            functools.partial(input_grads, input_maps), "input_grads", (flop * 4 * qw, 10e6),
            dict(me=me),
            dict(g1=g1, lg1=b.lg1, dqkv=[k.dqkv for k in back], ldqkv=[k.ldqkv for k in back], wlay=wlay),
            dict(w=input_w), dict(dx=rows_f, dxl=sds((lay_width, S), F32)), {},
            dict(wq=qkv_w, sem=dma),
        )

    both = jnp.concatenate(
        [jnp.concatenate([b.tg, f.tg]), jnp.concatenate([b.lg, f.lg])], axis=1
    )
    if paired:
        ds, us, qs = Scatter(SPLIT), Scatter(SPLIT), Scatter(SAME)
        gate = lax.optimization_barrier
        near = exchange(f.out[0], 1)
        near, done, both = gate((near, b.g1, both))
        norm = exchange(both, 1)
        d_near, d_first, sent = near, [], [done]
        for h in range(2):
            d_first.append(ds.first(h, f.out[2 * h + 2], near[16 * h : 16 * h + 8]))
            sent.append(ds.sent)
        ug = up_part(after(e.mid, sent))
        d_first, norm, dctx, core, _ = gate((d_first, norm, b.dctx, ug.out[0], ug.lup))
        both = both + norm
        norm = exchange(both, 2)
        near = exchange(core, 1)
        d_side = ds.side([[f.out[2 * h + 1], d_near[16 * h + 8 : 16 * h + 16], d_first[h]] for h in range(2)])
        back = [None] * TB
        back[3] = attend_back(3, after(dctx[3], ds.sent, both), ug)
        d_side, near, norm, dctx, core, _ = gate((d_side, near, norm, dctx, back[3].out[0], back[3].dqkv))
        both = both + norm
        norm = exchange(both, 4)
        a_near = exchange(core, 1)
        d_8 = ds.over_8(d_side)
        u_near, u_first, sent = near, [], [ds.sent, both]
        for h in range(2):
            u_first.append(us.first(h, ug.out[2 * h + 2], near[16 * h : 16 * h + 8]))
            sent.append(us.sent)
        back[2] = attend_back(2, after(dctx[2], sent), ug)
        u_first, d_8, a_near, norm, dctx, _ = gate((u_first, d_8, a_near, norm, dctx, back[2].dqkv))
        d_16 = ds.over_16(d_8)
        both = both + norm
        norm = exchange(both, 8)
        a_rows = (slice(0, half), slice(half, text_rows))
        u_side = us.side([[ug.out[2 * h + 1], u_near[16 * h + 8 : 16 * h + 16], u_first[h]] for h in range(2)])
        a_got = [None, qs.first(1, back[2].out[0][:, a_rows[1]], a_near[:, a_rows[1]])]
        back[1] = attend_back(1, after(dctx[1], us.sent, qs.sent, ds.sent, both), ug)
        u_side, d_16, a_got[1], norm, dctx, core, _ = gate(
            (u_side, d_16, a_got[1], norm, dctx, back[1].out[0], back[1].dqkv)
        )
        both = both + norm
        norm = exchange(both, 16)
        u_8 = us.over_8(u_side)
        a_second = exchange(core, 1)
        a_got[0] = qs.first(0, back[2].out[0][:, a_rows[0]], a_near[:, a_rows[0]])
        back[0] = attend_back(0, after(dctx[0], us.sent, qs.sent, both), ug)
        u_8, a_got[0], a_second, norm, g1, _ = gate((u_8, a_got[0], a_second, norm, b.g1, back[0].dqkv))
        both = both + norm
        u_16 = us.over_16(u_8)
        got = qs.side([[back[0].out[0][:, a_rows[h]], a_second[:, a_rows[h]], a_got[h]] for h in range(2)])
        last = input_part(after(g1, qs.sent, us.sent), back)
        settled = [
            (f.out[1::2], d_near, d_first, d_side, d_8, d_16),
            (ug.out[1::2], u_near, u_first, u_side, u_8, u_16),
        ]
        got, settled, both, _ = gate((got, settled, both, last.dx))
        a_grad, d_grad, u_grad = qs.finish(qs.along_z(got)), ds.settle(*settled[0]), us.settle(*settled[1])
        q_grad, packed = a_grad[:, :qw], a_grad[:, qw:]
        l_grad = jnp.concatenate([packed[i * LROWS : i * LROWS + lay_rows] for i in range(3)], axis=1)
    else:

        def scatter(array):
            flat = array.reshape(-1, array.shape[2])
            return lax.psum_scatter(flat, everywhere, scatter_dimension=0, tiled=True).astype(F32)

        ug = up_part(e.mid)
        back = [attend_back(t, b.dctx[t], ug) for t in range(TB)]
        last = input_part(b.g1, back)
        d_grad = scatter(f.out[0])
        u_grad = scatter(ug.out[0])
        a_out = jnp.concatenate([k.out[0] for k in back])
        packed = [a_out[:, i * LROWS : i * LROWS + lay_rows, qw:] for i in range(3)]
        q_grad = scatter(a_out[:, :, :qw])
        l_grad = scatter(jnp.concatenate(packed, axis=2))
        both = lax.psum(both, ("dp", "tensor"))
    lqw = 3 * low
    return (
        f.result,
        f.lresult.T,
        last.dx,
        last.dxl.T,
        jnp.stack([q_grad[:, i * ow : (i + 1) * ow] for i in range(3)], axis=1),
        u_grad[:, fw:].T,
        u_grad[:, :fw],
        d_grad.T,
        both[:, :width],
        jnp.stack([l_grad[:, i * low : (i + 1) * low] for i in range(3)], axis=1),
        l_grad[:, lqw : lqw + low].T,
        l_grad[:, lqw + low : lqw + low + lfw],
        l_grad[:, lqw + low + lfw :].T,
        both[:, width:],
    )


def solution(mesh):
    in_specs = (
        P(("dp", "tensor"), None),
        P(("dp", "tensor"), None),
        P(("dp", "tensor"), None),
        P(("dp", "tensor"), None),
        P("dp"),
        P("dp"),
        P("dp", None, "tensor"),
        P("tensor", "dp"),
        P("dp", "tensor"),
        P("tensor", "dp"),
        P(),
        P("dp", None, "tensor"),
        P("tensor", "dp"),
        P("dp", "tensor"),
        P("tensor", "dp"),
        P(),
    )
    out_specs = (
        P(("dp", "tensor"), None),
        P(("dp", "tensor"), None),
        P(("dp", "tensor"), None),
        P(("dp", "tensor"), None),
        P("dp", None, "tensor"),
        P("tensor", "dp"),
        P("dp", "tensor"),
        P("tensor", "dp"),
        P(),
        P("dp", None, "tensor"),
        P("tensor", "dp"),
        P("dp", "tensor"),
        P("tensor", "dp"),
        P(),
    )
    return jax.shard_map(body, mesh=mesh, in_specs=in_specs, out_specs=out_specs, check_vma=False)
```

```python
import functools
import math

import jax
import jax.numpy as jnp
import numpy as np
from jax import lax
from jax.experimental import pallas as pl
from jax.experimental.layout import Layout, with_layout_constraint
from jax.experimental.pallas import tpu as pltpu
from jax.sharding import PartitionSpec as P

TEXT_HEAD = 64
LAY_HEAD = 16
S = 512
NGROUPS = 8

TB = 4
DB = 8
LROWS = 32

SPLIT = ((2, 4), (4, 2))
SAME = ((2, 4), (2, 4))

epsilon = 1e-05
neg_large = -1e30
root_half = 1.0 / math.sqrt(2.0)
root_twopi = 1.0 / math.sqrt(2.0 * math.pi)
text_scale = float(TEXT_HEAD) ** (-0.5)
layout_scale = float(LAY_HEAD) ** (-0.5)

HINT = 0.1
BF = jnp.bfloat16
F32 = jnp.float32
ANY = pl.BlockSpec(memory_space=pl.ANY)
VM = pl.BlockSpec(memory_space=pltpu.VMEM)
SM = pl.BlockSpec(memory_space=pltpu.SMEM)
PARAMS = pltpu.CompilerParams(vmem_limit_bytes=60 * 1024 * 1024)


def nn(a, b):
    return jnp.dot(a, b, preferred_element_type=F32)


def nt(a, b):
    return lax.dot_general(a, b, (((1,), (1,)), ((), ())), preferred_element_type=F32)


def sds(shape, dtype):
    return jax.ShapeDtypeStruct(shape, dtype)


def cost(flops, read, trans=0):
    return pl.CostEstimate(flops=int(flops * HINT), bytes_accessed=int(read * HINT), transcendentals=int(trans * HINT))


def load_pieces(refs, maps, d0, size, lanes, dst, sem):
    for ref, entries in zip(refs, maps):
        for i, entry in enumerate(entries):
            if entry is None:
                continue
            rel, start, rows = entry
            spot = pl.multiple_of(((rel // TB) ^ d0) * size + start, rows)
            pltpu.make_async_copy(
                ref.at[i, :, lanes[0] : lanes[1]], dst.at[rel % TB, pl.ds(spot, rows), :], sem
            ).start()


def send_pieces(outs, maps, d0, buf, size, lanes, sem):
    for out, entries in zip(outs, maps):
        for i, entry in enumerate(entries):
            if entry is None:
                continue
            rel, start, rows = entry
            spot = pl.multiple_of(((rel // TB) ^ d0) * size + start, rows)
            pltpu.make_async_copy(
                buf.at[rel % TB, pl.ds(spot, rows), :], out.at[i, :, lanes[0] : lanes[1]], sem
            ).start()


def wait_pieces(dst, sem):
    pltpu.make_async_copy(dst, dst, sem).wait()


class Refs:
    def __init__(self, **entries):
        self.__dict__.update(entries)


def run(kernel, name, price, scalars, arrays, hbm, outs, hbm_outs, scratch):
    ins, in_tree = jax.tree.flatten((scalars, arrays, hbm))
    in_specs = [SM] * len(jax.tree.leaves(scalars)) + [VM] * len(jax.tree.leaves(arrays))
    in_specs += [ANY] * len(jax.tree.leaves(hbm))
    out_shapes, out_tree = jax.tree.flatten((outs, hbm_outs))
    out_specs = [VM] * len(jax.tree.leaves(outs)) + [ANY] * len(jax.tree.leaves(hbm_outs))
    scratch_shapes, scratch_names = list(scratch.values()), list(scratch)

    def inner(*refs):
        a, b = len(ins), len(ins) + len(out_shapes)
        s, v, h = jax.tree.unflatten(in_tree, refs[:a])
        o, ho = jax.tree.unflatten(out_tree, refs[a:b])
        kernel(Refs(**s, **v, **h, **o, **ho, **dict(zip(scratch_names, refs[b:]))))

    got = pl.pallas_call(
        inner,
        name=name,
        in_specs=in_specs,
        out_specs=out_specs,
        out_shape=out_shapes,
        scratch_shapes=scratch_shapes,
        compiler_params=PARAMS,
        cost_estimate=cost(*price),
    )(*ins)
    o, ho = jax.tree.unflatten(out_tree, got)
    return Refs(**o, **ho)


def attention_forward(maps, counted, k):
    d0 = k.me[0] // TB
    lay_width = k.select.shape[1]
    text_rows, lay_rows = k.wq.shape[1] // DB, lay_width // DB
    width = k.qkv.shape[1]
    load_pieces(k.w, maps, d0, text_rows, (0, k.wq.shape[2]), k.wq, k.sem)
    live = lax.broadcasted_iota(jnp.int32, (1, S), 1) < k.length[0]
    heads = width // 3 // TEXT_HEAD
    tw, lw = heads * TEXT_HEAD, heads * LAY_HEAD
    if hasattr(k, "xt"):
        k.xt[...] = k.x[...].T
        k.xlt[...] = k.xl[...].T
    wait_pieces(k.wq, k.sem)
    packed = k.wq[0, :, width:]
    if counted:
        place = lax.broadcasted_iota(jnp.int32, (8, k.wq.shape[1]), 1) % text_rows
        spare = (LROWS - lay_rows) // 2
        high = (place >= lay_rows) & (place < lay_rows + spare)
        low = (place >= lay_rows + spare) & (place < LROWS)
        digits = jnp.where(high, 32.0, jnp.where(low, 1.0, 0.0)).astype(BF)
        k.counts[...] = nn(digits, packed[:, 0:128])
    else:
        k.counts[...] = jnp.zeros(k.counts.shape, F32)
    wlt = jnp.concatenate([nn(k.select[j], packed).astype(BF) for j in range(3)], axis=1)
    k.wlay[...] = wlt
    qkv = nn(k.x[...], k.wq[0, :, 0:width]).astype(BF)
    k.qkv[...] = qkv
    lqkv = nn(k.xl[...], wlt[:, : 3 * lw]).astype(BF)
    k.lqkv[...] = lqkv
    for h in range(heads):
        a, b = h * TEXT_HEAD, h * LAY_HEAD
        ta, tb = slice(a, a + TEXT_HEAD), slice(b, b + LAY_HEAD)
        q = jnp.concatenate([qkv[:, ta] * BF(text_scale), lqkv[:, tb] * BF(layout_scale)], axis=1)
        key = jnp.concatenate([qkv[:, tw + a : tw + a + TEXT_HEAD], lqkv[:, lw + b : lw + b + LAY_HEAD]], axis=1)
        v = jnp.concatenate(
            [qkv[:, 2 * tw + a : 2 * tw + a + TEXT_HEAD], lqkv[:, 2 * lw + b : 2 * lw + b + LAY_HEAD]], axis=1
        )
        logits = jnp.where(live, nt(q, key), neg_large)
        top = jnp.max(logits, axis=-1, keepdims=True)
        raw = jnp.exp(logits - top)
        total = jnp.sum(raw, axis=-1, keepdims=True)
        probs = (raw * (1.0 / total)).astype(BF)
        ctx = nn(probs, v).astype(BF)
        k.ctx[:, ta] = ctx[:, :TEXT_HEAD]
        k.lctx[:, tb] = ctx[:, TEXT_HEAD:]
        k.lse[:, h : h + 1] = top + jnp.log(total)


def ffn_up(maps, k):
    d0 = k.me[0] // TB
    rows, fw, ow = k.wu.shape[1] // DB, k.wu.shape[2], k.wo.shape[2]
    low = k.lctx[0].shape[1]
    lf = (k.wlay[0].shape[1] - 4 * low) // 2
    load_pieces(k.u, maps, d0, rows, (fw, fw + ow), k.wo, k.sems.at[0])
    load_pieces(k.u, maps, d0, rows, (0, fw), k.wu, k.sems.at[1])
    tn, ln = k.tn[...], k.ln[...]
    lattn = nt(k.lctx[0][...], k.wlay[0][:, 3 * low : 4 * low])
    for t in range(1, TB):
        lattn = lattn + nt(k.lctx[t][...], k.wlay[t][:, 3 * low : 4 * low])
    wait_pieces(k.wo, k.sems.at[0])
    attn = nt(k.ctx[0][...], k.wo[0])
    for t in range(1, TB):
        attn = attn + nt(k.ctx[t][...], k.wo[t])
    n1, i1 = norm_stats(k.x[...].astype(F32) + attn)
    ln1, li1 = norm_stats(k.xl[...].astype(F32) + lattn)
    k.n1[...] = n1
    k.ln1[...] = ln1
    k.i1[:, 0:1] = i1
    k.i1[:, 1:2] = li1
    k.mid[...] = (n1 * tn[0:1] + tn[1:2]).astype(BF)
    k.lmid[...] = (ln1 * ln[0:1] + ln[1:2]).astype(BF)
    wait_pieces(k.wu, k.sems.at[1])

    def gelu(before):
        cdf = 0.5 * (1.0 + lax.erf(before * root_half))
        slope = cdf + before * jnp.exp(-0.5 * before * before) * root_twopi
        return (before * cdf).astype(BF), slope.astype(BF)

    def step(t, carry):
        hid, slope = gelu(nn(k.mid[...], k.wu[t]))
        k.hid[t] = hid
        k.slope[t] = slope
        return carry

    lax.fori_loop(0, TB, step, 0)
    for t in range(TB):
        lhid, lslope = gelu(nn(k.lmid[...], k.wlay[t][:, 4 * low : 4 * low + lf]))
        k.lhid[t] = lhid
        k.lslope[t] = lslope


def ffn_down(maps, sent, base, k):
    d0 = k.me[0] // TB
    rows, fw = k.wd.shape[1] // DB, k.wd.shape[2]
    lf = k.lhid.shape[2]
    load_pieces(k.d, maps, d0, rows, (0, fw), k.wd, k.sem)
    counts = k.known[...]
    for t in range(TB):
        counts = counts + k.counts[t][0:1]
    same = lax.broadcasted_iota(jnp.int32, counts.shape, 1) == k.group[0]
    mine = jnp.sum(jnp.where(same, counts, 0.0), axis=1, keepdims=True)
    keep = (lax.broadcasted_iota(jnp.int32, (S, 1), 0) < k.length[0]).astype(F32)
    scale = keep * (base / (mine + base))
    tn, ln = k.tn[...], k.ln[...]
    lbranch = k.ln1[...] * ln[0:1] + ln[1:2]
    for t in range(TB):
        lbranch = lbranch + nt(k.lhid[t], k.wlay[t][:, k.wlay[t].shape[1] - lf :])
    ln2, li2 = norm_stats(lbranch)
    k.lresult[...] = ((ln2 * ln[2:3] + ln[3:4]) * keep).T
    lge, lgain, lshift = norm_back(k.lcot[...].T * scale, ln2, li2, ln[2:3])
    k.lge[...] = lge
    k.lgb[...] = lge.astype(BF)
    k.lg[0:1] = lgain
    k.lg[1:2] = lshift
    wait_pieces(k.wd, k.sem)
    branch = k.n1[...] * tn[0:1] + tn[1:2]
    for t in range(TB):
        branch = branch + nt(k.hid[t], k.wd[t])
    n2, i2 = norm_stats(branch)
    k.result[...] = (n2 * tn[2:3] + tn[3:4]) * keep
    ge, gain, shift = norm_back(k.cot[...] * scale, n2, i2, tn[2:3])
    k.ge[...] = ge
    k.gb[...] = ge.astype(BF)
    k.tg[0:1] = gain
    k.tg[1:2] = shift
    k.gbt[...] = k.gb[...].T
    k.lgbt[...] = k.lgb[...].T

    def step(t, carry):
        k.buf[t] = nn(k.gbt[...], k.hid[t]).astype(BF)
        return carry

    lax.fori_loop(0, TB, step, 0)
    send_pieces(k.out, sent, d0, k.buf, rows, (0, fw), k.sem)
    for t in range(TB):
        k.ldown[t][...] = nn(k.lgbt[...], k.lhid[t]).astype(BF)
    wait_pieces(k.buf, k.sem)


def ffn_backward(maps, k):
    d0 = k.me[0] // TB
    rows, fw, ow = k.wu.shape[1] // DB, k.wu.shape[2], k.wo.shape[2]
    low = k.ldctx[0].shape[1]
    lf = (k.wlay[0].shape[1] - 4 * low) // 2
    load_pieces(k.d, maps[1], d0, rows, (0, fw), k.wd, k.sems.at[0])
    load_pieces(k.u, maps[0], d0, rows, (0, fw), k.wu, k.sems.at[1])
    load_pieces(k.u, maps[0], d0, rows, (fw, fw + ow), k.wo, k.sems.at[2])
    tn, ln = k.tn[...], k.ln[...]
    k.acc[...] = k.ge[...]
    k.lacc[...] = k.lge[...]
    for t in range(TB):
        ldbef = (nn(k.lgb[...], k.wlay[t][:, 4 * low + lf :]) * k.lslope[t]).astype(BF)
        k.ldbef[t] = ldbef
        k.lacc[...] += nt(ldbef, k.wlay[t][:, 4 * low : 4 * low + lf])
    wait_pieces(k.wd, k.sems.at[0])
    wait_pieces(k.wu, k.sems.at[1])

    def step(t, carry):
        dbef = (nn(k.gb[...], k.wd[t]) * k.slope[t]).astype(BF)
        k.dbef[t] = dbef
        k.acc[...] += nt(dbef, k.wu[t])
        return carry

    lax.fori_loop(0, TB, step, 0)
    g1, gain, shift = norm_back(k.acc[...], k.n1[...], k.i1[:, 0:1], tn[0:1])
    k.g1[...] = g1
    k.tg[0:1] = gain
    k.tg[1:2] = shift
    lg1, lgain, lshift = norm_back(k.lacc[...], k.ln1[...], k.i1[:, 1:2], ln[0:1])
    k.lg1[...] = lg1
    k.lg[0:1] = lgain
    k.lg[1:2] = lshift
    ga = g1.astype(BF)
    lga = lg1.astype(BF)
    wait_pieces(k.wo, k.sems.at[2])
    for t in range(TB):
        k.dctx[t][...] = nn(ga, k.wo[t]).astype(BF)
        k.ldctx[t][...] = nn(lga, k.wlay[t][:, 3 * low : 4 * low]).astype(BF)


def up_grads(maps, k):
    rows, fw, ow = k.buf.shape[1] // DB, k.buf.shape[2], k.obuf.shape[2]
    low = k.lctx[0].shape[1]
    d0 = k.me[0] // TB
    k.rt[...] = k.g1[...].astype(BF).T
    k.lrt[...] = k.lg1[...].astype(BF).T
    for t in range(TB):
        k.obuf[t] = nn(k.rt[...], k.ctx[t][...]).astype(BF)
        k.lup[t][:, 0:low] = nn(k.lrt[...], k.lctx[t][...]).astype(BF)
    send_pieces(k.out, maps, d0, k.obuf, rows, (fw, fw + ow), k.sems.at[1])
    k.rt[...] = k.mid[...].T
    k.lrt[...] = k.lmid[...].T

    def step(t, carry):
        k.buf[t] = nn(k.rt[...], k.dbef[t]).astype(BF)
        return carry

    lax.fori_loop(0, TB, step, 0)
    send_pieces(k.out, maps, d0, k.buf, rows, (0, fw), k.sems.at[0])
    for t in range(TB):
        k.lup[t][:, low:] = nn(k.lrt[...], k.ldbef[t]).astype(BF)
    wait_pieces(k.obuf, k.sems.at[1])
    wait_pieces(k.buf, k.sems.at[0])


def attention_backward(maps, k):
    width = k.qkv.shape[1]
    heads = width // 3 // TEXT_HEAD
    tw, lw = heads * TEXT_HEAD, heads * LAY_HEAD
    text_rows = k.buf.shape[1] // DB
    live = lax.broadcasted_iota(jnp.int32, (1, S), 1) < k.length[0]
    for h in range(heads):
        a, b = h * TEXT_HEAD, h * LAY_HEAD
        ta, tb = slice(a, a + TEXT_HEAD), slice(b, b + LAY_HEAD)
        for j, (dst, one, two) in enumerate(((k.qs, text_scale, layout_scale), (k.ks, 1.0, 1.0), (k.vs, 1.0, 1.0))):
            c, d = j * tw + a, j * lw + b
            parts = [k.qkv[:, c : c + TEXT_HEAD] * BF(one), k.lqkv[:, d : d + LAY_HEAD] * BF(two)]
            dst[h] = jnp.concatenate(parts, axis=1)
        gt, gl = k.dctx[:, ta], k.ldctx[:, tb]
        k.gs[h] = jnp.concatenate([gt, gl], axis=1)
        dot_t = jnp.sum(gt.astype(F32) * k.ctx[:, ta].astype(F32), axis=-1, keepdims=True)
        dot_l = jnp.sum(gl.astype(F32) * k.lctx[:, tb].astype(F32), axis=-1, keepdims=True)
        k.stats[h, :, 0:1] = dot_t
        k.stats[h, :, 1:2] = dot_t + dot_l
        k.stats[h, :, 2:3] = k.lse[:, h : h + 1]

    def step(h, carry):
        q, key, v, g = k.qs[h], k.ks[h], k.vs[h], k.gs[h]
        gt, vt = g[:, :TEXT_HEAD], v[:, :TEXT_HEAD]
        logits = jnp.where(live, nt(q, key), neg_large)
        probs = jnp.exp(logits - k.stats[h, :, 2:3])
        low = (probs * (nt(gt, vt) - k.stats[h, :, 0:1])).astype(BF)
        llow = (probs * (nt(g, v) - k.stats[h, :, 1:2])).astype(BF)
        dq = nn(low, key[:, :TEXT_HEAD]) * text_scale
        dql = nn(llow, key[:, TEXT_HEAD:]) * layout_scale
        dk = nn(q[:, :TEXT_HEAD].T, low).T
        dkl = nn(q[:, TEXT_HEAD:].T, llow).T
        dv = nn(g.T, probs.astype(BF)).T
        k.qs[h] = jnp.concatenate([dq, dql], axis=1).astype(BF)
        k.ks[h] = jnp.concatenate([dk, dkl], axis=1).astype(BF)
        k.vs[h] = dv.astype(BF)
        return carry

    lax.fori_loop(0, heads, step, 0)
    for h in range(heads):
        for j, src in enumerate((k.qs, k.ks, k.vs)):
            a, b = j * tw + h * TEXT_HEAD, j * lw + h * LAY_HEAD
            k.dqkv[:, a : a + TEXT_HEAD] = src[h, :, :TEXT_HEAD]
            k.ldqkv[:, b : b + LAY_HEAD] = src[h, :, TEXT_HEAD:]
    k.buf[0, :, 0:width] = nn(k.xt[...], k.dqkv[...]).astype(BF)
    lgrad = jnp.concatenate([nn(k.xlt[...], k.ldqkv[...]).astype(BF), k.lup[...], k.ldown[...]], axis=1)
    third = width // 3
    packed = nn(k.selt[0], lgrad[:, 0:third])
    for j in range(1, 3):
        packed = packed + nn(k.selt[j], lgrad[:, j * third : (j + 1) * third])
    k.buf[0, :, width:] = packed.astype(BF)
    d0 = k.me[0] // TB
    send_pieces(k.out, maps, d0, k.buf, text_rows, (0, k.buf.shape[2]), k.sem)
    wait_pieces(k.buf, k.sem)


def input_grads(maps, k):
    d0 = k.me[0] // TB
    text_rows, width = k.wq.shape[1] // DB, k.dqkv[0].shape[1]
    lw = k.ldqkv[0].shape[1]
    load_pieces(k.w, maps, d0, text_rows, (0, k.wq.shape[2]), k.wq, k.sem)
    dxl = k.lg1[...]
    for t in range(TB):
        dxl = dxl + nt(k.ldqkv[t][...], k.wlay[t][:, :lw])
    k.dxl[...] = dxl.T
    wait_pieces(k.wq, k.sem)
    dx = k.g1[...]
    for t in range(TB):
        dx = dx + nt(k.dqkv[t][...], k.wq[t, :, 0:width])
    k.dx[...] = dx


def norm_stats(values):
    centred = values - jnp.mean(values, axis=-1, keepdims=True)
    inverse = lax.rsqrt(jnp.mean(centred * centred, axis=-1, keepdims=True) + epsilon)
    return centred * inverse, inverse


def norm_back(upstream, normed, inverse, gain):
    scaled = upstream * gain
    inner = (
        scaled
        - jnp.mean(scaled, axis=-1, keepdims=True)
        - normed * jnp.mean(scaled * normed, axis=-1, keepdims=True)
    )
    return (
        inverse * inner,
        jnp.sum(upstream * normed, axis=0, keepdims=True),
        jnp.sum(upstream, axis=0, keepdims=True),
    )


def exchange(array, bit):
    size = lax.axis_size("dp") * lax.axis_size("tensor")
    return lax.ppermute(array, ("dp", "tensor"), [(i, i ^ bit) for i in range(size)])


Z = (0, 8, 16, 24)


def gather_maps(rows, steps):
    half = rows // 2
    tops = ((0, 0, 2), (4, 0, 2), (0, half, 4), (2, half, 4))
    return tuple(
        tuple((z | inner | top | core, start, half) for inner in (0, step) for z in steps)
        for core in (0, 1)
        for top, start, step in tops
    )


def scatter_maps(start, rows, bits):
    return tuple(
        tuple((z | inner | top, start, rows) for inner in (0, bits[1]) for z in Z)
        for top in (0, 1, bits[0], bits[0] | 1)
    )


def block(maps, t):
    return tuple(
        tuple((rel - t, start, rows) if rel % TB == t else None for rel, start, rows in entries) for entries in maps
    )


def after(array, *needed):
    return lax.optimization_barrier((array, needed))[0]


def rows_major(array):
    return with_layout_constraint(array, Layout(major_to_minor=(0, 1, 2)))


class Gather:
    def __init__(self, own):
        self.own, self.half = rows_major(own[None]), own.shape[0] // 2

    def along_z(self):
        got = [self.own] + [rows_major(exchange(self.own, z)) for z in Z[1:]]
        self.upper = rows_major(jnp.concatenate([g[:, : self.half] for g in got], axis=0))
        self.lower = rows_major(jnp.concatenate([g[:, self.half :] for g in got], axis=0))
        return self.lower

    def over_16(self):
        self.own = rows_major(jnp.concatenate([self.own, exchange(self.own, 16)], axis=0))

    def over_8(self):
        got = [self.own, exchange(self.own, 8)]
        self.upper = rows_major(jnp.concatenate([g[:, : self.half] for g in got], axis=0))
        self.lower = rows_major(jnp.concatenate([g[:, self.half :] for g in got], axis=0))

    def sides(self):
        self.upper = rows_major(jnp.concatenate([self.upper, exchange(self.upper, 2)], axis=0))
        self.lower = rows_major(jnp.concatenate([self.lower, exchange(self.lower, 4)], axis=0))
        return self.lower

    def cross(self):
        self.here = [self.upper, rows_major(exchange(self.upper, 4)), self.lower, rows_major(exchange(self.lower, 2))]
        return self.here


def swap(arrays):
    return [rows_major(exchange(array, 1)) for array in arrays]


def rounded(parts):
    return rows_major(sum(p.astype(F32) for p in parts).astype(BF))


class Scatter:
    def __init__(self, bits):
        self.bits = bits

    def first(self, h, far, near):
        self.sent = rounded([far, near])
        return exchange(self.sent, self.bits[h][0])

    def side(self, parts):
        self.parts = parts
        self.sent = [rounded([p[4:8] for p in half]) for half in parts]
        return [exchange(sent, self.bits[h][1]) for h, sent in enumerate(self.sent)]

    def along_z(self, got):
        self.parts = [half + [g] for half, g in zip(self.parts, got)]
        self.sent = [
            rows_major(jnp.concatenate([rounded([p[i : i + 1] for p in half]) for half in self.parts], axis=1))
            for i in range(1, 4)
        ]
        return [exchange(piece, z) for piece, z in zip(self.sent, Z[1:])]

    def over_8(self, got):
        self.parts = [half + [g] for half, g in zip(self.parts, got)]
        self.sent = rows_major(
            jnp.concatenate(
                [
                    jnp.concatenate([rounded([p[i : i + 1] for p in half]) for half in self.parts], axis=1)
                    for i in (1, 3)
                ]
            )
        )
        return exchange(self.sent, 8)

    def over_16(self, got):
        rows = got.shape[1] // 2
        parts = [[p[2:3] for p in half] + [got[1:2, h * rows : (h + 1) * rows]] for h, half in enumerate(self.parts)]
        self.sent = rows_major(jnp.concatenate([rounded(half) for half in parts], axis=1))
        return exchange(self.sent, 16)

    def settle(self, own, near, first, side, over_8, over_16):
        rows = own[0].shape[1]
        halves = [
            [own[h][0], near[16 * h + 8], first[h][0], side[h][0], over_8[0, h * rows : (h + 1) * rows]]
            for h in range(2)
        ]
        kept = jnp.concatenate([sum(p.astype(F32) for p in half) for half in halves], axis=0)
        return kept + over_16[0].astype(F32)

    def finish(self, got):
        kept = jnp.concatenate([sum(p[0].astype(F32) for p in half) for half in self.parts], axis=0)
        return kept + sum(g[0].astype(F32) for g in got)


def body(
    text_input,
    layout_input,
    text_cotangent,
    layout_cotangent,
    page_group,
    page_length,
    text_qkv,
    text_out,
    text_up,
    text_down,
    text_norm,
    layout_qkv,
    layout_out,
    layout_up,
    layout_down,
    layout_norm,
):
    dp_pages = page_length.shape[0]
    dp, tensor = lax.axis_size("dp"), lax.axis_size("tensor")
    width, lay_width = text_input.shape[1], layout_input.shape[1]
    text_rows, lay_rows = width // DB, lay_width // DB

    qkv_own = jnp.concatenate([text_qkv[:, i] for i in range(3)], axis=1)
    up_own = jnp.concatenate([text_up, text_out.T], axis=1)
    down_own = text_down.T
    lay_own = jnp.concatenate(
        [layout_qkv[:, i] for i in range(3)] + [layout_out.T, layout_up, layout_down.T], axis=1
    )
    qw, ow, fw = qkv_own.shape[1], text_out.shape[0], text_up.shape[1]
    low, lfw, lpack = layout_out.shape[0], layout_up.shape[1], lay_own.shape[1]
    mine = jnp.arange(dp_pages, dtype=jnp.int32) == lax.axis_index("tensor")
    length = jnp.sum(jnp.where(mine, page_length, 0)).reshape(1)
    group = jnp.sum(jnp.where(mine, page_group, 0)).reshape(1)
    base = float(dp_pages * dp * S) / (2.0 * NGROUPS)
    paired = dp == DB and tensor == TB
    everywhere = ("tensor", "dp")
    if paired:
        digits = jnp.concatenate([page_length >> 5, page_length & 31])[:, None]
        groups = jnp.concatenate([page_group, page_group])[:, None]
        column = lax.broadcasted_iota(jnp.int32, (LROWS - lay_rows, lpack), 1) == groups
        spare = jnp.where(column, digits, 0).astype(BF)
        packed = jnp.concatenate([lay_own, spare], axis=0)
        packed = jnp.concatenate([packed[:, i * ow : (i + 1) * ow] for i in range(3)], axis=0)
        ga = Gather(jnp.concatenate([qkv_own, packed], axis=1))
        barrier = lax.optimization_barrier
        ga.along_z()
        ga.sides()
        ga.upper, ga.lower, up_own = barrier((ga.upper, ga.lower, up_own))
        gu = Gather(up_own)
        ga.cross()
        gu.over_16()
        weights_map = gather_maps(text_rows, Z)
        a_map = [block(weights_map[4 * (t % 2) : 4 * (t % 2) + 4], t) for t in range(TB)]
        u_map = d_map = gather_maps(text_rows, (0, 16, 8, 24))
        half = text_rows // 2
        up, lo = scatter_maps(0, half, SPLIT[0]), scatter_maps(half, half, SPLIT[1])
        u_send = d_send = (up[3] + up[1] + lo[3] + lo[1], up[0], up[2], lo[0], lo[2])
        a_send = [(block(scatter_maps(0, text_rows, SAME[0]), t)[t],) for t in range(TB)]
        me = (lax.axis_index("dp") * TB + lax.axis_index("tensor")).astype(jnp.int32).reshape(1)
        known = jnp.zeros((1, 128), F32)
    else:

        def gather(array, rows):
            whole = lax.all_gather(array, everywhere, axis=0, tiled=True)
            return whole.reshape(TB * DB, rows, array.shape[1])

        spare = ((0, 0), (0, LROWS - lay_rows), (0, 0))
        packed = jnp.pad(gather(lay_own, lay_rows), spare)
        packed = jnp.concatenate([packed[:, :, i * ow : (i + 1) * ow] for i in range(3)], axis=1)
        first = jnp.concatenate([gather(qkv_own, text_rows), packed], axis=2)
        a_in = [[first[t * DB : (t + 1) * DB]] for t in range(TB)]
        u_in, d_in = [gather(up_own, text_rows)], [gather(down_own, text_rows)]
        u_map = d_map = u_send = d_send = (tuple((d * TB + t, 0, text_rows) for t in range(TB) for d in range(DB)),)
        a_map = a_send = [(tuple((d * TB, 0, text_rows) for d in range(DB)),)] * TB
        me = jnp.zeros((1,), jnp.int32)
        labels = jnp.arange(NGROUPS, dtype=jnp.int32)
        member = (page_group[:, None] == labels[None, :]).astype(F32)
        counts = lax.psum(jnp.sum(member * page_length.astype(F32)[:, None], axis=0), "dp")
        known = jnp.pad(counts, (0, 128 - NGROUPS)).reshape(1, 128)

    chosen = np.zeros((3, lay_width, width), np.float32)
    for j in range(3):
        for a in range(lay_width):
            chosen[j, a, (a // lay_rows) * text_rows + j * LROWS + a % lay_rows] = 1.0
    select, select_t = jnp.asarray(chosen, BF), jnp.asarray(chosen.transpose(0, 2, 1), BF)
    V, dma = pltpu.VMEM, pltpu.SemaphoreType.DMA
    flop = 2.0 * S * width
    rows_f, rows_b = sds((S, width), F32), sds((S, width), BF)
    lay_f, lay_b = sds((S, lay_width), F32), sds((S, lay_width), BF)
    heads_held = ow // TEXT_HEAD
    head, stats = V((heads_held, S, TEXT_HEAD + LAY_HEAD), BF), V((heads_held, S, 128), F32)
    text_w, out_w, qkv_w = V((TB, width, fw), BF), V((TB, width, ow), BF), V((TB, width, qw + ow), BF)

    def attend(t, w):
        outs = dict(
            qkv=sds((S, qw), BF), lqkv=sds((S, 3 * low), BF), ctx=sds((S, ow), BF), lctx=sds((S, low), BF),
            lse=sds((S, 128), F32), wlay=sds((lay_width, lpack), BF), counts=sds((8, 128), F32),
        )
        if t == 0:
            outs.update(xt=sds((width, S), BF), xlt=sds((lay_width, S), BF))
        return run(
            functools.partial(attention_forward, a_map[t], paired and t == 0), "attention_forward",
            (flop * (qw + 3 * S), 5e6, 1e6),
            dict(me=me, length=length), dict(x=text_input, xl=layout_input, select=select), dict(w=w),
            outs, {},
            dict(wq=V((1, width, qw + ow), BF), sem=dma),
        )

    if paired:
        ga.here, gu.own = barrier((ga.here, gu.own))
        heads = [None] * TB
        gu.over_8()
        near = swap(ga.here[::2])
        heads[0] = attend(0, ga.here)
        gu.upper, gu.lower, near, here, down_own, _ = barrier(
            (gu.upper, gu.lower, near, ga.here, down_own, heads[0].ctx)
        )
        gd = Gather(down_own)
        gu.sides()
        gd.over_16()
        far = swap(here[1::2])
        heads[2] = attend(2, here)
        gu.upper, gu.lower, gd.own, near, far, _ = barrier((gu.upper, gu.lower, gd.own, near, far, heads[2].ctx))
        a_far = [near[0], far[0], near[1], far[1]]
        gu.cross()
        gd.over_8()
        near = swap(gu.here[::2])
        heads[1] = attend(1, a_far)
        gu.here, near, gd.upper, gd.lower, first, _ = barrier(
            (gu.here, near, gd.upper, gd.lower, a_far[0], heads[1].ctx)
        )
        gd.sides()
        far = swap(gu.here[1::2])
        heads[3] = attend(3, [first] + a_far[1:])
        gd.upper, gd.lower, near, far, ctx_last = barrier((gd.upper, gd.lower, near, far, heads[3].ctx))
        u_far = [near[0], far[0], near[1], far[1]]
        gd.cross()
        near = swap(gd.here[::2])
        u_in = gu.here + u_far
        input_w, input_maps = ga.here + a_far, weights_map
    else:
        heads = [attend(t, a_in[t]) for t in range(TB)]
        ctx_last = heads[-1].ctx
        input_w = [a[0] for a in a_in]
        input_maps = tuple(tuple((rel + t, start, rows) for rel, start, rows in a_map[t][0]) for t in range(TB))
    ctx, lctx = [h.ctx for h in heads[:-1]] + [ctx_last], [h.lctx for h in heads]
    wlay = [h.wlay for h in heads]
    e = run(
        functools.partial(ffn_up, u_map), "ffn_up", (flop * 4 * (fw + ow), 25e6, 4e6),
        dict(me=me),
        dict(x=text_input, xl=layout_input, ctx=ctx, lctx=lctx, wlay=wlay, tn=text_norm, ln=layout_norm),
        dict(u=u_in),
        dict(hid=sds((TB, S, fw), BF), slope=sds((TB, S, fw), BF), lhid=sds((TB, S, lfw), BF),
             lslope=sds((TB, S, lfw), BF), mid=rows_b, lmid=lay_b, n1=rows_f, ln1=lay_f, i1=sds((S, 128), F32)),
        {},
        dict(wu=text_w, wo=out_w, sems=dma((2,))),
    )
    if paired:
        gd.here, near, _ = barrier((gd.here, near, e.hid))
        far = swap(gd.here[1::2])
        d_in = gd.here + [near[0], far[0], near[1], far[1]]

    def outs_of(maps, wide):
        return [sds((len(m), m[0][2], wide), BF) for m in maps]

    f = run(
        functools.partial(ffn_down, d_map, d_send, base), "ffn_down", (flop * 8 * fw, 20e6),
        dict(me=me, length=length, group=group),
        dict(n1=e.n1, ln1=e.ln1, hid=e.hid, lhid=e.lhid, wlay=wlay, counts=[h.counts for h in heads],
             known=known, tn=text_norm, ln=layout_norm, cot=text_cotangent, lcot=layout_cotangent.T),
        dict(d=d_in),
        dict(result=rows_f, lresult=sds((lay_width, S), F32), gb=rows_b, lgb=lay_b, ge=rows_f, lge=lay_f,
             tg=sds((2, width), F32), lg=sds((2, lay_width), F32), ldown=[sds((lay_width, lfw), BF)] * TB),
        dict(out=outs_of(d_send, fw)),
        dict(wd=text_w, buf=text_w, gbt=V((width, S), BF), lgbt=V((lay_width, S), BF), sem=dma),
    )
    b = run(
        functools.partial(ffn_backward, (u_map, d_map)), "ffn_backward", (flop * 4 * (2 * fw + ow), 40e6),
        dict(me=me),
        dict(gb=after(f.gb, f.ldown[0]), lgb=f.lgb, ge=f.ge, lge=f.lge, slope=e.slope, lslope=e.lslope, n1=e.n1,
             ln1=e.ln1, i1=e.i1, wlay=wlay, tn=text_norm, ln=layout_norm),
        dict(u=u_in, d=d_in),
        dict(g1=rows_f, lg1=lay_f, dctx=[sds((S, ow), BF)] * TB, ldctx=[sds((S, low), BF)] * TB,
             dbef=sds((TB, S, fw), BF), ldbef=sds((TB, S, lfw), BF), tg=sds((2, width), F32),
             lg=sds((2, lay_width), F32)),
        {},
        dict(wu=text_w, wd=text_w, wo=out_w, acc=V((S, width), F32), lacc=V((S, lay_width), F32), sems=dma((3,))),
    )

    def up_part(mid):
        return run(
            functools.partial(up_grads, u_send), "up_grads", (flop * 4 * (fw + ow), 15e6),
            dict(me=me), dict(g1=b.g1, lg1=b.lg1, ctx=ctx, lctx=lctx, mid=mid, lmid=e.lmid, dbef=b.dbef, ldbef=b.ldbef),
            {},
            dict(lup=[sds((lay_width, low + lfw), BF)] * TB), dict(out=outs_of(u_send, fw + ow)),
            dict(buf=text_w, obuf=out_w, rt=V((width, S), BF), lrt=V((lay_width, S), BF), sems=dma((2,))),
        )

    def attend_back(t, dctx, ug):
        h = heads[t]
        return run(
            functools.partial(attention_backward, a_send[t]), "attention_backward", (flop * (qw + 6 * S), 8e6, 1e6),
            dict(me=me, length=length),
            dict(xt=heads[0].xt, xlt=heads[0].xlt, selt=select_t, qkv=h.qkv, lqkv=h.lqkv, ctx=h.ctx, lctx=h.lctx,
                 lse=h.lse, dctx=dctx, ldctx=b.ldctx[t], lup=ug.lup[t], ldown=f.ldown[t]),
            {},
            dict(dqkv=sds((S, qw), BF), ldqkv=sds((S, 3 * low), BF)),
            dict(out=[sds((DB, text_rows, qw + ow), BF)]),
            dict(buf=V((1, width, qw + ow), BF), qs=head, ks=head, vs=head, gs=head, stats=stats, sem=dma),
        )

    def input_part(g1, back):
        return run(
            functools.partial(input_grads, input_maps), "input_grads", (flop * 4 * qw, 10e6),
            dict(me=me),
            dict(g1=g1, lg1=b.lg1, dqkv=[k.dqkv for k in back], ldqkv=[k.ldqkv for k in back], wlay=wlay),
            dict(w=input_w), dict(dx=rows_f, dxl=sds((lay_width, S), F32)), {},
            dict(wq=qkv_w, sem=dma),
        )

    both = jnp.concatenate(
        [jnp.concatenate([b.tg, f.tg]), jnp.concatenate([b.lg, f.lg])], axis=1
    )
    if paired:
        ds, us, qs = Scatter(SPLIT), Scatter(SPLIT), Scatter(SAME)
        gate = lax.optimization_barrier
        near = exchange(f.out[0], 1)
        near, done, both = gate((near, b.g1, both))
        norm = exchange(both, 1)
        d_near, d_first, sent = near, [], [done]
        for h in range(2):
            d_first.append(ds.first(h, f.out[2 * h + 2], near[16 * h : 16 * h + 8]))
            sent.append(ds.sent)
        ug = up_part(after(e.mid, sent))
        d_first, norm, dctx, core, _ = gate((d_first, norm, b.dctx, ug.out[0], ug.lup))
        both = both + norm
        norm = exchange(both, 2)
        near = exchange(core, 1)
        d_side = ds.side([[f.out[2 * h + 1], d_near[16 * h + 8 : 16 * h + 16], d_first[h]] for h in range(2)])
        back = [None] * TB
        back[3] = attend_back(3, after(dctx[3], ds.sent, both), ug)
        d_side, near, norm, dctx, core, _ = gate((d_side, near, norm, dctx, back[3].out[0], back[3].dqkv))
        both = both + norm
        norm = exchange(both, 4)
        a_near = exchange(core, 1)
        d_8 = ds.over_8(d_side)
        u_near, u_first, sent = near, [], [ds.sent, both]
        for h in range(2):
            u_first.append(us.first(h, ug.out[2 * h + 2], near[16 * h : 16 * h + 8]))
            sent.append(us.sent)
        back[2] = attend_back(2, after(dctx[2], sent), ug)
        u_first, d_8, a_near, norm, dctx, _ = gate((u_first, d_8, a_near, norm, dctx, back[2].dqkv))
        d_16 = ds.over_16(d_8)
        both = both + norm
        norm = exchange(both, 8)
        a_rows = (slice(0, half), slice(half, text_rows))
        u_side = us.side([[ug.out[2 * h + 1], u_near[16 * h + 8 : 16 * h + 16], u_first[h]] for h in range(2)])
        a_got = [None, qs.first(1, back[2].out[0][:, a_rows[1]], a_near[:, a_rows[1]])]
        back[1] = attend_back(1, after(dctx[1], us.sent, qs.sent, ds.sent, both), ug)
        u_side, d_16, a_got[1], norm, dctx, core, _ = gate(
            (u_side, d_16, a_got[1], norm, dctx, back[1].out[0], back[1].dqkv)
        )
        both = both + norm
        norm = exchange(both, 16)
        u_8 = us.over_8(u_side)
        a_second = exchange(core, 1)
        a_got[0] = qs.first(0, back[2].out[0][:, a_rows[0]], a_near[:, a_rows[0]])
        back[0] = attend_back(0, after(dctx[0], us.sent, qs.sent, both), ug)
        u_8, a_got[0], a_second, norm, g1, _ = gate((u_8, a_got[0], a_second, norm, b.g1, back[0].dqkv))
        u_16 = us.over_16(u_8)
        got = qs.side([[back[0].out[0][:, a_rows[h]], a_second[:, a_rows[h]], a_got[h]] for h in range(2)])
        last = input_part(after(g1, qs.sent, us.sent), back)
        settled = [
            (f.out[1::2], d_near, d_first, d_side, d_8, d_16),
            (ug.out[1::2], u_near, u_first, u_side, u_8, u_16),
        ]
        got, _ = gate((got, last.dx))
        got = qs.along_z(got)
        settled, both, norm, _ = gate((settled, both, norm, qs.sent))
        both = both + norm
        a_grad, d_grad, u_grad = qs.finish(got), ds.settle(*settled[0]), us.settle(*settled[1])
        q_grad, packed = a_grad[:, :qw], a_grad[:, qw:]
        l_grad = jnp.concatenate([packed[i * LROWS : i * LROWS + lay_rows] for i in range(3)], axis=1)
    else:

        def scatter(array):
            flat = array.reshape(-1, array.shape[2])
            return lax.psum_scatter(flat, everywhere, scatter_dimension=0, tiled=True).astype(F32)

        ug = up_part(e.mid)
        back = [attend_back(t, b.dctx[t], ug) for t in range(TB)]
        last = input_part(b.g1, back)
        d_grad = scatter(f.out[0])
        u_grad = scatter(ug.out[0])
        a_out = jnp.concatenate([k.out[0] for k in back])
        packed = [a_out[:, i * LROWS : i * LROWS + lay_rows, qw:] for i in range(3)]
        q_grad = scatter(a_out[:, :, :qw])
        l_grad = scatter(jnp.concatenate(packed, axis=2))
        both = lax.psum(both, ("dp", "tensor"))
    lqw = 3 * low
    return (
        f.result,
        f.lresult.T,
        last.dx,
        last.dxl.T,
        jnp.stack([q_grad[:, i * ow : (i + 1) * ow] for i in range(3)], axis=1),
        u_grad[:, fw:].T,
        u_grad[:, :fw],
        d_grad.T,
        both[:, :width],
        jnp.stack([l_grad[:, i * low : (i + 1) * low] for i in range(3)], axis=1),
        l_grad[:, lqw : lqw + low].T,
        l_grad[:, lqw + low : lqw + low + lfw],
        l_grad[:, lqw + low + lfw :].T,
        both[:, width:],
    )


def solution(mesh):
    in_specs = (
        P(("dp", "tensor"), None),
        P(("dp", "tensor"), None),
        P(("dp", "tensor"), None),
        P(("dp", "tensor"), None),
        P("dp"),
        P("dp"),
        P("dp", None, "tensor"),
        P("tensor", "dp"),
        P("dp", "tensor"),
        P("tensor", "dp"),
        P(),
        P("dp", None, "tensor"),
        P("tensor", "dp"),
        P("dp", "tensor"),
        P("tensor", "dp"),
        P(),
    )
    out_specs = (
        P(("dp", "tensor"), None),
        P(("dp", "tensor"), None),
        P(("dp", "tensor"), None),
        P(("dp", "tensor"), None),
        P("dp", None, "tensor"),
        P("tensor", "dp"),
        P("dp", "tensor"),
        P("tensor", "dp"),
        P(),
        P("dp", None, "tensor"),
        P("tensor", "dp"),
        P("dp", "tensor"),
        P("tensor", "dp"),
        P(),
    )
    return jax.shard_map(body, mesh=mesh, in_specs=in_specs, out_specs=out_specs, check_vma=False)
```

```python
import functools
import math

import jax
import jax.numpy as jnp
import numpy as np
from jax import lax
from jax.experimental import pallas as pl
from jax.experimental.layout import Layout, with_layout_constraint
from jax.experimental.pallas import tpu as pltpu
from jax.sharding import PartitionSpec as P

TEXT_HEAD = 64
LAY_HEAD = 16
S = 512
NGROUPS = 8

TB = 4
DB = 8
LROWS = 32

SPLIT = ((2, 4), (4, 2))
SAME = ((2, 4), (2, 4))

epsilon = 1e-05
neg_large = -1e30
root_half = 1.0 / math.sqrt(2.0)
root_twopi = 1.0 / math.sqrt(2.0 * math.pi)
text_scale = float(TEXT_HEAD) ** (-0.5)
layout_scale = float(LAY_HEAD) ** (-0.5)

HINT = 0.1
BF = jnp.bfloat16
F32 = jnp.float32
ANY = pl.BlockSpec(memory_space=pl.ANY)
VM = pl.BlockSpec(memory_space=pltpu.VMEM)
SM = pl.BlockSpec(memory_space=pltpu.SMEM)
PARAMS = pltpu.CompilerParams(vmem_limit_bytes=60 * 1024 * 1024)


def nn(a, b):
    return jnp.dot(a, b, preferred_element_type=F32)


def nt(a, b):
    return lax.dot_general(a, b, (((1,), (1,)), ((), ())), preferred_element_type=F32)


def sds(shape, dtype):
    return jax.ShapeDtypeStruct(shape, dtype)


def cost(flops, read, trans=0):
    return pl.CostEstimate(flops=int(flops * HINT), bytes_accessed=int(read * HINT), transcendentals=int(trans * HINT))


def load_pieces(refs, maps, d0, size, lanes, dst, sem):
    for ref, entries in zip(refs, maps):
        for i, entry in enumerate(entries):
            if entry is None:
                continue
            rel, start, rows = entry
            spot = pl.multiple_of(((rel // TB) ^ d0) * size + start, rows)
            pltpu.make_async_copy(
                ref.at[i, :, lanes[0] : lanes[1]], dst.at[rel % TB, pl.ds(spot, rows), :], sem
            ).start()


def send_pieces(outs, maps, d0, buf, size, lanes, sem):
    for out, entries in zip(outs, maps):
        for i, entry in enumerate(entries):
            if entry is None:
                continue
            rel, start, rows = entry
            spot = pl.multiple_of(((rel // TB) ^ d0) * size + start, rows)
            pltpu.make_async_copy(
                buf.at[rel % TB, pl.ds(spot, rows), :], out.at[i, :, lanes[0] : lanes[1]], sem
            ).start()


def wait_pieces(dst, sem):
    pltpu.make_async_copy(dst, dst, sem).wait()


class Refs:
    def __init__(self, **entries):
        self.__dict__.update(entries)


def run(kernel, name, price, scalars, arrays, hbm, outs, hbm_outs, scratch):
    ins, in_tree = jax.tree.flatten((scalars, arrays, hbm))
    in_specs = [SM] * len(jax.tree.leaves(scalars)) + [VM] * len(jax.tree.leaves(arrays))
    in_specs += [ANY] * len(jax.tree.leaves(hbm))
    out_shapes, out_tree = jax.tree.flatten((outs, hbm_outs))
    out_specs = [VM] * len(jax.tree.leaves(outs)) + [ANY] * len(jax.tree.leaves(hbm_outs))
    scratch_shapes, scratch_names = list(scratch.values()), list(scratch)

    def inner(*refs):
        a, b = len(ins), len(ins) + len(out_shapes)
        s, v, h = jax.tree.unflatten(in_tree, refs[:a])
        o, ho = jax.tree.unflatten(out_tree, refs[a:b])
        kernel(Refs(**s, **v, **h, **o, **ho, **dict(zip(scratch_names, refs[b:]))))

    got = pl.pallas_call(
        inner,
        name=name,
        in_specs=in_specs,
        out_specs=out_specs,
        out_shape=out_shapes,
        scratch_shapes=scratch_shapes,
        compiler_params=PARAMS,
        cost_estimate=cost(*price),
    )(*ins)
    o, ho = jax.tree.unflatten(out_tree, got)
    return Refs(**o, **ho)


def attention_forward(maps, counted, k):
    d0 = k.me[0] // TB
    lay_width = k.select.shape[1]
    text_rows, lay_rows = k.wq.shape[1] // DB, lay_width // DB
    width = k.qkv.shape[1]
    load_pieces(k.w, maps, d0, text_rows, (0, k.wq.shape[2]), k.wq, k.sem)
    live = lax.broadcasted_iota(jnp.int32, (1, S), 1) < k.length[0]
    heads = width // 3 // TEXT_HEAD
    tw, lw = heads * TEXT_HEAD, heads * LAY_HEAD
    if hasattr(k, "xt"):
        k.xt[...] = k.x[...].T
        k.xlt[...] = k.xl[...].T
    wait_pieces(k.wq, k.sem)
    packed = k.wq[0, :, width:]
    if counted:
        place = lax.broadcasted_iota(jnp.int32, (8, k.wq.shape[1]), 1) % text_rows
        spare = (LROWS - lay_rows) // 2
        high = (place >= lay_rows) & (place < lay_rows + spare)
        low = (place >= lay_rows + spare) & (place < LROWS)
        digits = jnp.where(high, 32.0, jnp.where(low, 1.0, 0.0)).astype(BF)
        k.counts[...] = nn(digits, packed[:, 0:128])
    else:
        k.counts[...] = jnp.zeros(k.counts.shape, F32)
    wlt = jnp.concatenate([nn(k.select[j], packed).astype(BF) for j in range(3)], axis=1)
    k.wlay[...] = wlt
    qkv = nn(k.x[...], k.wq[0, :, 0:width]).astype(BF)
    k.qkv[...] = qkv
    lqkv = nn(k.xl[...], wlt[:, : 3 * lw]).astype(BF)
    k.lqkv[...] = lqkv
    for h in range(heads):
        a, b = h * TEXT_HEAD, h * LAY_HEAD
        ta, tb = slice(a, a + TEXT_HEAD), slice(b, b + LAY_HEAD)
        q = jnp.concatenate([qkv[:, ta] * BF(text_scale), lqkv[:, tb] * BF(layout_scale)], axis=1)
        key = jnp.concatenate([qkv[:, tw + a : tw + a + TEXT_HEAD], lqkv[:, lw + b : lw + b + LAY_HEAD]], axis=1)
        v = jnp.concatenate(
            [qkv[:, 2 * tw + a : 2 * tw + a + TEXT_HEAD], lqkv[:, 2 * lw + b : 2 * lw + b + LAY_HEAD]], axis=1
        )
        logits = jnp.where(live, nt(q, key), neg_large)
        top = jnp.max(logits, axis=-1, keepdims=True)
        raw = jnp.exp(logits - top)
        total = jnp.sum(raw, axis=-1, keepdims=True)
        probs = (raw * (1.0 / total)).astype(BF)
        ctx = nn(probs, v).astype(BF)
        k.ctx[:, ta] = ctx[:, :TEXT_HEAD]
        k.lctx[:, tb] = ctx[:, TEXT_HEAD:]
        k.lse[:, h : h + 1] = top + jnp.log(total)


def ffn_up(maps, k):
    d0 = k.me[0] // TB
    rows, fw, ow = k.wu.shape[1] // DB, k.wu.shape[2], k.wo.shape[2]
    low = k.lctx[0].shape[1]
    lf = (k.wlay[0].shape[1] - 4 * low) // 2
    load_pieces(k.u, maps, d0, rows, (fw, fw + ow), k.wo, k.sems.at[0])
    load_pieces(k.u, maps, d0, rows, (0, fw), k.wu, k.sems.at[1])
    tn, ln = k.tn[...], k.ln[...]
    lattn = nt(k.lctx[0][...], k.wlay[0][:, 3 * low : 4 * low])
    for t in range(1, TB):
        lattn = lattn + nt(k.lctx[t][...], k.wlay[t][:, 3 * low : 4 * low])
    wait_pieces(k.wo, k.sems.at[0])
    attn = nt(k.ctx[0][...], k.wo[0])
    for t in range(1, TB):
        attn = attn + nt(k.ctx[t][...], k.wo[t])
    n1, i1 = norm_stats(k.x[...].astype(F32) + attn)
    ln1, li1 = norm_stats(k.xl[...].astype(F32) + lattn)
    k.n1[...] = n1
    k.ln1[...] = ln1
    k.i1[:, 0:1] = i1
    k.i1[:, 1:2] = li1
    k.mid[...] = (n1 * tn[0:1] + tn[1:2]).astype(BF)
    k.lmid[...] = (ln1 * ln[0:1] + ln[1:2]).astype(BF)
    wait_pieces(k.wu, k.sems.at[1])

    def gelu(before):
        cdf = 0.5 * (1.0 + lax.erf(before * root_half))
        slope = cdf + before * jnp.exp(-0.5 * before * before) * root_twopi
        return (before * cdf).astype(BF), slope.astype(BF)

    def step(t, carry):
        hid, slope = gelu(nn(k.mid[...], k.wu[t]))
        k.hid[t] = hid
        k.slope[t] = slope
        return carry

    lax.fori_loop(0, TB, step, 0)
    for t in range(TB):
        lhid, lslope = gelu(nn(k.lmid[...], k.wlay[t][:, 4 * low : 4 * low + lf]))
        k.lhid[t] = lhid
        k.lslope[t] = lslope


def ffn_down(maps, sent, base, k):
    d0 = k.me[0] // TB
    rows, fw = k.wd.shape[1] // DB, k.wd.shape[2]
    lf = k.lhid.shape[2]
    load_pieces(k.d, maps, d0, rows, (0, fw), k.wd, k.sem)
    counts = k.known[...]
    for t in range(TB):
        counts = counts + k.counts[t][0:1]
    same = lax.broadcasted_iota(jnp.int32, counts.shape, 1) == k.group[0]
    mine = jnp.sum(jnp.where(same, counts, 0.0), axis=1, keepdims=True)
    keep = (lax.broadcasted_iota(jnp.int32, (S, 1), 0) < k.length[0]).astype(F32)
    scale = keep * (base / (mine + base))
    tn, ln = k.tn[...], k.ln[...]
    lbranch = k.ln1[...] * ln[0:1] + ln[1:2]
    for t in range(TB):
        lbranch = lbranch + nt(k.lhid[t], k.wlay[t][:, k.wlay[t].shape[1] - lf :])
    ln2, li2 = norm_stats(lbranch)
    k.lresult[...] = ((ln2 * ln[2:3] + ln[3:4]) * keep).T
    lge, lgain, lshift = norm_back(k.lcot[...].T * scale, ln2, li2, ln[2:3])
    k.lge[...] = lge
    k.lgb[...] = lge.astype(BF)
    k.lg[0:1] = lgain
    k.lg[1:2] = lshift
    wait_pieces(k.wd, k.sem)
    branch = k.n1[...] * tn[0:1] + tn[1:2]
    for t in range(TB):
        branch = branch + nt(k.hid[t], k.wd[t])
    n2, i2 = norm_stats(branch)
    k.result[...] = (n2 * tn[2:3] + tn[3:4]) * keep
    ge, gain, shift = norm_back(k.cot[...] * scale, n2, i2, tn[2:3])
    k.ge[...] = ge
    k.gb[...] = ge.astype(BF)
    k.tg[0:1] = gain
    k.tg[1:2] = shift
    k.gbt[...] = k.gb[...].T
    k.lgbt[...] = k.lgb[...].T

    def step(t, carry):
        k.buf[t] = nn(k.gbt[...], k.hid[t]).astype(BF)
        return carry

    lax.fori_loop(0, TB, step, 0)
    send_pieces(k.out, sent, d0, k.buf, rows, (0, fw), k.sem)
    for t in range(TB):
        k.ldown[t][...] = nn(k.lgbt[...], k.lhid[t]).astype(BF)
    wait_pieces(k.buf, k.sem)


def ffn_backward(maps, k):
    d0 = k.me[0] // TB
    rows, fw, ow = k.wu.shape[1] // DB, k.wu.shape[2], k.wo.shape[2]
    low = k.ldctx[0].shape[1]
    lf = (k.wlay[0].shape[1] - 4 * low) // 2
    load_pieces(k.d, maps[1], d0, rows, (0, fw), k.wd, k.sems.at[0])
    load_pieces(k.u, maps[0], d0, rows, (0, fw), k.wu, k.sems.at[1])
    load_pieces(k.u, maps[0], d0, rows, (fw, fw + ow), k.wo, k.sems.at[2])
    tn, ln = k.tn[...], k.ln[...]
    k.acc[...] = k.ge[...]
    k.lacc[...] = k.lge[...]
    for t in range(TB):
        ldbef = (nn(k.lgb[...], k.wlay[t][:, 4 * low + lf :]) * k.lslope[t]).astype(BF)
        k.ldbef[t] = ldbef
        k.lacc[...] += nt(ldbef, k.wlay[t][:, 4 * low : 4 * low + lf])
    wait_pieces(k.wd, k.sems.at[0])
    wait_pieces(k.wu, k.sems.at[1])

    def step(t, carry):
        dbef = (nn(k.gb[...], k.wd[t]) * k.slope[t]).astype(BF)
        k.dbef[t] = dbef
        k.acc[...] += nt(dbef, k.wu[t])
        return carry

    lax.fori_loop(0, TB, step, 0)
    g1, gain, shift = norm_back(k.acc[...], k.n1[...], k.i1[:, 0:1], tn[0:1])
    k.g1[...] = g1
    k.tg[0:1] = gain
    k.tg[1:2] = shift
    lg1, lgain, lshift = norm_back(k.lacc[...], k.ln1[...], k.i1[:, 1:2], ln[0:1])
    k.lg1[...] = lg1
    k.lg[0:1] = lgain
    k.lg[1:2] = lshift
    ga = g1.astype(BF)
    lga = lg1.astype(BF)
    wait_pieces(k.wo, k.sems.at[2])
    for t in range(TB):
        k.dctx[t][...] = nn(ga, k.wo[t]).astype(BF)
        k.ldctx[t][...] = nn(lga, k.wlay[t][:, 3 * low : 4 * low]).astype(BF)


def up_grads(maps, k):
    rows, fw, ow = k.buf.shape[1] // DB, k.buf.shape[2], k.obuf.shape[2]
    low = k.lctx[0].shape[1]
    d0 = k.me[0] // TB
    k.rt[...] = k.g1[...].astype(BF).T
    k.lrt[...] = k.lg1[...].astype(BF).T
    for t in range(TB):
        k.obuf[t] = nn(k.rt[...], k.ctx[t][...]).astype(BF)
        k.lup[t][:, 0:low] = nn(k.lrt[...], k.lctx[t][...]).astype(BF)
    send_pieces(k.out, maps, d0, k.obuf, rows, (fw, fw + ow), k.sems.at[1])
    k.rt[...] = k.mid[...].T
    k.lrt[...] = k.lmid[...].T

    def step(t, carry):
        k.buf[t] = nn(k.rt[...], k.dbef[t]).astype(BF)
        return carry

    lax.fori_loop(0, TB, step, 0)
    send_pieces(k.out, maps, d0, k.buf, rows, (0, fw), k.sems.at[0])
    for t in range(TB):
        k.lup[t][:, low:] = nn(k.lrt[...], k.ldbef[t]).astype(BF)
    wait_pieces(k.obuf, k.sems.at[1])
    wait_pieces(k.buf, k.sems.at[0])


def attention_backward(maps, k):
    width = k.qkv.shape[1]
    heads = width // 3 // TEXT_HEAD
    tw, lw = heads * TEXT_HEAD, heads * LAY_HEAD
    text_rows = k.buf.shape[1] // DB
    live = lax.broadcasted_iota(jnp.int32, (1, S), 1) < k.length[0]
    for h in range(heads):
        a, b = h * TEXT_HEAD, h * LAY_HEAD
        ta, tb = slice(a, a + TEXT_HEAD), slice(b, b + LAY_HEAD)
        for j, (dst, one, two) in enumerate(((k.qs, text_scale, layout_scale), (k.ks, 1.0, 1.0), (k.vs, 1.0, 1.0))):
            c, d = j * tw + a, j * lw + b
            parts = [k.qkv[:, c : c + TEXT_HEAD] * BF(one), k.lqkv[:, d : d + LAY_HEAD] * BF(two)]
            dst[h] = jnp.concatenate(parts, axis=1)
        gt, gl = k.dctx[:, ta], k.ldctx[:, tb]
        k.gs[h] = jnp.concatenate([gt, gl], axis=1)
        dot_t = jnp.sum(gt.astype(F32) * k.ctx[:, ta].astype(F32), axis=-1, keepdims=True)
        dot_l = jnp.sum(gl.astype(F32) * k.lctx[:, tb].astype(F32), axis=-1, keepdims=True)
        k.stats[h, :, 0:1] = dot_t
        k.stats[h, :, 1:2] = dot_t + dot_l
        k.stats[h, :, 2:3] = k.lse[:, h : h + 1]

    def step(h, carry):
        q, key, v, g = k.qs[h], k.ks[h], k.vs[h], k.gs[h]
        gt, vt = g[:, :TEXT_HEAD], v[:, :TEXT_HEAD]
        logits = jnp.where(live, nt(q, key), neg_large)
        probs = jnp.exp(logits - k.stats[h, :, 2:3])
        low = (probs * (nt(gt, vt) - k.stats[h, :, 0:1])).astype(BF)
        llow = (probs * (nt(g, v) - k.stats[h, :, 1:2])).astype(BF)
        dq = nn(low, key[:, :TEXT_HEAD]) * text_scale
        dql = nn(llow, key[:, TEXT_HEAD:]) * layout_scale
        dk = nn(q[:, :TEXT_HEAD].T, low).T
        dkl = nn(q[:, TEXT_HEAD:].T, llow).T
        dv = nn(g.T, probs.astype(BF)).T
        k.qs[h] = jnp.concatenate([dq, dql], axis=1).astype(BF)
        k.ks[h] = jnp.concatenate([dk, dkl], axis=1).astype(BF)
        k.vs[h] = dv.astype(BF)
        return carry

    lax.fori_loop(0, heads, step, 0)
    for h in range(heads):
        for j, src in enumerate((k.qs, k.ks, k.vs)):
            a, b = j * tw + h * TEXT_HEAD, j * lw + h * LAY_HEAD
            k.dqkv[:, a : a + TEXT_HEAD] = src[h, :, :TEXT_HEAD]
            k.ldqkv[:, b : b + LAY_HEAD] = src[h, :, TEXT_HEAD:]
    k.buf[0, :, 0:width] = nn(k.xt[...], k.dqkv[...]).astype(BF)
    lgrad = jnp.concatenate([nn(k.xlt[...], k.ldqkv[...]).astype(BF), k.lup[...], k.ldown[...]], axis=1)
    third = width // 3
    packed = nn(k.selt[0], lgrad[:, 0:third])
    for j in range(1, 3):
        packed = packed + nn(k.selt[j], lgrad[:, j * third : (j + 1) * third])
    k.buf[0, :, width:] = packed.astype(BF)
    d0 = k.me[0] // TB
    send_pieces(k.out, maps, d0, k.buf, text_rows, (0, k.buf.shape[2]), k.sem)
    wait_pieces(k.buf, k.sem)


def input_grads(maps, k):
    d0 = k.me[0] // TB
    text_rows, width = k.wq.shape[1] // DB, k.dqkv[0].shape[1]
    lw = k.ldqkv[0].shape[1]
    load_pieces(k.w, maps, d0, text_rows, (0, k.wq.shape[2]), k.wq, k.sem)
    dxl = k.lg1[...]
    for t in range(TB):
        dxl = dxl + nt(k.ldqkv[t][...], k.wlay[t][:, :lw])
    k.dxl[...] = dxl.T
    wait_pieces(k.wq, k.sem)
    dx = k.g1[...]
    for t in range(TB):
        dx = dx + nt(k.dqkv[t][...], k.wq[t, :, 0:width])
    k.dx[...] = dx


def norm_stats(values):
    centred = values - jnp.mean(values, axis=-1, keepdims=True)
    inverse = lax.rsqrt(jnp.mean(centred * centred, axis=-1, keepdims=True) + epsilon)
    return centred * inverse, inverse


def norm_back(upstream, normed, inverse, gain):
    scaled = upstream * gain
    inner = (
        scaled
        - jnp.mean(scaled, axis=-1, keepdims=True)
        - normed * jnp.mean(scaled * normed, axis=-1, keepdims=True)
    )
    return (
        inverse * inner,
        jnp.sum(upstream * normed, axis=0, keepdims=True),
        jnp.sum(upstream, axis=0, keepdims=True),
    )


def exchange(array, bit):
    size = lax.axis_size("dp") * lax.axis_size("tensor")
    return lax.ppermute(array, ("dp", "tensor"), [(i, i ^ bit) for i in range(size)])


Z = (0, 8, 16, 24)


def gather_maps(rows, steps):
    half = rows // 2
    tops = ((0, 0, 2), (4, 0, 2), (0, half, 4), (2, half, 4))
    return tuple(
        tuple((z | inner | top | core, start, half) for inner in (0, step) for z in steps)
        for core in (0, 1)
        for top, start, step in tops
    )


def scatter_maps(start, rows, bits):
    return tuple(
        tuple((z | inner | top, start, rows) for inner in (0, bits[1]) for z in Z)
        for top in (0, 1, bits[0], bits[0] | 1)
    )


def block(maps, t):
    return tuple(
        tuple((rel - t, start, rows) if rel % TB == t else None for rel, start, rows in entries) for entries in maps
    )


def after(array, *needed):
    return lax.optimization_barrier((array, needed))[0]


def rows_major(array):
    return with_layout_constraint(array, Layout(major_to_minor=(0, 1, 2)))


class Gather:
    def __init__(self, own):
        self.own, self.half = rows_major(own[None]), own.shape[0] // 2

    def along_z(self):
        got = [self.own] + [rows_major(exchange(self.own, z)) for z in Z[1:]]
        self.upper = rows_major(jnp.concatenate([g[:, : self.half] for g in got], axis=0))
        self.lower = rows_major(jnp.concatenate([g[:, self.half :] for g in got], axis=0))
        return self.lower

    def over_16(self):
        self.own = rows_major(jnp.concatenate([self.own, exchange(self.own, 16)], axis=0))

    def over_8(self):
        got = [self.own, exchange(self.own, 8)]
        self.upper = rows_major(jnp.concatenate([g[:, : self.half] for g in got], axis=0))
        self.lower = rows_major(jnp.concatenate([g[:, self.half :] for g in got], axis=0))

    def sides(self):
        self.upper = rows_major(jnp.concatenate([self.upper, exchange(self.upper, 2)], axis=0))
        self.lower = rows_major(jnp.concatenate([self.lower, exchange(self.lower, 4)], axis=0))
        return self.lower

    def cross(self):
        self.here = [self.upper, rows_major(exchange(self.upper, 4)), self.lower, rows_major(exchange(self.lower, 2))]
        return self.here


def swap(arrays):
    return [rows_major(exchange(array, 1)) for array in arrays]


def rounded(parts):
    return rows_major(sum(p.astype(F32) for p in parts).astype(BF))


class Scatter:
    def __init__(self, bits):
        self.bits = bits

    def first(self, h, far, near):
        self.sent = rounded([far, near])
        return exchange(self.sent, self.bits[h][0])

    def side(self, parts):
        self.parts = parts
        self.sent = [rounded([p[4:8] for p in half]) for half in parts]
        return [exchange(sent, self.bits[h][1]) for h, sent in enumerate(self.sent)]

    def along_z(self, got):
        self.parts = [half + [g] for half, g in zip(self.parts, got)]
        self.sent = [
            rows_major(jnp.concatenate([rounded([p[i : i + 1] for p in half]) for half in self.parts], axis=1))
            for i in range(1, 4)
        ]
        return [exchange(piece, z) for piece, z in zip(self.sent, Z[1:])]

    def over_8(self, got):
        self.parts = [half + [g] for half, g in zip(self.parts, got)]
        self.sent = rows_major(
            jnp.concatenate(
                [
                    jnp.concatenate([rounded([p[i : i + 1] for p in half]) for half in self.parts], axis=1)
                    for i in (1, 3)
                ]
            )
        )
        return exchange(self.sent, 8)

    def over_16(self, got):
        rows = got.shape[1] // 2
        parts = [[p[2:3] for p in half] + [got[1:2, h * rows : (h + 1) * rows]] for h, half in enumerate(self.parts)]
        self.sent = rows_major(jnp.concatenate([rounded(half) for half in parts], axis=1))
        return exchange(self.sent, 16)

    def settle(self, cols, *arrays):
        own, near, first, side, over_8, over_16 = jax.tree.map(lambda a: a[:, :, cols], arrays)
        rows = own[0].shape[1]
        halves = [
            [own[h][0], near[16 * h + 8], first[h][0], side[h][0], over_8[0, h * rows : (h + 1) * rows]]
            for h in range(2)
        ]
        kept = jnp.concatenate([sum(p.astype(F32) for p in half) for half in halves], axis=0)
        return kept + over_16[0].astype(F32)

    def finish(self, got):
        kept = jnp.concatenate([sum(p[0].astype(F32) for p in half) for half in self.parts], axis=0)
        return kept + sum(g[0].astype(F32) for g in got)


def body(
    text_input,
    layout_input,
    text_cotangent,
    layout_cotangent,
    page_group,
    page_length,
    text_qkv,
    text_out,
    text_up,
    text_down,
    text_norm,
    layout_qkv,
    layout_out,
    layout_up,
    layout_down,
    layout_norm,
):
    dp_pages = page_length.shape[0]
    dp, tensor = lax.axis_size("dp"), lax.axis_size("tensor")
    width, lay_width = text_input.shape[1], layout_input.shape[1]
    text_rows, lay_rows = width // DB, lay_width // DB

    qkv_own = jnp.concatenate([text_qkv[:, i] for i in range(3)], axis=1)
    up_own = jnp.concatenate([text_up, text_out.T], axis=1)
    down_own = text_down.T
    lay_own = jnp.concatenate(
        [layout_qkv[:, i] for i in range(3)] + [layout_out.T, layout_up, layout_down.T], axis=1
    )
    qw, ow, fw = qkv_own.shape[1], text_out.shape[0], text_up.shape[1]
    low, lfw, lpack = layout_out.shape[0], layout_up.shape[1], lay_own.shape[1]
    mine = jnp.arange(dp_pages, dtype=jnp.int32) == lax.axis_index("tensor")
    length = jnp.sum(jnp.where(mine, page_length, 0)).reshape(1)
    group = jnp.sum(jnp.where(mine, page_group, 0)).reshape(1)
    base = float(dp_pages * dp * S) / (2.0 * NGROUPS)
    paired = dp == DB and tensor == TB
    everywhere = ("tensor", "dp")
    if paired:
        digits = jnp.concatenate([page_length >> 5, page_length & 31])[:, None]
        groups = jnp.concatenate([page_group, page_group])[:, None]
        column = lax.broadcasted_iota(jnp.int32, (LROWS - lay_rows, lpack), 1) == groups
        spare = jnp.where(column, digits, 0).astype(BF)
        packed = jnp.concatenate([lay_own, spare], axis=0)
        packed = jnp.concatenate([packed[:, i * ow : (i + 1) * ow] for i in range(3)], axis=0)
        ga = Gather(jnp.concatenate([qkv_own, packed], axis=1))
        barrier = lax.optimization_barrier
        ga.along_z()
        ga.sides()
        ga.upper, ga.lower, up_own = barrier((ga.upper, ga.lower, up_own))
        gu = Gather(up_own)
        ga.cross()
        gu.over_16()
        weights_map = gather_maps(text_rows, Z)
        a_map = [block(weights_map[4 * (t % 2) : 4 * (t % 2) + 4], t) for t in range(TB)]
        u_map = d_map = gather_maps(text_rows, (0, 16, 8, 24))
        half = text_rows // 2
        up, lo = scatter_maps(0, half, SPLIT[0]), scatter_maps(half, half, SPLIT[1])
        u_send = d_send = (up[3] + up[1] + lo[3] + lo[1], up[0], up[2], lo[0], lo[2])
        a_send = [(block(scatter_maps(0, text_rows, SAME[0]), t)[t],) for t in range(TB)]
        me = (lax.axis_index("dp") * TB + lax.axis_index("tensor")).astype(jnp.int32).reshape(1)
        known = jnp.zeros((1, 128), F32)
    else:

        def gather(array, rows):
            whole = lax.all_gather(array, everywhere, axis=0, tiled=True)
            return whole.reshape(TB * DB, rows, array.shape[1])

        spare = ((0, 0), (0, LROWS - lay_rows), (0, 0))
        packed = jnp.pad(gather(lay_own, lay_rows), spare)
        packed = jnp.concatenate([packed[:, :, i * ow : (i + 1) * ow] for i in range(3)], axis=1)
        first = jnp.concatenate([gather(qkv_own, text_rows), packed], axis=2)
        a_in = [[first[t * DB : (t + 1) * DB]] for t in range(TB)]
        u_in, d_in = [gather(up_own, text_rows)], [gather(down_own, text_rows)]
        u_map = d_map = u_send = d_send = (tuple((d * TB + t, 0, text_rows) for t in range(TB) for d in range(DB)),)
        a_map = a_send = [(tuple((d * TB, 0, text_rows) for d in range(DB)),)] * TB
        me = jnp.zeros((1,), jnp.int32)
        labels = jnp.arange(NGROUPS, dtype=jnp.int32)
        member = (page_group[:, None] == labels[None, :]).astype(F32)
        counts = lax.psum(jnp.sum(member * page_length.astype(F32)[:, None], axis=0), "dp")
        known = jnp.pad(counts, (0, 128 - NGROUPS)).reshape(1, 128)

    chosen = np.zeros((3, lay_width, width), np.float32)
    for j in range(3):
        for a in range(lay_width):
            chosen[j, a, (a // lay_rows) * text_rows + j * LROWS + a % lay_rows] = 1.0
    select, select_t = jnp.asarray(chosen, BF), jnp.asarray(chosen.transpose(0, 2, 1), BF)
    V, dma = pltpu.VMEM, pltpu.SemaphoreType.DMA
    flop = 2.0 * S * width
    rows_f, rows_b = sds((S, width), F32), sds((S, width), BF)
    lay_f, lay_b = sds((S, lay_width), F32), sds((S, lay_width), BF)
    heads_held = ow // TEXT_HEAD
    head, stats = V((heads_held, S, TEXT_HEAD + LAY_HEAD), BF), V((heads_held, S, 128), F32)
    text_w, out_w, qkv_w = V((TB, width, fw), BF), V((TB, width, ow), BF), V((TB, width, qw + ow), BF)

    def attend(t, w):
        outs = dict(
            qkv=sds((S, qw), BF), lqkv=sds((S, 3 * low), BF), ctx=sds((S, ow), BF), lctx=sds((S, low), BF),
            lse=sds((S, 128), F32), wlay=sds((lay_width, lpack), BF), counts=sds((8, 128), F32),
        )
        if t == 0:
            outs.update(xt=sds((width, S), BF), xlt=sds((lay_width, S), BF))
        return run(
            functools.partial(attention_forward, a_map[t], paired and t == 0), "attention_forward",
            (flop * (qw + 3 * S), 5e6, 1e6),
            dict(me=me, length=length), dict(x=text_input, xl=layout_input, select=select), dict(w=w),
            outs, {},
            dict(wq=V((1, width, qw + ow), BF), sem=dma),
        )

    if paired:
        ga.here, gu.own = barrier((ga.here, gu.own))
        heads = [None] * TB
        gu.over_8()
        near = swap(ga.here[::2])
        heads[0] = attend(0, ga.here)
        gu.upper, gu.lower, near, here, down_own, _ = barrier(
            (gu.upper, gu.lower, near, ga.here, down_own, heads[0].ctx)
        )
        gd = Gather(down_own)
        gu.sides()
        gd.over_16()
        far = swap(here[1::2])
        heads[2] = attend(2, here)
        gu.upper, gu.lower, gd.own, near, far, _ = barrier((gu.upper, gu.lower, gd.own, near, far, heads[2].ctx))
        a_far = [near[0], far[0], near[1], far[1]]
        gu.cross()
        gd.over_8()
        near = swap(gu.here[::2])
        heads[1] = attend(1, a_far)
        gu.here, near, gd.upper, gd.lower, first, _ = barrier(
            (gu.here, near, gd.upper, gd.lower, a_far[0], heads[1].ctx)
        )
        gd.sides()
        far = swap(gu.here[1::2])
        heads[3] = attend(3, [first] + a_far[1:])
        gd.upper, gd.lower, near, far, ctx_last = barrier((gd.upper, gd.lower, near, far, heads[3].ctx))
        u_far = [near[0], far[0], near[1], far[1]]
        gd.cross()
        near = swap(gd.here[::2])
        u_in = gu.here + u_far
        input_w, input_maps = ga.here + a_far, weights_map
    else:
        heads = [attend(t, a_in[t]) for t in range(TB)]
        ctx_last = heads[-1].ctx
        input_w = [a[0] for a in a_in]
        input_maps = tuple(tuple((rel + t, start, rows) for rel, start, rows in a_map[t][0]) for t in range(TB))
    ctx, lctx = [h.ctx for h in heads[:-1]] + [ctx_last], [h.lctx for h in heads]
    wlay = [h.wlay for h in heads]
    e = run(
        functools.partial(ffn_up, u_map), "ffn_up", (flop * 4 * (fw + ow), 25e6, 4e6),
        dict(me=me),
        dict(x=text_input, xl=layout_input, ctx=ctx, lctx=lctx, wlay=wlay, tn=text_norm, ln=layout_norm),
        dict(u=u_in),
        dict(hid=sds((TB, S, fw), BF), slope=sds((TB, S, fw), BF), lhid=sds((TB, S, lfw), BF),
             lslope=sds((TB, S, lfw), BF), mid=rows_b, lmid=lay_b, n1=rows_f, ln1=lay_f, i1=sds((S, 128), F32)),
        {},
        dict(wu=text_w, wo=out_w, sems=dma((2,))),
    )
    if paired:
        gd.here, near, _ = barrier((gd.here, near, e.hid))
        far = swap(gd.here[1::2])
        d_in = gd.here + [near[0], far[0], near[1], far[1]]

    def outs_of(maps, wide):
        return [sds((len(m), m[0][2], wide), BF) for m in maps]

    f = run(
        functools.partial(ffn_down, d_map, d_send, base), "ffn_down", (flop * 8 * fw, 20e6),
        dict(me=me, length=length, group=group),
        dict(n1=e.n1, ln1=e.ln1, hid=e.hid, lhid=e.lhid, wlay=wlay, counts=[h.counts for h in heads],
             known=known, tn=text_norm, ln=layout_norm, cot=text_cotangent, lcot=layout_cotangent.T),
        dict(d=d_in),
        dict(result=rows_f, lresult=sds((lay_width, S), F32), gb=rows_b, lgb=lay_b, ge=rows_f, lge=lay_f,
             tg=sds((2, width), F32), lg=sds((2, lay_width), F32), ldown=[sds((lay_width, lfw), BF)] * TB),
        dict(out=outs_of(d_send, fw)),
        dict(wd=text_w, buf=text_w, gbt=V((width, S), BF), lgbt=V((lay_width, S), BF), sem=dma),
    )
    b = run(
        functools.partial(ffn_backward, (u_map, d_map)), "ffn_backward", (flop * 4 * (2 * fw + ow), 40e6),
        dict(me=me),
        dict(gb=after(f.gb, f.ldown[0]), lgb=f.lgb, ge=f.ge, lge=f.lge, slope=e.slope, lslope=e.lslope, n1=e.n1,
             ln1=e.ln1, i1=e.i1, wlay=wlay, tn=text_norm, ln=layout_norm),
        dict(u=u_in, d=d_in),
        dict(g1=rows_f, lg1=lay_f, dctx=[sds((S, ow), BF)] * TB, ldctx=[sds((S, low), BF)] * TB,
             dbef=sds((TB, S, fw), BF), ldbef=sds((TB, S, lfw), BF), tg=sds((2, width), F32),
             lg=sds((2, lay_width), F32)),
        {},
        dict(wu=text_w, wd=text_w, wo=out_w, acc=V((S, width), F32), lacc=V((S, lay_width), F32), sems=dma((3,))),
    )

    def up_part(mid):
        return run(
            functools.partial(up_grads, u_send), "up_grads", (flop * 4 * (fw + ow), 15e6),
            dict(me=me), dict(g1=b.g1, lg1=b.lg1, ctx=ctx, lctx=lctx, mid=mid, lmid=e.lmid, dbef=b.dbef, ldbef=b.ldbef),
            {},
            dict(lup=[sds((lay_width, low + lfw), BF)] * TB), dict(out=outs_of(u_send, fw + ow)),
            dict(buf=text_w, obuf=out_w, rt=V((width, S), BF), lrt=V((lay_width, S), BF), sems=dma((2,))),
        )

    def attend_back(t, dctx, ug):
        h = heads[t]
        return run(
            functools.partial(attention_backward, a_send[t]), "attention_backward", (flop * (qw + 6 * S), 8e6, 1e6),
            dict(me=me, length=length),
            dict(xt=heads[0].xt, xlt=heads[0].xlt, selt=select_t, qkv=h.qkv, lqkv=h.lqkv, ctx=h.ctx, lctx=h.lctx,
                 lse=h.lse, dctx=dctx, ldctx=b.ldctx[t], lup=ug.lup[t], ldown=f.ldown[t]),
            {},
            dict(dqkv=sds((S, qw), BF), ldqkv=sds((S, 3 * low), BF)),
            dict(out=[sds((DB, text_rows, qw + ow), BF)]),
            dict(buf=V((1, width, qw + ow), BF), qs=head, ks=head, vs=head, gs=head, stats=stats, sem=dma),
        )

    def input_part(g1, back):
        return run(
            functools.partial(input_grads, input_maps), "input_grads", (flop * 4 * qw, 10e6),
            dict(me=me),
            dict(g1=g1, lg1=b.lg1, dqkv=[k.dqkv for k in back], ldqkv=[k.ldqkv for k in back], wlay=wlay),
            dict(w=input_w), dict(dx=rows_f, dxl=sds((lay_width, S), F32)), {},
            dict(wq=qkv_w, sem=dma),
        )

    both = jnp.concatenate(
        [jnp.concatenate([b.tg, f.tg]), jnp.concatenate([b.lg, f.lg])], axis=1
    )
    if paired:
        ds, us, qs = Scatter(SPLIT), Scatter(SPLIT), Scatter(SAME)
        gate = lax.optimization_barrier
        near = exchange(f.out[0], 1)
        near, done, both = gate((near, b.g1, both))
        norm = exchange(both, 1)
        d_near, d_first, sent = near, [], [done]
        for h in range(2):
            d_first.append(ds.first(h, f.out[2 * h + 2], near[16 * h : 16 * h + 8]))
            sent.append(ds.sent)
        ug = up_part(after(e.mid, sent))
        d_first, norm, dctx, core, _ = gate((d_first, norm, b.dctx, ug.out[0], ug.lup))
        both = both + norm
        norm = exchange(both, 2)
        near = exchange(core, 1)
        d_side = ds.side([[f.out[2 * h + 1], d_near[16 * h + 8 : 16 * h + 16], d_first[h]] for h in range(2)])
        back = [None] * TB
        back[3] = attend_back(3, after(dctx[3], ds.sent, both), ug)
        d_side, near, norm, dctx, core, _ = gate((d_side, near, norm, dctx, back[3].out[0], back[3].dqkv))
        both = both + norm
        norm = exchange(both, 4)
        a_near = exchange(core, 1)
        d_8 = ds.over_8(d_side)
        u_near, u_first, sent = near, [], [ds.sent, both]
        for h in range(2):
            u_first.append(us.first(h, ug.out[2 * h + 2], near[16 * h : 16 * h + 8]))
            sent.append(us.sent)
        back[2] = attend_back(2, after(dctx[2], sent), ug)
        u_first, d_8, a_near, norm, dctx, _ = gate((u_first, d_8, a_near, norm, dctx, back[2].dqkv))
        d_16 = ds.over_16(d_8)
        both = both + norm
        norm = exchange(both, 8)
        a_rows = (slice(0, half), slice(half, text_rows))
        u_side = us.side([[ug.out[2 * h + 1], u_near[16 * h + 8 : 16 * h + 16], u_first[h]] for h in range(2)])
        a_got = [None, qs.first(1, back[2].out[0][:, a_rows[1]], a_near[:, a_rows[1]])]
        back[1] = attend_back(1, after(dctx[1], us.sent, qs.sent, ds.sent, both), ug)
        u_side, d_16, a_got[1], norm, dctx, core, _ = gate(
            (u_side, d_16, a_got[1], norm, dctx, back[1].out[0], back[1].dqkv)
        )
        both = both + norm
        norm = exchange(both, 16)
        u_8 = us.over_8(u_side)
        a_second = exchange(core, 1)
        a_got[0] = qs.first(0, back[2].out[0][:, a_rows[0]], a_near[:, a_rows[0]])
        back[0] = attend_back(0, after(dctx[0], us.sent, qs.sent, both), ug)
        u_8, a_got[0], a_second, norm, g1, _ = gate((u_8, a_got[0], a_second, norm, b.g1, back[0].dqkv))
        u_16 = us.over_16(u_8)
        got = qs.side([[back[0].out[0][:, a_rows[h]], a_second[:, a_rows[h]], a_got[h]] for h in range(2)])
        last = input_part(after(g1, qs.sent, us.sent), back)
        settled = [
            (f.out[1::2], d_near, d_first, d_side, d_8, d_16),
            (ug.out[1::2], u_near, u_first, u_side, u_8, u_16),
        ]
        got, _ = gate((got, last.dx))
        got = qs.along_z(got)
        settled, both, norm, _ = gate((settled, both, norm, qs.sent))
        both = both + norm
        a_grad, d_grad, u_grad = qs.finish(got), ds.settle(slice(None), *settled[0]), [us.settle(c, *settled[1]) for c in (slice(0, fw), slice(fw, None))]
        q_grad, packed = a_grad[:, :qw], a_grad[:, qw:]
        l_grad = jnp.concatenate([packed[i * LROWS : i * LROWS + lay_rows] for i in range(3)], axis=1)
    else:

        def scatter(array):
            flat = array.reshape(-1, array.shape[2])
            return lax.psum_scatter(flat, everywhere, scatter_dimension=0, tiled=True).astype(F32)

        ug = up_part(e.mid)
        back = [attend_back(t, b.dctx[t], ug) for t in range(TB)]
        last = input_part(b.g1, back)
        d_grad = scatter(f.out[0])
        u_grad = scatter(ug.out[0])
        u_grad = [u_grad[:, :fw], u_grad[:, fw:]]
        a_out = jnp.concatenate([k.out[0] for k in back])
        packed = [a_out[:, i * LROWS : i * LROWS + lay_rows, qw:] for i in range(3)]
        q_grad = scatter(a_out[:, :, :qw])
        l_grad = scatter(jnp.concatenate(packed, axis=2))
        both = lax.psum(both, ("dp", "tensor"))
    lqw = 3 * low
    return (
        f.result,
        f.lresult.T,
        last.dx,
        last.dxl.T,
        jnp.stack([q_grad[:, i * ow : (i + 1) * ow] for i in range(3)], axis=1),
        u_grad[1].T,
        u_grad[0],
        d_grad.T,
        both[:, :width],
        jnp.stack([l_grad[:, i * low : (i + 1) * low] for i in range(3)], axis=1),
        l_grad[:, lqw : lqw + low].T,
        l_grad[:, lqw + low : lqw + low + lfw],
        l_grad[:, lqw + low + lfw :].T,
        both[:, width:],
    )


def solution(mesh):
    in_specs = (
        P(("dp", "tensor"), None),
        P(("dp", "tensor"), None),
        P(("dp", "tensor"), None),
        P(("dp", "tensor"), None),
        P("dp"),
        P("dp"),
        P("dp", None, "tensor"),
        P("tensor", "dp"),
        P("dp", "tensor"),
        P("tensor", "dp"),
        P(),
        P("dp", None, "tensor"),
        P("tensor", "dp"),
        P("dp", "tensor"),
        P("tensor", "dp"),
        P(),
    )
    out_specs = (
        P(("dp", "tensor"), None),
        P(("dp", "tensor"), None),
        P(("dp", "tensor"), None),
        P(("dp", "tensor"), None),
        P("dp", None, "tensor"),
        P("tensor", "dp"),
        P("dp", "tensor"),
        P("tensor", "dp"),
        P(),
        P("dp", None, "tensor"),
        P("tensor", "dp"),
        P("dp", "tensor"),
        P("tensor", "dp"),
        P(),
    )
    return jax.shard_map(body, mesh=mesh, in_specs=in_specs, out_specs=out_specs, check_vma=False)
```
